32 devices in a mesh: fsdp: 8 (over z, x), tp: 4 (over y, core).
Axes of the slice: x: 2, y: 2, z: 4, core: 2. Of those that a mesh axis runs over, the one named last changes fastest.
Arguments:
- images: bfloat16 [256, 196, 512], P('fsdp'), may hold values from -6 to 6
- attn_norm_gain: bfloat16 [512], P('fsdp'), may hold values from 0.25 to 1.75
- attn_norm_bias: bfloat16 [512], P('fsdp'), may hold values from -1.75 to 1.75
- qkv_weight: bfloat16 [512, 3, 512], P('fsdp', None, 'tp'), may hold values from -0.25 to 0.25
- qkv_bias: bfloat16 [3, 512], P(None, 'tp'), may hold values from -1.75 to 1.75
- position_table: bfloat16 [169, 16], P(None, 'tp'), may hold values from -6 to 6
- proj_weight: bfloat16 [512, 512], P('tp', 'fsdp'), may hold values from -1 to 1
- proj_bias: bfloat16 [512], P('fsdp'), may hold values from -3 to 3
- mlp_norm_gain: bfloat16 [512], P('fsdp'), may hold values from 0.25 to 1.75
- mlp_norm_bias: bfloat16 [512], P('fsdp'), may hold values from -1.75 to 1.75
- fc1_weight: bfloat16 [512, 2048], P('fsdp', 'tp'), may hold values from -0.25 to 0.25
- fc1_bias: bfloat16 [2048], P('tp'), may hold values from -3 to 3
- fc2_weight: bfloat16 [2048, 512], P('tp', 'fsdp'), may hold values from -0.125 to 0.125
- fc2_bias: bfloat16 [512], P('fsdp'), may hold values from -3 to 3
- image_count: int32 [8], P('fsdp'), may hold values from 1 to 32, as said below
- out_grad: bfloat16 [256, 196, 512], P('fsdp'), may hold values from -6 to 6
Outputs:
- output: bfloat16 [256, 196, 512], P('fsdp')
- images_grad: bfloat16 [256, 196, 512], P('fsdp')
- attn_norm_gain_grad: float32 [512], P('fsdp')
- attn_norm_bias_grad: float32 [512], P('fsdp')
- qkv_weight_grad: float32 [512, 3, 512], P('fsdp', None, 'tp')
- qkv_bias_grad: float32 [3, 512], P(None, 'tp')
- position_table_grad: float32 [169, 16], P(None, 'tp')
- proj_weight_grad: float32 [512, 512], P('tp', 'fsdp')
- proj_bias_grad: float32 [512], P('fsdp')
- mlp_norm_gain_grad: float32 [512], P('fsdp')
- mlp_norm_bias_grad: float32 [512], P('fsdp')
- fc1_weight_grad: float32 [512, 2048], P('fsdp', 'tp')
- fc1_bias_grad: float32 [2048], P('tp')
- fc2_weight_grad: float32 [2048, 512], P('tp', 'fsdp')
- fc2_bias_grad: float32 [512], P('fsdp')
The draws below stay inside these ranges and needn't reach their ends.
Inputs may be any that keep to these rules, and one draw needn't show every extreme that they name: Slots 0 to image_count[i] - 1 of image block i hold images; some block is full and some holds one image.
All inputs are finite; a program needn't handle non-finite values.
Results may differ from the reference program's by a relative error of at most 0.0095.
Values may be sent and summed in bfloat16 or wider, within the bound.
A program may use at most 256 MiB of HBM per device.

```python
import jax
import jax.numpy as jnp
import numpy as np
from jax import lax

C = 512
HEADS = 16
FF = 2048
WIN = 7
SHIFT = 3
SIDE = 14
IMG_DEV = 32
IMAGES = 256
REL_SPAN = 169
N_FSDP = 8


def draw_image_count(key, part):
    count_key, order_key = jax.random.split(jax.random.fold_in(key, 17))
    counts = jax.random.randint(count_key, (N_FSDP,), 1, IMG_DEV + 1)
    ranking = jax.random.permutation(order_key, N_FSDP)
    counts = jnp.where(ranking == 0, IMG_DEV, counts)
    counts = jnp.where(ranking == 1, 1, counts)
    return counts.astype(jnp.int32)


def level_of(key, dims, cuts, smallest, high):
    factor_of = 1.0
    for axis_at, parts in cuts:
        heights = jax.random.uniform(jax.random.fold_in(jax.random.fold_in(key, 6), axis_at), (parts,), jnp.float32, smallest / len(cuts), high / len(cuts))
        factor_of = factor_of * jnp.repeat(jnp.exp(heights), dims[axis_at] // parts).reshape((-1,) + (1,) * (len(dims) - 1 - axis_at))
    return factor_of


def noise(rng, dims, scale, bound, cuts=(), held_as=jnp.bfloat16):
    drawn = jax.random.normal(rng, dims, jnp.float32) * scale
    if len(cuts) > 0:
        drawn = level_of(rng, dims, cuts, -0.22, 0.18) * drawn
    return jnp.clip(drawn, min=-bound, max=bound).astype(held_as)


def setup_inputs(seed: int = 0) -> dict:
    keys = jax.random.split(jax.random.key(seed), 17)
    return {
        "images": noise(keys[0], (IMAGES, SIDE * SIDE, C), 1.0, 6.0, ((0, 8),)),
        "attn_norm_gain": jnp.clip(1.0 + 0.15 * jax.random.normal(keys[1], (C,), jnp.float32), 0.25, 1.75).astype(jnp.bfloat16),
        "attn_norm_bias": noise(keys[2], (C,), 0.3, 1.75, ((0, 8),)),
        "qkv_weight": noise(keys[3], (C, 3, C), C ** -0.5, 0.25, ((0, 8), (2, 4))),
        "qkv_bias": noise(keys[4], (3, C), 0.3, 1.75, ((1, 4),)),
        "position_table": noise(keys[5], (REL_SPAN, HEADS), 1.0, 6.0, ((1, 4),)),
        "proj_weight": noise(keys[6], (C, C), (C // 16) ** -0.5, 1.0, ((0, 4), (1, 8))),
        "proj_bias": noise(keys[7], (C,), 0.5, 3.0, ((0, 8),)),
        "mlp_norm_gain": jnp.clip(1.0 + 0.15 * jax.random.normal(keys[8], (C,), jnp.float32), 0.25, 1.75).astype(jnp.bfloat16),
        "mlp_norm_bias": noise(keys[9], (C,), 0.3, 1.75, ((0, 8),)),
        "fc1_weight": noise(keys[10], (C, FF), C ** -0.5, 0.25, ((0, 8), (1, 4))),
        "fc1_bias": noise(keys[11], (FF,), 0.5, 3.0, ((0, 4),)),
        "fc2_weight": noise(keys[12], (FF, C), FF ** -0.5, 0.125, ((0, 4), (1, 8))),
        "fc2_bias": noise(keys[13], (C,), 0.5, 3.0, ((0, 8),)),
        "image_count": draw_image_count(jax.random.fold_in(keys[16], 71), 0),
        "out_grad": noise(keys[15], (IMAGES, SIDE * SIDE, C), 1.0, 6.0, ((0, 8),)),
    }


@jax.custom_vjp
def low(v):
    return lax.optimization_barrier(v.astype(jnp.bfloat16)).astype(jnp.float32)

@jax.custom_vjp
def low_back(v):
    return v

def low_keep(v):
    return (low(v), None)

def low_pass(kept, grad):
    return (grad,)

def back_keep(v):
    return (v, None)

def back_low(kept, grad):
    return (low(grad),)
low.defvjp(low_keep, low_pass)
low_back.defvjp(back_keep, back_low)
EPSILON = 1e-05
highest = lax.Precision.HIGHEST

def window_tables():
    offsets = np.arange(WIN)
    window_rows = np.repeat(offsets, WIN)
    window_cols = np.tile(offsets, WIN)
    relative = (window_rows[:, None] - window_rows[None, :] + WIN - 1) * (2 * WIN - 1) + (window_cols[:, None] - window_cols[None, :] + WIN - 1)
    region = np.zeros((SIDE, SIDE), np.int32)
    bounds = ((0, SIDE - WIN), (SIDE - WIN, SIDE - SHIFT), (SIDE - SHIFT, SIDE))
    region_id = 0
    for row_range in bounds:
        for col_range in bounds:
            region[row_range[0]:row_range[1], col_range[0]:col_range[1]] = region_id
            region_id = region_id + 1
    across = SIDE // WIN
    region_windows = region.reshape(across, WIN, across, WIN).transpose(0, 2, 1, 3).reshape(across * across, WIN * WIN)
    shift_mask = np.where(region_windows[:, :, None] == region_windows[:, None, :], 0.0, -100.0).astype(np.float32)
    table_hot = (relative.reshape(-1)[None, :] == np.arange((2 * WIN - 1) * (2 * WIN - 1))[:, None]).astype(np.float32)
    return (relative.astype(np.int32), shift_mask, table_hot)

def to_windows(blocks):
    leading = blocks.shape[0]
    trailing = blocks.shape[2:]
    across = SIDE // WIN
    shaped = blocks.reshape((leading, SIDE, SIDE) + trailing)
    shaped = jnp.roll(shaped, (-SHIFT, -SHIFT), axis=(1, 2))
    shaped = shaped.reshape((leading, across, WIN, across, WIN) + trailing)
    permute = (0, 1, 3, 2, 4) + tuple(range(5, 5 + len(trailing)))
    return shaped.transpose(permute).reshape((leading, across * across, WIN * WIN) + trailing)

def from_windows(blocks):
    leading = blocks.shape[0]
    trailing = blocks.shape[3:]
    across = SIDE // WIN
    shaped = blocks.reshape((leading, across, across, WIN, WIN) + trailing)
    permute = (0, 1, 3, 2, 4) + tuple(range(5, 5 + len(trailing)))
    shaped = shaped.transpose(permute).reshape((leading, SIDE, SIDE) + trailing)
    shaped = jnp.roll(shaped, (SHIFT, SHIFT), axis=(1, 2))
    return shaped.reshape((leading, SIDE * SIDE) + trailing)

def standardize(features, gain_vector, shift_term):
    centered = features - lax.optimization_barrier(jnp.mean(features, axis=-1, keepdims=True))
    variance = lax.optimization_barrier(jnp.mean(centered * centered, axis=-1, keepdims=True))
    return centered * lax.rsqrt(variance + EPSILON) * gain_vector + shift_term

def layer(inputs, attn_norm_gain, attn_norm_bias, qkv_weight, qkv_bias, position_table, proj_weight, proj_bias, mlp_norm_gain, mlp_norm_bias, fc1_weight, fc1_bias, fc2_weight, fc2_bias):
    relative, shift_mask, table_hot = window_tables()
    head_count = position_table.shape[1]
    head_size = qkv_weight.shape[2] // head_count
    score_scale = head_size ** (-0.5)
    normed = low(standardize(inputs, attn_norm_gain, attn_norm_bias))
    projected = low_back(jnp.einsum('btc,cjd->btjd', normed, qkv_weight, precision=highest) + qkv_bias)
    windowed = to_windows(projected)
    shape_heads = windowed.shape[:3] + (head_count, head_size)
    queries = low(windowed[:, :, :, 0] * score_scale).reshape(shape_heads)
    key_vectors = low(windowed[:, :, :, 1]).reshape(shape_heads)
    value_vectors = low(windowed[:, :, :, 2]).reshape(shape_heads)
    position_bias = jnp.transpose(position_table[jnp.asarray(relative)], (2, 0, 1))
    scores = jnp.einsum('bwqhd,bwkhd->bwhqk', queries, key_vectors, precision=highest)
    scores = scores + position_bias[None, None] + jnp.asarray(shift_mask)[None, :, None]
    scores = low_back(scores)
    weights = low(jax.nn.softmax(scores, axis=-1))
    mixed_heads = jnp.einsum('bwhqk,bwkhd->bwqhd', weights, value_vectors, precision=highest)
    mixed_heads = from_windows(mixed_heads.reshape(mixed_heads.shape[:3] + (head_count * head_size,)))
    mixed_heads = low_back(low(mixed_heads))
    attended = low_back(jnp.dot(mixed_heads, proj_weight, precision=highest) + proj_bias)
    residual = inputs + attended
    normed_two = low(standardize(residual, mlp_norm_gain, mlp_norm_bias))
    hidden = low_back(jnp.dot(normed_two, fc1_weight, precision=highest) + fc1_bias)
    activated = low(jax.nn.gelu(hidden, approximate=False))
    branch = low_back(jnp.dot(activated, fc2_weight, precision=highest) + fc2_bias)
    return residual + branch

def reference(images, attn_norm_gain, attn_norm_bias, qkv_weight, qkv_bias, position_table, proj_weight, proj_bias, mlp_norm_gain, mlp_norm_bias, fc1_weight, fc1_bias, fc2_weight, fc2_bias, image_count, out_grad):
    params = tuple((parameter.astype(jnp.float32) for parameter in (attn_norm_gain, attn_norm_bias, qkv_weight, qkv_bias, position_table, proj_weight, proj_bias, mlp_norm_gain, mlp_norm_bias, fc1_weight, fc1_bias, fc2_weight, fc2_bias)))
    groups = images.reshape(N_FSDP, IMG_DEV, SIDE * SIDE, C)
    cotangents = out_grad.reshape(N_FSDP, IMG_DEV, SIDE * SIDE, C)
    alive_mask = (jnp.arange(IMG_DEV, dtype=jnp.int32)[None, :] < image_count[:, None]).astype(jnp.float32)

    def visit_group(totals, group_item):
        batch_rows, cotangent, living = group_item
        outputs, pullback = jax.vjp(layer, batch_rows.astype(jnp.float32), *params)
        weight_mask = living[:, None, None]
        gradients = pullback(cotangent.astype(jnp.float32) * weight_mask)
        totals = tuple((total + gradient for total, gradient in zip(totals, gradients[1:])))
        return (totals, ((outputs * weight_mask).astype(jnp.bfloat16), gradients[0].astype(jnp.bfloat16)))
    initial = tuple((jnp.zeros_like(parameter) for parameter in params))
    totals, (outputs, input_grads) = lax.scan(visit_group, initial, (groups, cotangents, alive_mask))
    return (outputs.reshape(images.shape), input_grads.reshape(images.shape), totals[0], totals[1], totals[2], totals[3], totals[4], totals[5], totals[6], totals[7], totals[8], totals[9], totals[10], totals[11], totals[12])
```

```python
import functools
import jax
import jax.numpy as jnp
import numpy as np
from jax import lax
from jax.experimental import pallas as pl
from jax.experimental.pallas import tpu as pltpu

HD = 32
WIN = 7
SHIFT = 3
SIDE = 14
AREA = WIN * WIN
ROWS = 64
GROUP = 4
EPSILON = 1e-05
F32 = jnp.float32
BF16 = jnp.bfloat16
PADDED = -1e30


def window_constants():
    offsets = np.arange(WIN)
    rows, cols = np.repeat(offsets, WIN), np.tile(offsets, WIN)
    relative = (rows[:, None] - rows[None, :] + WIN - 1) * (2 * WIN - 1) + (
        cols[:, None] - cols[None, :] + WIN - 1
    )
    span = (2 * WIN - 1) ** 2
    hot = np.zeros((span, ROWS, ROWS), np.float32)
    hot[:, :AREA, :AREA] = (relative.T[None] == np.arange(span)[:, None, None])
    region = np.zeros((SIDE, SIDE), np.int32)
    bounds = ((0, SIDE - WIN), (SIDE - WIN, SIDE - SHIFT), (SIDE - SHIFT, SIDE))
    for a, rr in enumerate(bounds):
        for b, cc in enumerate(bounds):
            region[rr[0] : rr[1], cc[0] : cc[1]] = 3 * a + b
    across = SIDE // WIN
    cut = region.reshape(across, WIN, across, WIN).transpose(0, 2, 1, 3).reshape(across * across, AREA)
    mask = np.zeros((across * across, ROWS, ROWS), np.float32)
    mask[:, :AREA, :AREA] = np.where(cut[:, :, None] == cut[:, None, :], 0.0, -100.0)
    mask[:, AREA:, :] = PADDED
    mask = np.tile(mask, (1, 1, GROUP))
    perm = np.zeros((across * across * ROWS, SIDE * SIDE), np.float32)
    for w in range(across * across):
        for s in range(AREA):
            r = ((w // across) * WIN + s // WIN + SHIFT) % SIDE
            c = ((w % across) * WIN + s % WIN + SHIFT) % SIDE
            perm[w * ROWS + s, r * SIDE + c] = 1.0
    return hot, mask, perm


def dot(a, b, dims=((1,), (0,))):
    return lax.dot_general(a, b, (dims, ((), ())), preferred_element_type=F32)


NT = ((1,), (1,))
TN = ((0,), (0,))


def standardize(x):
    c = x - jnp.mean(x, axis=-1, keepdims=True)
    inv = lax.rsqrt(jnp.mean(c * c, axis=-1, keepdims=True) + EPSILON)
    return c * inv, inv


def head_masks(dtype):
    lane = lax.broadcasted_iota(jnp.int32, (1, GROUP * HD), 1) // HD
    return [(lane == h).astype(F32).astype(dtype) for h in range(GROUP)]


def spread(x, masks):
    return jnp.concatenate([x * m for m in masks], axis=0)


def gather_heads(y, masks):
    out = y[:ROWS] * masks[0]
    for h in range(1, GROUP):
        out = out + y[h * ROWS : (h + 1) * ROWS] * masks[h]
    return out


def attn_fwd_kernel(img_ref, w_ref, b_ref, vec_ref, tab_ref, mask_ref, perm_ref, permt_ref, qkv_ref, p_ref, mix_ref, bias_scr, o_scr):
    n_win = mask_ref.shape[0]
    n_grp = w_ref.shape[1] // (3 * GROUP * HD)
    gw = GROUP * HD

    @pl.when(pl.program_id(0) == 0)
    def _():
        for g in range(n_grp):
            full = jnp.concatenate([tab_ref[g * GROUP + h] for h in range(GROUP)], axis=1)
            for w in range(n_win):
                bias_scr[g, w] = full + mask_ref[w]

    x = img_ref[0].astype(F32)
    xhat, _ = standardize(x)
    normed = (xhat * vec_ref[0:1] + vec_ref[1:2]).astype(BF16)
    xp = dot(perm_ref[...], normed).astype(BF16)
    mb, mf = head_masks(BF16), head_masks(F32)
    for g in range(n_grp):
        c0 = g * 3 * gw
        acc = dot(xp, w_ref[:, c0 : c0 + 3 * gw]) + b_ref[0:1, c0 : c0 + 3 * gw]
        q = (acc[:, :gw] * (HD ** -0.5)).astype(BF16)
        k = acc[:, gw : 2 * gw].astype(BF16)
        v = acc[:, 2 * gw :].astype(BF16)
        qkv_ref[0, :, c0 : c0 + gw] = q
        qkv_ref[0, :, c0 + gw : c0 + 2 * gw] = k
        qkv_ref[0, :, c0 + 2 * gw : c0 + 3 * gw] = v
        for w in range(n_win):
            r = slice(w * ROWS, (w + 1) * ROWS)
            s = dot(k[r], spread(q[r], mb), NT) + bias_scr[g, w]
            e = jnp.exp(s - jnp.max(s, axis=0, keepdims=True))
            p = (e * (1.0 / jnp.sum(e, axis=0, keepdims=True))).astype(BF16)
            p_ref[0, g, w] = p
            o = gather_heads(dot(p, v[r], TN), mf)
            o_scr[r, g * gw : (g + 1) * gw] = o.astype(BF16)
    mix_ref[0] = dot(permt_ref[...], o_scr[...]).astype(BF16)


def attn_fwd(images, wqkv, bqkv, vecs, table, consts):
    mask, perm, permt = consts
    n = images.shape[0]
    t, c = images.shape[1:]
    n_win, n_grp = mask.shape[0], wqkv.shape[1] // (3 * GROUP * HD)
    rows = n_win * ROWS
    whole = lambda a: pl.BlockSpec(a.shape, lambda i: (0,) * a.ndim)
    return pl.pallas_call(
        attn_fwd_kernel,
        grid=(n,),
        in_specs=[pl.BlockSpec((1, t, c), lambda i: (i, 0, 0))] + [whole(a) for a in (wqkv, bqkv, vecs, table, mask, perm, permt)],
        out_specs=[
            pl.BlockSpec((1, rows, wqkv.shape[1]), lambda i: (i, 0, 0)),
            pl.BlockSpec((1, n_grp, n_win, ROWS, GROUP * ROWS), lambda i: (i, 0, 0, 0, 0)),
            pl.BlockSpec((1, t, c), lambda i: (i, 0, 0)),
        ],
        out_shape=[
            jax.ShapeDtypeStruct((n, rows, wqkv.shape[1]), BF16),
            jax.ShapeDtypeStruct((n, n_grp, n_win, ROWS, GROUP * ROWS), BF16),
            jax.ShapeDtypeStruct((n, t, c), BF16),
        ],
        scratch_shapes=[
            pltpu.VMEM((n_grp, n_win, ROWS, GROUP * ROWS), F32),
            pltpu.VMEM((rows, c), BF16),
        ],
        compiler_params=pltpu.CompilerParams(vmem_limit_bytes=48 << 20),
        name="attn_fwd",
    )(images, wqkv, bqkv, vecs, table, mask, perm, permt)


SQRT_HALF = float(np.sqrt(0.5))
INV_SQRT_2PI = float(1.0 / np.sqrt(2.0 * np.pi))


def mlp_kernel(live_ref, img_ref, og_ref, mix_ref, wp_ref, w1_ref, w2_ref, vec_ref, b1_ref,
               out_ref, gres_ref, gmix_ref, dwp_ref, dw1_ref, dw2_ref, dvec_ref, db1_ref,
               *, ipb, chunk):
    step = pl.program_id(0)
    n_tok, c = img_ref.shape[1:]
    rows = ipb * n_tok

    @pl.when(step == 0)
    def _():
        dwp_ref[...] = jnp.zeros_like(dwp_ref)
        dw1_ref[...] = jnp.zeros_like(dw1_ref)
        dw2_ref[...] = jnp.zeros_like(dw2_ref)
        dvec_ref[...] = jnp.zeros_like(dvec_ref)
        db1_ref[...] = jnp.zeros_like(db1_ref)

    flat = lambda ref: jnp.concatenate([ref[i] for i in range(ipb)], axis=0) if ipb > 1 else ref[0]
    live = jnp.concatenate(
        [jnp.full((n_tok, 1), 1.0, F32) * live_ref[step * ipb + i] for i in range(ipb)], axis=0
    )
    mixed = flat(mix_ref)
    up = flat(og_ref).astype(F32) * live
    up16 = up.astype(BF16)
    res = flat(img_ref).astype(F32) + (dot(mixed, wp_ref[...], NT) + vec_ref[2:3])
    xhat, inv = standardize(res)
    normed = (xhat * vec_ref[3:4] + vec_ref[4:5]).astype(BF16)
    branch = jnp.zeros((rows, c), F32)
    dn = jnp.zeros((rows, c), F32)
    for c0 in range(0, w1_ref.shape[1], chunk):
        cs = slice(c0, c0 + chunk)
        hid = dot(normed, w1_ref[:, cs]) + b1_ref[0:1, cs]
        cdf = 0.5 * (1.0 + lax.erf(hid * SQRT_HALF))
        act = (hid * cdf).astype(BF16)
        slope = cdf + hid * (jnp.exp(-0.5 * hid * hid) * INV_SQRT_2PI)
        branch = branch + dot(act, w2_ref[:, cs], NT)
        dw2_ref[:, cs] += dot(up16, act, TN)
        dh = (dot(up16, w2_ref[:, cs]) * slope).astype(BF16)
        db1_ref[0:1, cs] += jnp.sum(dh.astype(F32), axis=0, keepdims=True)
        dw1_ref[:, cs] += dot(normed, dh, TN)
        dn = dn + dot(dh, w1_ref[:, cs], NT)
    out = (live * (res + (branch + vec_ref[5:6]))).astype(BF16)
    d = dn * vec_ref[3:4]
    gres = up + inv * (d - jnp.mean(d, axis=-1, keepdims=True) - xhat * jnp.mean(d * xhat, axis=-1, keepdims=True))
    gatt = gres.astype(BF16)
    dwp_ref[...] += dot(gatt, mixed, TN)
    gmix = dot(gatt, wp_ref[...]).astype(BF16)
    for i in range(ipb):
        r = slice(i * n_tok, (i + 1) * n_tok)
        out_ref[i] = out[r]
        gres_ref[i] = gres[r]
        gmix_ref[i] = gmix[r]
    dvec_ref[2:3] += jnp.sum(gatt.astype(F32), axis=0, keepdims=True)
    dvec_ref[3:4] += jnp.sum(dn * xhat, axis=0, keepdims=True)
    dvec_ref[4:5] += jnp.sum(dn, axis=0, keepdims=True)
    dvec_ref[5:6] += jnp.sum(up, axis=0, keepdims=True)


def mlp(live, images, out_grad, mixed, wp, w1, w2, vecs, b1, ipb=2, chunk=512):
    n, t, c = images.shape
    ff = w1.shape[1]
    whole = lambda s: pl.BlockSpec(s, lambda i: (0,) * len(s))
    once = lambda s: pl.BlockSpec(s, lambda i: (0,) * len(s), pipeline_mode=pl.Buffered(1))
    blk = pl.BlockSpec((ipb, t, c), lambda i: (i, 0, 0))
    return pl.pallas_call(
        functools.partial(mlp_kernel, ipb=ipb, chunk=chunk),
        grid=(n // ipb,),
        in_specs=[pl.BlockSpec(memory_space=pltpu.SMEM), blk, blk, blk] + [once(a.shape) for a in (wp, w1, w2, vecs, b1)],
        out_specs=[blk, blk, blk] + [whole(s) for s in ((c, c), (c, ff), (c, ff), (8, c), (1, ff))],
        out_shape=[
            jax.ShapeDtypeStruct((n, t, c), BF16),
            jax.ShapeDtypeStruct((n, t, c), F32),
            jax.ShapeDtypeStruct((n, t, c), BF16),
            jax.ShapeDtypeStruct((c, c), F32),
            jax.ShapeDtypeStruct((c, ff), F32),
            jax.ShapeDtypeStruct((c, ff), F32),
            jax.ShapeDtypeStruct((8, c), F32),
            jax.ShapeDtypeStruct((1, ff), F32),
        ],
        compiler_params=pltpu.CompilerParams(vmem_limit_bytes=56 << 20),
        name="mlp",
    )(live, images, out_grad, mixed, wp, w1, w2, vecs, b1)


def attn_bwd_kernel(img_ref, gres_ref, gmix_ref, qkv_ref, p_ref, w_ref, vec_ref, perm_ref, permt_ref,
                    gin_ref, dw_ref, dvec_ref, db_ref, dtab_ref, dqkv_scr):
    n_grp, n_win = p_ref.shape[1:3]
    gw = GROUP * HD

    @pl.when(pl.program_id(0) == 0)
    def _():
        dw_ref[...] = jnp.zeros_like(dw_ref)
        dvec_ref[...] = jnp.zeros_like(dvec_ref)
        db_ref[...] = jnp.zeros_like(db_ref)
        dtab_ref[...] = jnp.zeros_like(dtab_ref)

    mb, mf = head_masks(BF16), head_masks(F32)
    x = img_ref[0].astype(F32)
    xhat, inv = standardize(x)
    normed = (xhat * vec_ref[0:1] + vec_ref[1:2]).astype(BF16)
    xp = dot(perm_ref[...], normed).astype(BF16)
    gm = dot(perm_ref[...], gmix_ref[0]).astype(BF16)
    for g in range(n_grp):
        c0 = g * 3 * gw
        tab = jnp.zeros((ROWS, GROUP * ROWS), F32)
        for w in range(n_win):
            r = slice(w * ROWS, (w + 1) * ROWS)
            q = qkv_ref[0, r, c0 : c0 + gw]
            k = qkv_ref[0, r, c0 + gw : c0 + 2 * gw]
            v = qkv_ref[0, r, c0 + 2 * gw : c0 + 3 * gw]
            do = spread(gm[r, g * gw : (g + 1) * gw], mb)
            p = p_ref[0, g, w]
            dqkv_scr[r, c0 + 2 * gw : c0 + 3 * gw] = dot(p, do).astype(BF16)
            dp = dot(v, do, NT)
            pf = p.astype(F32)
            ds = pf * (dp - jnp.sum(pf * dp, axis=0, keepdims=True))
            tab = tab + ds
            ds16 = ds.astype(BF16)
            dqkv_scr[r, c0 + gw : c0 + 2 * gw] = dot(ds16, spread(q, mb)).astype(BF16)
            dq = gather_heads(dot(ds16, k, TN), mf) * (HD ** -0.5)
            dqkv_scr[r, c0 : c0 + gw] = dq.astype(BF16)
        dtab_ref[g] += tab
    dqkv = dqkv_scr[...]
    db_ref[0:1] += jnp.sum(dqkv.astype(F32), axis=0, keepdims=True)
    dw_ref[...] += dot(xp, dqkv, TN)
    dn = dot(dqkv, w_ref[...], NT)
    hi = dn.astype(BF16)
    lo = (dn - hi.astype(F32)).astype(BF16)
    dn = dot(permt_ref[...], hi) + dot(permt_ref[...], lo)
    d = dn * vec_ref[0:1]
    gin = inv * (d - jnp.mean(d, axis=-1, keepdims=True) - xhat * jnp.mean(d * xhat, axis=-1, keepdims=True))
    gin_ref[0] = (gres_ref[0] + gin).astype(BF16)
    dvec_ref[0:1] += jnp.sum(dn * xhat, axis=0, keepdims=True)
    dvec_ref[1:2] += jnp.sum(dn, axis=0, keepdims=True)


def attn_bwd(images, gres, gmix, qkv, p, wqkv, vecs, consts):
    _, perm, permt = consts
    n, t, c = images.shape
    rows, cols = qkv.shape[1:]
    n_grp, n_win = p.shape[1:3]
    whole = lambda s: pl.BlockSpec(s, lambda i: (0,) * len(s))
    blk = pl.BlockSpec((1, t, c), lambda i: (i, 0, 0))
    return pl.pallas_call(
        attn_bwd_kernel,
        grid=(n,),
        in_specs=[blk, blk, blk, pl.BlockSpec((1, rows, cols), lambda i: (i, 0, 0)),
                  pl.BlockSpec((1,) + p.shape[1:], lambda i: (i, 0, 0, 0, 0))] + [whole(a.shape) for a in (wqkv, vecs, perm, permt)],
        out_specs=[blk] + [whole(s) for s in ((c, cols), (8, c), (1, cols), (n_grp, ROWS, GROUP * ROWS))],
        out_shape=[
            jax.ShapeDtypeStruct((n, t, c), BF16),
            jax.ShapeDtypeStruct((c, cols), F32),
            jax.ShapeDtypeStruct((8, c), F32),
            jax.ShapeDtypeStruct((1, cols), F32),
            jax.ShapeDtypeStruct((n_grp, ROWS, GROUP * ROWS), F32),
        ],
        scratch_shapes=[pltpu.VMEM((rows, cols), BF16)],
        compiler_params=pltpu.CompilerParams(vmem_limit_bytes=48 << 20),
        name="attn_bwd",
    )(images, gres, gmix, qkv, p, wqkv, vecs, perm, permt)


def per_device(
    images,
    attn_norm_gain,
    attn_norm_bias,
    qkv_weight,
    qkv_bias,
    position_table,
    proj_weight,
    proj_bias,
    mlp_norm_gain,
    mlp_norm_bias,
    fc1_weight,
    fc1_bias,
    fc2_weight,
    fc2_bias,
    image_count,
    out_grad,
    *,
    fsdp,
    tp,
):
    both = ("fsdp", "tp")
    hot, mask, perm = window_constants()
    mask = jnp.asarray(mask)
    hot = jnp.asarray(hot)
    perm16 = jnp.asarray(perm, BF16)
    consts = (mask, perm16, jnp.asarray(perm.T, BF16))
    gw = GROUP * HD
    cut = qkv_weight.shape[0]
    width = attn_norm_gain.shape[0] * fsdp
    ff = fc1_bias.shape[0] * tp
    ff_cut = ff // tp
    n_slots = images.shape[0]
    mine = n_slots // tp
    first = lax.axis_index("tp") * mine
    img = lax.dynamic_slice_in_dim(images, first, mine, 0)
    cot = lax.dynamic_slice_in_dim(out_grad, first, mine, 0)
    live = (first + jnp.arange(mine, dtype=jnp.int32) < image_count[0]).astype(F32)

    pack = jnp.concatenate(
        [qkv_weight.reshape(cut, 3 * gw), proj_weight.T, fc1_weight, fc2_weight.T], axis=1
    )
    full = lax.all_gather(pack, both, axis=0, tiled=False).reshape(fsdp, tp, cut, pack.shape[1])
    full = full.transpose(0, 2, 1, 3)
    piece = lambda a, b: full[..., a:b].reshape(width, tp * (b - a))
    w_qkv = piece(0, 3 * gw)
    w_proj = piece(3 * gw, 4 * gw)
    w_one = piece(4 * gw, 4 * gw + ff_cut)
    w_two = piece(4 * gw + ff_cut, 4 * gw + 2 * ff_cut)
    zero = jnp.zeros_like(attn_norm_gain)
    vecs = jnp.stack(
        [attn_norm_gain, attn_norm_bias, proj_bias, mlp_norm_gain, mlp_norm_bias, fc2_bias, zero, zero]
    )
    vecs = lax.all_gather(vecs, "fsdp", axis=1, tiled=True).astype(F32)
    tail = jnp.concatenate([qkv_bias.reshape(-1), fc1_bias, position_table.reshape(-1)])
    tail = lax.all_gather(tail, "tp", axis=0, tiled=False)
    n_qkv = qkv_bias.size
    b_qkv = tail[:, :n_qkv].reshape(1, tp * n_qkv).astype(F32)
    b_one = tail[:, n_qkv : n_qkv + ff_cut].reshape(1, ff).astype(F32)
    table = tail[:, n_qkv + ff_cut :].reshape((tp,) + position_table.shape)
    table = table.transpose(0, 2, 1).reshape(-1, position_table.shape[0])
    table = jnp.dot(table, hot.astype(BF16).reshape(hot.shape[0], -1), preferred_element_type=F32)
    table = table.reshape(-1, ROWS, ROWS)

    qkv, probs, mixed = attn_fwd(img, w_qkv, b_qkv, vecs, table, consts)
    out, gres, gmix, d_proj, d_one, d_two, dv_two, db_one = mlp(
        live, img, cot, mixed, w_proj, w_one, w_two, vecs, b_one
    )
    gin, d_qkv, dv_one, db_qkv, d_tab = attn_bwd(img, gres, gmix, qkv, probs, w_qkv, vecs, consts)

    output = lax.all_gather(out, "tp", axis=0, tiled=True)
    images_grad = lax.all_gather(gin, "tp", axis=0, tiled=True)
    split = lambda a: a.reshape(fsdp, cut, tp, a.shape[1] // tp)
    grads = jnp.concatenate([split(a) for a in (d_qkv, d_proj, d_one, d_two)], axis=3)
    grads = grads.transpose(0, 2, 1, 3).reshape(fsdp * tp * cut, pack.shape[1])
    grads = lax.psum_scatter(grads, both, scatter_dimension=0, tiled=True)
    d_tab = jnp.einsum(
        "gjhi,rji->rgh",
        d_tab.reshape(-1, ROWS, GROUP, ROWS),
        hot,
        precision=lax.Precision.HIGHEST,
    ).reshape(hot.shape[0], -1)
    dvec = jnp.concatenate([dv_one[:2], dv_two[2:6]])
    small = lax.psum(
        jnp.concatenate([dvec.reshape(-1), db_qkv[0], db_one[0], d_tab.T.reshape(-1)]), both
    )
    dvec = small[: 6 * width].reshape(6, width)
    dvec = lax.dynamic_slice_in_dim(dvec, lax.axis_index("fsdp") * cut, cut, 1)
    at = 6 * width
    t = lax.axis_index("tp")
    dqkv_bias = lax.dynamic_slice_in_dim(small, at + t * n_qkv, n_qkv, 0).reshape(qkv_bias.shape)
    at = at + tp * n_qkv
    dfc1_bias = lax.dynamic_slice_in_dim(small, at + t * ff_cut, ff_cut, 0)
    at = at + ff
    size = position_table.size
    dtable = lax.dynamic_slice_in_dim(small, at + t * size, size, 0)
    dtable = dtable.reshape(position_table.shape[::-1]).T
    return (
        output,
        images_grad,
        dvec[0],
        dvec[1],
        grads[:, : 3 * gw].reshape(qkv_weight.shape),
        dqkv_bias,
        dtable,
        grads[:, 3 * gw : 4 * gw].T,
        dvec[2],
        dvec[3],
        dvec[4],
        grads[:, 4 * gw : 4 * gw + ff_cut],
        dfc1_bias,
        grads[:, 4 * gw + ff_cut :].T,
        dvec[5],
    )


def solution(mesh):
    P = jax.sharding.PartitionSpec
    return jax.shard_map(
        functools.partial(per_device, fsdp=mesh.shape["fsdp"], tp=mesh.shape["tp"]),
        mesh=mesh,
        in_specs=(
            P("fsdp", None, None),
            P("fsdp"),
            P("fsdp"),
            P("fsdp", None, "tp"),
            P(None, "tp"),
            P(None, "tp"),
            P("tp", "fsdp"),
            P("fsdp"),
            P("fsdp"),
            P("fsdp"),
            P("fsdp", "tp"),
            P("tp"),
            P("tp", "fsdp"),
            P("fsdp"),
            P("fsdp"),
            P("fsdp", None, None),
        ),
        out_specs=(
            P("fsdp", None, None),
            P("fsdp", None, None),
            P("fsdp"),
            P("fsdp"),
            P("fsdp", None, "tp"),
            P(None, "tp"),
            P(None, "tp"),
            P("tp", "fsdp"),
            P("fsdp"),
            P("fsdp"),
            P("fsdp"),
            P("fsdp", "tp"),
            P("tp"),
            P("tp", "fsdp"),
            P("fsdp"),
        ),
        check_vma=False,
    )
```

```python
import functools
import jax
import jax.numpy as jnp
import numpy as np
from jax import lax
from jax.experimental import pallas as pl
from jax.experimental.pallas import tpu as pltpu

HD = 32
WIN = 7
SHIFT = 3
SIDE = 14
AREA = WIN * WIN
ROWS = 64
GROUP = 4
EPSILON = 1e-05
F32 = jnp.float32
BF16 = jnp.bfloat16
PADDED = -1e30
MESH = pl.DeviceIdType.MESH


def window_constants():
    offsets = np.arange(WIN)
    rows, cols = np.repeat(offsets, WIN), np.tile(offsets, WIN)
    relative = (rows[:, None] - rows[None, :] + WIN - 1) * (2 * WIN - 1) + (
        cols[:, None] - cols[None, :] + WIN - 1
    )
    span = (2 * WIN - 1) ** 2
    index = np.full((ROWS, ROWS), span, np.int32)
    index[:AREA, :AREA] = relative.T
    region = np.zeros((SIDE, SIDE), np.int32)
    bounds = ((0, SIDE - WIN), (SIDE - WIN, SIDE - SHIFT), (SIDE - SHIFT, SIDE))
    for a, rr in enumerate(bounds):
        for b, cc in enumerate(bounds):
            region[rr[0] : rr[1], cc[0] : cc[1]] = 3 * a + b
    across = SIDE // WIN
    cut = region.reshape(across, WIN, across, WIN).transpose(0, 2, 1, 3).reshape(across * across, AREA)
    mask = np.zeros((across * across, ROWS, ROWS), np.float32)
    mask[:, :AREA, :AREA] = np.where(cut[:, :, None] == cut[:, None, :], 0.0, -100.0)
    mask[:, AREA:, :] = PADDED
    mask = np.tile(mask, (1, 1, GROUP))
    perm = np.zeros((across * across * ROWS, SIDE * SIDE), np.float32)
    for w in range(across * across):
        for s in range(AREA):
            r = ((w // across) * WIN + s // WIN + SHIFT) % SIDE
            c = ((w % across) * WIN + s % WIN + SHIFT) % SIDE
            perm[w * ROWS + s, r * SIDE + c] = 1.0
    return index, mask, perm


def dot(a, b, dims=((1,), (0,))):
    return lax.dot_general(a, b, (dims, ((), ())), preferred_element_type=F32)


NT = ((1,), (1,))
TN = ((0,), (0,))


def standardize(x):
    c = x - jnp.mean(x, axis=-1, keepdims=True)
    inv = lax.rsqrt(jnp.mean(c * c, axis=-1, keepdims=True) + EPSILON)
    return c * inv, inv


def head_masks(dtype):
    lane = lax.broadcasted_iota(jnp.int32, (1, GROUP * HD), 1) // HD
    return [(lane == h).astype(F32).astype(dtype) for h in range(GROUP)]


def spread(x, masks):
    return jnp.concatenate([x * m for m in masks], axis=0)


def gather_heads(y, masks):
    out = y[:ROWS] * masks[0]
    for h in range(1, GROUP):
        out = out + y[h * ROWS : (h + 1) * ROWS] * masks[h]
    return out


def bits_of(n):
    return [1 << b for b in reversed(range(n.bit_length() - 1))]

class Cube:
    def __init__(self, fsdp, tp):
        self.f, self.t = lax.axis_index("fsdp"), lax.axis_index("tp")
        self.digits = [("tp", b) for b in bits_of(tp)] + [("fsdp", b) for b in bits_of(fsdp)]
        self.own = [lax.rem((self.t if a == "tp" else self.f) // b, 2) for a, b in self.digits]
        self.count = len(self.digits)
        self.n_t = len(bits_of(tp))

    def partner(self, k):
        axis, b = self.digits[k]
        step = b * (1 - 2 * self.own[k])
        if axis == "tp":
            return (self.f, self.t + step)
        return (self.f + step, self.t)

    def at(self, free, flip=None):
        out = []
        for k in range(self.count):
            if k in free:
                out.append(slice(None))
            else:
                out.append(1 - self.own[k] if k == flip else self.own[k])
        return tuple(out)


def greet(cube, digits):
    bar = pltpu.get_barrier_semaphore()
    for k in digits:
        pl.semaphore_signal(bar, inc=1, device_id=cube.partner(k), device_id_type=MESH)
    pl.semaphore_wait(bar, len(digits))


def gather_orders(cube):
    t, f = list(range(cube.n_t)), list(range(cube.n_t, cube.count))
    return (f + t, f[:-1] + t[:-1] + f[-1:] + t[-1:])


class Gather:
    def __init__(self, cube, full, chunks, send, recv):
        self.cube, self.full, self.chunks, self.send, self.recv = cube, full, chunks, send, recv
        self.orders = gather_orders(cube)

    def copies(self, c, s):
        lo, hi = self.chunks[c]
        rows = self.full.shape[self.cube.count]
        half = rows // 2
        for h, order in enumerate(self.orders):
            ref = self.full.at[self.cube.at(order[:s]) + (pl.ds(h * half, half), pl.ds(lo, hi - lo))]
            i = (c * self.cube.count + s) * 2 + h
            yield pltpu.make_async_remote_copy(ref, ref, self.send.at[i], self.recv.at[i],
                device_id=self.cube.partner(order[s]), device_id_type=MESH)

    def start(self, c, s):
        for copy in self.copies(c, s):
            copy.start()

    def wait(self, c, s):
        for copy in self.copies(c, s):
            copy.wait()

    def plan(self):
        n = self.cube.count
        return sorted(((c, s) for c in range(len(self.chunks)) for s in range(n + 1)), key=lambda e: (e[0] + e[1], e[0]))

    def advance(self, c, s):
        if s > 0:
            self.wait(c, s - 1)
        if s < self.cube.count:
            self.start(c, s)


def ag_kernel(pack_ref, full_ref, local, send, recv, *, fsdp, tp, chunks):
    cube = Cube(fsdp, tp)
    own = pltpu.make_async_copy(pack_ref, full_ref.at[cube.at(())], local)
    own.start()
    greet(cube, range(cube.count))
    own.wait()
    g = Gather(cube, full_ref, chunks, send, recv)
    for c, s in g.plan():
        g.advance(c, s)


def all_gather(pack, fsdp, tp, chunks):
    digits = len(bits_of(fsdp)) + len(bits_of(tp))
    n = len(chunks) * digits * 2
    return pl.pallas_call(
        functools.partial(ag_kernel, fsdp=fsdp, tp=tp, chunks=chunks),
        in_specs=[pl.BlockSpec(memory_space=pl.ANY)],
        out_specs=pl.BlockSpec(memory_space=pl.ANY),
        out_shape=jax.ShapeDtypeStruct((2,) * digits + pack.shape, pack.dtype),
        scratch_shapes=[pltpu.SemaphoreType.DMA, pltpu.SemaphoreType.DMA((n,)), pltpu.SemaphoreType.DMA((n,))],
        compiler_params=pltpu.CompilerParams(collective_id=1, has_side_effects=True),
        name="weights",
    )(pack)
def attn_fwd_kernel(img_ref, w_ref, b_ref, vec_ref, tab_ref, mask_ref, perm_ref, permt_ref, qkv_ref, p_ref, mix_ref, bias_scr, o_scr):
    n_win = mask_ref.shape[0]
    n_grp = w_ref.shape[0]
    gw = GROUP * HD

    @pl.when(pl.program_id(0) == 0)
    def _():
        for g in range(n_grp):
            full = jnp.concatenate([tab_ref[g * GROUP + h] for h in range(GROUP)], axis=1)
            for w in range(n_win):
                bias_scr[g, w] = full + mask_ref[w]

    x = img_ref[0].astype(F32)
    xhat, _ = standardize(x)
    normed = (xhat * vec_ref[0:1] + vec_ref[1:2]).astype(BF16)
    xp = dot(perm_ref[...], normed).astype(BF16)
    mb, mf = head_masks(BF16), head_masks(F32)
    for g in range(n_grp):
        c0 = g * 3 * gw
        acc = dot(xp, w_ref[g]) + b_ref[0:1, c0 : c0 + 3 * gw]
        q = (acc[:, :gw] * (HD ** -0.5)).astype(BF16)
        k = acc[:, gw : 2 * gw].astype(BF16)
        v = acc[:, 2 * gw :].astype(BF16)
        qkv_ref[0, :, c0 : c0 + gw] = q
        qkv_ref[0, :, c0 + gw : c0 + 2 * gw] = k
        qkv_ref[0, :, c0 + 2 * gw : c0 + 3 * gw] = v
        for w in range(n_win):
            r = slice(w * ROWS, (w + 1) * ROWS)
            s = dot(k[r], spread(q[r], mb), NT) + bias_scr[g, w]
            e = jnp.exp(s - jnp.max(s, axis=0, keepdims=True))
            p = (e * (1.0 / jnp.sum(e, axis=0, keepdims=True))).astype(BF16)
            p_ref[0, g, w] = p
            o = gather_heads(dot(p, v[r], TN), mf)
            o_scr[r, g * gw : (g + 1) * gw] = o.astype(BF16)
    mix_ref[0] = dot(permt_ref[...], o_scr[...]).astype(BF16)


def attn_fwd(images, w_all, bqkv, vecs, table, consts):
    mask, perm, permt = consts
    n = images.shape[0]
    t, c = images.shape[1:]
    n_win, n_grp = mask.shape[0], w_all.shape[0]
    cols = n_grp * 3 * GROUP * HD
    rows = n_win * ROWS
    whole = lambda a: pl.BlockSpec(a.shape, lambda i: (0,) * a.ndim)
    return pl.pallas_call(
        attn_fwd_kernel,
        grid=(n,),
        in_specs=[pl.BlockSpec((1, t, c), lambda i: (i, 0, 0)), pl.BlockSpec((n_grp, c, 3 * GROUP * HD), lambda i: (0, 0, 0))]
        + [whole(a) for a in (bqkv, vecs, table, mask, perm, permt)],
        out_specs=[
            pl.BlockSpec((1, rows, cols), lambda i: (i, 0, 0)),
            pl.BlockSpec((1, n_grp, n_win, ROWS, GROUP * ROWS), lambda i: (i, 0, 0, 0, 0)),
            pl.BlockSpec((1, t, c), lambda i: (i, 0, 0)),
        ],
        out_shape=[
            jax.ShapeDtypeStruct((n, rows, cols), BF16),
            jax.ShapeDtypeStruct((n, n_grp, n_win, ROWS, GROUP * ROWS), BF16),
            jax.ShapeDtypeStruct((n, t, c), BF16),
        ],
        scratch_shapes=[
            pltpu.VMEM((n_grp, n_win, ROWS, GROUP * ROWS), F32),
            pltpu.VMEM((rows, c), BF16),
        ],
        compiler_params=pltpu.CompilerParams(vmem_limit_bytes=48 << 20),
        name="attn_fwd",
    )(images, w_all, bqkv, vecs, table, mask, perm, permt)


SQRT_HALF = float(np.sqrt(0.5))
INV_SQRT_2PI = float(1.0 / np.sqrt(2.0 * np.pi))


class Spread:
    def __init__(self, cube, full, send, recv):
        self.cube, self.full, self.send, self.recv = cube, full, send, recv
        self.stages = cube.n_t

    def ref(self, s, i):
        own = self.cube.own
        return self.full.at[tuple(slice(None) if k < s else own[k] for k in range(self.stages)) + (i,)]

    def copy(self, s, i):
        ref = self.ref(s, i)
        return pltpu.make_async_remote_copy(
            ref, ref, self.send.at[s, i], self.recv.at[s, i], device_id=self.cube.partner(s), device_id_type=MESH
        )


def mlp_kernel(live_ref, img_ref, og_ref, mix_ref, w1_ref, w2_ref, wp_ref, vec_ref, b1_ref,
               full_ref, gres_ref, gmix_ref, grad_ref, dvec_ref, db1_ref,
               dw1, dw2, dwp, wp, out_scr, local, send, recv, *, ipb, fsdp, tp):
    step, steps = pl.program_id(0), pl.num_programs(0)
    n_tok, c = img_ref.shape[1:]
    rows = ipb * n_tok
    n_grp, _, chunk = w1_ref.shape
    cube = Cube(fsdp, tp)
    spread_out = Spread(cube, full_ref, send, recv)

    def keep(i):
        return pltpu.make_async_copy(out_scr.at[i], spread_out.ref(0, i), local.at[i])

    @pl.when(step == 0)
    def _():
        greet(cube, range(cube.n_t))
        dw1[...] = jnp.zeros_like(dw1)
        dw2[...] = jnp.zeros_like(dw2)
        dwp[...] = jnp.zeros_like(dwp)
        dvec_ref[...] = jnp.zeros_like(dvec_ref)
        db1_ref[...] = jnp.zeros_like(db1_ref)
        for g in range(n_grp):
            wp[:, g * GROUP * HD : (g + 1) * GROUP * HD] = wp_ref[g]

    @pl.when(step >= 1)
    def _():
        keep(step - 1).wait()
        spread_out.copy(0, step - 1).start()

    for s in range(1, cube.n_t):

        @pl.when(step >= 1 + s)
        def _():
            spread_out.copy(s - 1, step - 1 - s).wait()
            spread_out.copy(s, step - 1 - s).start()

    flat = lambda ref: jnp.concatenate([ref[i] for i in range(ipb)], axis=0) if ipb > 1 else ref[0]
    live = jnp.concatenate(
        [jnp.full((n_tok, 1), 1.0, F32) * live_ref[step * ipb + i] for i in range(ipb)], axis=0
    )
    mixed = flat(mix_ref)
    up = flat(og_ref).astype(F32) * live
    up16 = up.astype(BF16)
    res = flat(img_ref).astype(F32) + (dot(mixed, wp[...], NT) + vec_ref[2:3])
    xhat, inv = standardize(res)
    normed = (xhat * vec_ref[3:4] + vec_ref[4:5]).astype(BF16)
    branch = jnp.zeros((rows, c), F32)
    dn = jnp.zeros((rows, c), F32)
    for g in range(n_grp):
        cs = slice(g * chunk, (g + 1) * chunk)
        hid = dot(normed, w1_ref[g]) + b1_ref[0:1, cs]
        cdf = 0.5 * (1.0 + lax.erf(hid * SQRT_HALF))
        act = (hid * cdf).astype(BF16)
        slope = cdf + hid * (jnp.exp(-0.5 * hid * hid) * INV_SQRT_2PI)
        branch = branch + dot(act, w2_ref[g], NT)
        dw2[g] += dot(up16, act, TN)
        dh = (dot(up16, w2_ref[g]) * slope).astype(BF16)
        db1_ref[0:1, cs] += jnp.sum(dh.astype(F32), axis=0, keepdims=True)
        dw1[g] += dot(normed, dh, TN)
        dn = dn + dot(dh, w1_ref[g], NT)
    out = (live * (res + (branch + vec_ref[5:6]))).astype(BF16)
    for i in range(ipb):
        out_scr[step, i] = out[i * n_tok : (i + 1) * n_tok]
    keep(step).start()
    d = dn * vec_ref[3:4]
    gres = up + inv * (d - jnp.mean(d, axis=-1, keepdims=True) - xhat * jnp.mean(d * xhat, axis=-1, keepdims=True))
    gatt = gres.astype(BF16)
    dwp[...] += dot(gatt, mixed, TN)
    gmix = dot(gatt, wp[...]).astype(BF16)
    for i in range(ipb):
        r = slice(i * n_tok, (i + 1) * n_tok)
        gres_ref[i] = gres[r]
        gmix_ref[i] = gmix[r]
    dvec_ref[2:3] += jnp.sum(gatt.astype(F32), axis=0, keepdims=True)
    dvec_ref[3:4] += jnp.sum(dn * xhat, axis=0, keepdims=True)
    dvec_ref[4:5] += jnp.sum(dn, axis=0, keepdims=True)
    dvec_ref[5:6] += jnp.sum(up, axis=0, keepdims=True)

    @pl.when(step == steps - 1)
    def _():
        last = full_ref.shape[cube.n_t] - 1
        keep(last).wait()
        spread_out.copy(0, last).start()
        for g in range(n_grp):
            grad_ref[g, :, :chunk] = dw1[g].astype(BF16)
            grad_ref[g, :, chunk : 2 * chunk] = dw2[g].astype(BF16)
            grad_ref[g, :, 2 * chunk :] = dwp[:, g * GROUP * HD : (g + 1) * GROUP * HD].astype(BF16)
        for s in range(1, cube.n_t):
            for i in range(max(last - s, 0), last + 1):
                if i + s >= last:
                    spread_out.copy(s - 1, i).wait()
                    spread_out.copy(s, i).start()
        for i in range(last + 1):
            spread_out.copy(cube.n_t - 1, i).wait()


def mlp(live, images, out_grad, mixed, w_all, vecs, b1, fsdp, tp, ipb=2):
    n, t, c = images.shape
    n_grp = w_all.shape[0]
    ff = b1.shape[1]
    chunk, gw = ff // n_grp, GROUP * HD
    steps, n_t = n // ipb, len(bits_of(tp))
    whole = lambda s: pl.BlockSpec(s, lambda i: (0,) * len(s))
    once = lambda s, at=None: pl.BlockSpec(s, lambda i: at or (0,) * len(s), pipeline_mode=pl.Buffered(1))
    blk = pl.BlockSpec((ipb, t, c), lambda i: (i, 0, 0))
    first = 4 * gw
    return pl.pallas_call(
        functools.partial(mlp_kernel, ipb=ipb, fsdp=fsdp, tp=tp),
        grid=(steps,),
        in_specs=[pl.BlockSpec(memory_space=pltpu.SMEM), blk, blk, blk]
        + [
            once((n_grp, c, chunk), (0, 0, first // chunk)),
            once((n_grp, c, chunk), (0, 0, first // chunk + 1)),
            once((n_grp, c, gw), (0, 0, (first + 2 * chunk) // gw)),
        ]
        + [once(a.shape) for a in (vecs, b1)],
        out_specs=[pl.BlockSpec(memory_space=pl.ANY), blk, blk]
        + [whole(s) for s in ((n_grp, c, 2 * chunk + gw), (8, c), (1, ff))],
        out_shape=[
            jax.ShapeDtypeStruct((2,) * n_t + (steps, ipb, t, c), BF16),
            jax.ShapeDtypeStruct((n, t, c), F32),
            jax.ShapeDtypeStruct((n, t, c), BF16),
            jax.ShapeDtypeStruct((n_grp, c, 2 * chunk + gw), BF16),
            jax.ShapeDtypeStruct((8, c), F32),
            jax.ShapeDtypeStruct((1, ff), F32),
        ],
        scratch_shapes=[
            pltpu.VMEM((n_grp, c, chunk), F32),
            pltpu.VMEM((n_grp, c, chunk), F32),
            pltpu.VMEM((c, c), F32),
            pltpu.VMEM((c, c), BF16),
            pltpu.VMEM((steps, ipb, t, c), BF16),
            pltpu.SemaphoreType.DMA((steps,)),
            pltpu.SemaphoreType.DMA((n_t, steps)),
            pltpu.SemaphoreType.DMA((n_t, steps)),
        ],
        compiler_params=pltpu.CompilerParams(
            vmem_limit_bytes=58 << 20, collective_id=2, has_side_effects=True
        ),
        name="mlp",
    )(live, images, out_grad, mixed, w_all, w_all, w_all, vecs, b1)


def blocks_of(ref, n, body):
    if n == 0:
        body(())
        return

    def one(i, carry):
        body(tuple(lax.rem(lax.div(i, 2 ** (n - 1 - k)), 2) for k in range(n)))
        return carry

    lax.fori_loop(0, 2**n, one, 0)


class Reduce:
    def __init__(self, cube, acc, order, bufs, send, recv, n_digits):
        self.cube, self.acc, self.order, self.bufs = cube, acc, order, bufs
        self.send, self.recv, self.n_digits = send, recv, n_digits
        self.stages = len(order)

    def at(self, free, flip=None):
        own = self.cube.own
        return tuple(
            slice(None) if k in free else (1 - own[k] if k == flip else own[k]) for k in range(self.n_digits)
        )

    def left(self, s):
        return [k for k in self.order[s + 1 :] if k < self.n_digits]

    def copy(self, s):
        return pltpu.make_async_remote_copy(
            self.acc.at[self.at(self.left(s), self.order[s])],
            self.bufs[s],
            self.send.at[s],
            self.recv.at[s],
            device_id=self.cube.partner(self.order[s]),
            device_id_type=MESH,
        )

    def start(self, s):
        self.copy(s).start()

    def finish(self, s, out=None):
        self.copy(s).wait()
        free = sorted(self.left(s))
        own = self.cube.own

        def add(index):
            at = dict(zip(free, index))
            dst = tuple(at.get(k, own[k]) for k in range(self.n_digits))
            total = self.acc[dst].astype(F32) + self.bufs[s][index].astype(F32)
            if out is None:
                self.acc[dst] = total.astype(self.acc.dtype)
            else:
                out(total)

        blocks_of(self.acc, len(free), add)


def reduce_orders(n_t, n):
    t, f = list(range(n_t)), list(range(n_t, n))
    t_in, f_in = t[1:][::-1], f[::-1]
    early = (t_in + f_in + t[:1], t_in + f[:-1][::-1] + f[-1:] + t[:1])
    late = (t_in + f[-1:] + t[:1] + f[:-1][::-1], t_in + t[:1] + f_in)
    return early, late, t[::-1] + f_in


def attn_bwd_kernel(img_ref, gres_ref, gmix_ref, qkv_ref, p_ref, w_ref, vec_ref, perm_ref, permt_ref, grad_ref, dvec_in, db1_ref,
                    full_ref, dqkv_ref, dw1_ref, dw2_ref, dwp_ref, small_ref,
                    dqkv_scr, dw_ref, dvec_ref, db_ref, dtab_ref, gin_scr,
                    acc_a, acc_b, late_a, late_b, small, *rest, fsdp, tp):
    step, steps = pl.program_id(0), pl.num_programs(0)
    n_img = full_ref.shape[len(bits_of(tp))]
    n_grp, n_win = p_ref.shape[1:3]
    gw = GROUP * HD
    ff_cut = dw1_ref.shape[1]
    cube = Cube(fsdp, tp)
    n, n_t = cube.count, cube.n_t
    early, late, both = reduce_orders(n_t, n)
    bufs, (load, local, send, recv, rs_send, rs_recv) = rest[: 5 * n], rest[5 * n :]
    cut_bufs = [bufs[k * n : (k + 1) * n] for k in range(5)]
    reduces = [
        Reduce(cube, acc, order, buf, rs_send.at[k], rs_recv.at[k], digits)
        for k, (acc, order, buf, digits) in enumerate(
            zip((acc_a, acc_b, late_a, late_b, small), early + late + (both,), cut_bufs, (n, n, n, n, n_t))
        )
    ]
    first, second, third, fourth, fifth = reduces
    loads = [
        pltpu.make_async_copy(grad_ref.at[(slice(None),) * n + (slice(None), pl.ds(0, ff_cut))], acc_a, load.at[0]),
        pltpu.make_async_copy(
            grad_ref.at[(slice(None),) * n + (slice(None), pl.ds(ff_cut, ff_cut + gw))], acc_b, load.at[1]
        ),
    ]
    spread_in = Spread(cube, full_ref, send, recv)

    def keep(i):
        return pltpu.make_async_copy(gin_scr.at[i], spread_in.ref(0, i), local.at[i])

    def result_a(total):
        dw1_ref[...] = total

    def result_b(total):
        dw2_ref[...] = total[:, :ff_cut].T
        dwp_ref[...] = total[:, ff_cut:].T

    events = {}

    def plan(at, *work):
        events.setdefault(at, []).extend(work)

    points = n_grp + 1

    def advance(red, s, out=None):
        def go():
            red.finish(s, out if s == n - 1 else None)
            if s < n - 1:
                red.start(s + 1)

        return go

    begin = 2
    plan(begin, lambda: [(ld.wait(), red.start(0)) for ld, red in zip(loads, (first, second))])
    span = (n_img * points - begin - 2) // (n + 1)
    for s in range(n):
        plan(begin + (s + 1) * span, advance(first, s, result_a), advance(second, s, result_b))

    def point(k):
        for at in sorted(events):
            if at % points == k:

                @pl.when(step == at // points)
                def _(at=at):
                    for work in events[at]:
                        work()

    @pl.when(step == 0)
    def _():
        for ld in loads:
            ld.start()
        greet(cube, range(n))
        dw_ref[...] = jnp.zeros_like(dw_ref)
        dvec_ref[...] = dvec_in[...]
        db_ref[...] = jnp.zeros_like(db_ref)
        dtab_ref[...] = jnp.zeros_like(dtab_ref)

    @pl.when(step >= 1)
    def _():
        keep(step - 1).wait()
        spread_in.copy(0, step - 1).start()

    for s in range(1, n_t):

        @pl.when(step >= 1 + s)
        def _():
            spread_in.copy(s - 1, step - 1 - s).wait()
            spread_in.copy(s, step - 1 - s).start()

    mb, mf = head_masks(BF16), head_masks(F32)
    x = img_ref[0].astype(F32)
    xhat, inv = standardize(x)
    normed = (xhat * vec_ref[0:1] + vec_ref[1:2]).astype(BF16)
    xp = dot(perm_ref[...], normed).astype(BF16)
    gm = dot(perm_ref[...], gmix_ref[0]).astype(BF16)
    dn = jnp.zeros((n_win * ROWS, x.shape[1]), F32)
    for g in range(n_grp):
        point(g)
        c0 = g * 3 * gw
        tab = jnp.zeros((ROWS, GROUP * ROWS), F32)
        for w in range(n_win):
            r = slice(w * ROWS, (w + 1) * ROWS)
            q = qkv_ref[0, r, c0 : c0 + gw]
            k = qkv_ref[0, r, c0 + gw : c0 + 2 * gw]
            v = qkv_ref[0, r, c0 + 2 * gw : c0 + 3 * gw]
            do = spread(gm[r, g * gw : (g + 1) * gw], mb)
            p = p_ref[0, g, w]
            dqkv_scr[r, 2 * gw : 3 * gw] = dot(p, do).astype(BF16)
            dp = dot(v, do, NT)
            pf = p.astype(F32)
            ds = pf * (dp - jnp.sum(pf * dp, axis=0, keepdims=True))
            tab = tab + ds
            ds16 = ds.astype(BF16)
            dqkv_scr[r, gw : 2 * gw] = dot(ds16, spread(q, mb)).astype(BF16)
            dq = gather_heads(dot(ds16, k, TN), mf) * (HD ** -0.5)
            dqkv_scr[r, :gw] = dq.astype(BF16)
        dtab_ref[g] += tab
        dqkv = dqkv_scr[...]
        db_ref[0:1, c0 : c0 + 3 * gw] += jnp.sum(dqkv.astype(F32), axis=0, keepdims=True)
        dw_ref[g] += dot(xp, dqkv, TN)
        dn = dn + dot(dqkv, w_ref[g], NT)
    point(n_grp)
    hi = dn.astype(BF16)
    lo = (dn - hi.astype(F32)).astype(BF16)
    dn = dot(permt_ref[...], hi) + dot(permt_ref[...], lo)
    d = dn * vec_ref[0:1]
    gin = inv * (d - jnp.mean(d, axis=-1, keepdims=True) - xhat * jnp.mean(d * xhat, axis=-1, keepdims=True))
    gin_scr[step] = (gres_ref[0] + gin).astype(BF16)
    keep(step).start()
    dvec_ref[0:1] += jnp.sum(dn * xhat, axis=0, keepdims=True)
    dvec_ref[1:2] += jnp.sum(dn, axis=0, keepdims=True)

    @pl.when(step == steps - 1)
    def _():
        last = n_img - 1
        c, half = x.shape[1], 2 * gw
        cut = c // fsdp

        def fill(index):
            t, f = index[:n_t], index[n_t:]
            at = lambda part: functools.reduce(lambda a, b: 2 * a + b, part)
            rows = pl.ds(pl.multiple_of(at(f) * cut, cut), cut)
            late_a[index] = dw_ref[at(t), rows, :half].astype(BF16)
            late_b[index] = dw_ref[at(t), rows, half:].astype(BF16)

        blocks_of(late_a, n, fill)
        third.start(0)
        fourth.start(0)

        for g in range(n_grp):
            index = tuple((g >> (n_t - 1 - k)) & 1 for k in range(n_t))
            panel = small.at[index]
            panel[:ROWS] = dtab_ref[g]
            c0, f0, wide = g * 3 * gw, g * ff_cut, GROUP * ROWS
            panel[ROWS : ROWS + 1] = db_ref[0:1, c0 : c0 + wide]
            panel[ROWS + 1 : ROWS + 2] = jnp.concatenate(
                [db_ref[0:1, c0 + wide : c0 + 3 * gw], jnp.zeros((1, 2 * wide - 3 * gw), F32)], axis=1
            )
            for k in range(ff_cut // wide):
                panel[ROWS + 2 + k : ROWS + 3 + k] = db1_ref[0:1, f0 + k * wide : f0 + (k + 1) * wide]
            for i in range(6):
                for k in range(c // wide):
                    r = ROWS + 2 + ff_cut // wide + i * (c // wide) + k
                    panel[r : r + 1] = dvec_ref[i : i + 1, k * wide : (k + 1) * wide]
        fifth.start(0)

        keep(last).wait()
        spread_in.copy(0, last).start()
        for s in range(1, n_t):
            for i in range(max(last - s, 0), last + 1):
                if i + s >= last:
                    spread_in.copy(s - 1, i).wait()
                    spread_in.copy(s, i).start()

        def result_c(total):
            dqkv_ref[:, :half] = total

        def result_d(total):
            dqkv_ref[:, half:] = total

        def result_e(total):
            small_ref[...] = total

        for s in range(n):
            advance(third, s, result_c)()
            advance(fourth, s, result_d)()
            advance(fifth, s, result_e)()
        for i in range(n_img):
            spread_in.copy(n_t - 1, i).wait()


def attn_bwd(images, gres, gmix, qkv, p, w_all, vecs, consts, grads, dvec, db1, fsdp, tp):
    _, perm, permt = consts
    n_img, t, c = images.shape
    rows, cols = qkv.shape[1:]
    n_grp, n_win = p.shape[1:3]
    gw, wide = GROUP * HD, GROUP * ROWS
    ff_cut = db1.shape[1] // n_grp
    cut = c // fsdp
    n_t = len(bits_of(tp))
    n = n_t + len(bits_of(fsdp))
    digits = (2,) * n
    n_small = ROWS + 2 + ff_cut // wide + 6 * (c // wide)
    early, late, both = reduce_orders(n_t, n)
    half = 2 * gw
    bufs = []
    for order, width in zip(early + late, (ff_cut, ff_cut + gw, half, gw)):
        for s in range(n):
            bufs.append(pltpu.VMEM((2,) * (n - 1 - s) + (cut, width), BF16))
    for s in range(n):
        bufs.append(pltpu.VMEM((2,) * max(n_t - 1 - s, 0) + (n_small, wide), F32))
    whole = lambda s: pl.BlockSpec(s, lambda i: (0,) * len(s))
    once = lambda s: pl.BlockSpec(s, lambda i: (0,) * len(s), pipeline_mode=pl.Buffered(1))
    blk = pl.BlockSpec((1, t, c), lambda i: (i, 0, 0))
    any_spec = pl.BlockSpec(memory_space=pl.ANY)
    return pl.pallas_call(
        functools.partial(attn_bwd_kernel, fsdp=fsdp, tp=tp),
        grid=(n_img,),
        in_specs=[blk, blk, blk, pl.BlockSpec((1, rows, cols), lambda i: (i, 0, 0)),
                  pl.BlockSpec((1,) + p.shape[1:], lambda i: (i, 0, 0, 0, 0)), once((n_grp, c, 3 * gw))]
        + [once(a.shape) for a in (vecs, perm, permt)] + [any_spec] + [once(a.shape) for a in (dvec, db1)],
        out_specs=[any_spec] + [whole(s) for s in ((cut, 3 * gw), (cut, ff_cut), (ff_cut, cut), (gw, cut), (n_small, wide))],
        out_shape=[
            jax.ShapeDtypeStruct((2,) * n_t + (n_img, t, c), BF16),
            jax.ShapeDtypeStruct((cut, 3 * gw), F32),
            jax.ShapeDtypeStruct((cut, ff_cut), F32),
            jax.ShapeDtypeStruct((ff_cut, cut), F32),
            jax.ShapeDtypeStruct((gw, cut), F32),
            jax.ShapeDtypeStruct((n_small, wide), F32),
        ],
        scratch_shapes=[
            pltpu.VMEM((rows, 3 * gw), BF16),
            pltpu.VMEM((n_grp, c, 3 * gw), F32),
            pltpu.VMEM((8, c), F32),
            pltpu.VMEM((1, cols), F32),
            pltpu.VMEM((n_grp, ROWS, wide), F32),
            pltpu.VMEM((n_img, t, c), BF16),
            pltpu.VMEM(digits + (cut, ff_cut), BF16),
            pltpu.VMEM(digits + (cut, ff_cut + gw), BF16),
            pltpu.VMEM(digits + (cut, half), BF16),
            pltpu.VMEM(digits + (cut, gw), BF16),
            pltpu.VMEM((2,) * n_t + (n_small, wide), F32),
            *bufs,
            pltpu.SemaphoreType.DMA((2,)),
            pltpu.SemaphoreType.DMA((n_img,)),
            pltpu.SemaphoreType.DMA((n_t, n_img)),
            pltpu.SemaphoreType.DMA((n_t, n_img)),
            pltpu.SemaphoreType.DMA((5, n)),
            pltpu.SemaphoreType.DMA((5, n)),
        ],
        compiler_params=pltpu.CompilerParams(
            vmem_limit_bytes=58 << 20, collective_id=3, has_side_effects=True
        ),
        name="attn_bwd",
    )(images, gres, gmix, qkv, p, w_all, vecs, perm, permt, grads.reshape(digits + (cut, 2 * ff_cut + gw)), dvec, db1)


def per_device(
    images,
    attn_norm_gain,
    attn_norm_bias,
    qkv_weight,
    qkv_bias,
    position_table,
    proj_weight,
    proj_bias,
    mlp_norm_gain,
    mlp_norm_bias,
    fc1_weight,
    fc1_bias,
    fc2_weight,
    fc2_bias,
    image_count,
    out_grad,
    *,
    fsdp,
    tp,
):
    index, mask, perm = window_constants()
    span = position_table.shape[0]
    hot = jnp.asarray(index)[None] == jnp.arange(span, dtype=jnp.int32)[:, None, None]
    perm16 = jnp.asarray(perm).astype(BF16)
    consts = (jnp.asarray(mask), perm16, perm16.T)
    gw = GROUP * HD
    cut = qkv_weight.shape[0]
    width = cut * fsdp
    ff_cut = fc1_bias.shape[0]
    n_slots, n_tok, _ = images.shape
    mine = n_slots // tp
    first = lax.axis_index("tp") * mine
    img = lax.dynamic_slice_in_dim(images, first, mine, 0)
    cot = lax.dynamic_slice_in_dim(out_grad, first, mine, 0)
    live = (first + jnp.arange(mine, dtype=jnp.int32) < image_count[0]).astype(F32)

    vectors = (attn_norm_gain, attn_norm_bias, proj_bias, mlp_norm_gain, mlp_norm_bias, fc2_bias)
    flat = jnp.concatenate(vectors + (qkv_bias.reshape(-1), fc1_bias, position_table.reshape(-1)))
    lines = -(-flat.size // gw)
    flat = jnp.pad(flat, (0, lines * gw - flat.size)).reshape(lines, gw)
    pack = jnp.concatenate(
        [
            qkv_weight.reshape(cut, 3 * gw),
            jnp.pad(flat, ((0, cut - lines), (0, 0))),
            fc1_weight,
            fc2_weight.T,
            proj_weight.T,
        ],
        axis=1,
    )
    first_cols, cols = 4 * gw, pack.shape[1]
    chunks = ((0, first_cols), (first_cols, first_cols + ff_cut), (first_cols + ff_cut, cols))
    w_all = all_gather(pack, fsdp, tp, chunks)
    w_all = w_all.reshape(tp, width, cols)
    small = w_all[:, :, 3 * gw : 4 * gw].reshape(tp, fsdp, cut, gw)[:, :, :lines].reshape(tp, fsdp, lines * gw)
    vecs = small[0, :, : 6 * cut].reshape(fsdp, 6, cut).transpose(1, 0, 2).reshape(6, width).astype(F32)
    vecs = jnp.pad(vecs, ((0, 2), (0, 0)))
    rest = small[:, 0, 6 * cut :]
    n_qkv = qkv_bias.size
    b_qkv = rest[:, :n_qkv].reshape(1, tp * n_qkv).astype(F32)
    b_one = rest[:, n_qkv : n_qkv + ff_cut].reshape(1, tp * ff_cut).astype(F32)
    table = rest[:, n_qkv + ff_cut : n_qkv + ff_cut + position_table.size].reshape((tp,) + position_table.shape)
    table = table.transpose(0, 2, 1).reshape(-1, span)
    table = jnp.dot(table, hot.astype(BF16).reshape(span, -1), preferred_element_type=F32)
    table = table.reshape(-1, ROWS, ROWS)

    qkv, probs, mixed = attn_fwd(img, w_all, b_qkv, vecs, table, consts)
    output, gres, gmix, grads, dvec, db_one = mlp(live, img, cot, mixed, w_all, vecs, b_one, fsdp, tp)
    images_grad, d_qkv, d_one, d_two, d_proj, small = attn_bwd(
        img, gres, gmix, qkv, probs, w_all, vecs, consts, grads, dvec, db_one, fsdp, tp
    )
    wide = GROUP * ROWS
    d_tab = jnp.einsum(
        "jhi,rji->rh",
        small[:ROWS].reshape(ROWS, GROUP, ROWS),
        hot.astype(F32),
        precision=lax.Precision.HIGHEST,
    )
    at = ROWS + 2
    dqkv_bias = small[ROWS:at].reshape(-1)[:n_qkv].reshape(qkv_bias.shape)
    dfc1_bias = small[at : at + ff_cut // wide].reshape(-1)
    dvec = small[at + ff_cut // wide :].reshape(6, width)
    dvec = lax.dynamic_slice_in_dim(dvec, lax.axis_index("fsdp") * cut, cut, 1)
    return (
        output.reshape(images.shape),
        images_grad.reshape(images.shape),
        dvec[0],
        dvec[1],
        d_qkv.reshape(qkv_weight.shape),
        dqkv_bias,
        d_tab,
        d_proj,
        dvec[2],
        dvec[3],
        dvec[4],
        d_one,
        dfc1_bias,
        d_two,
        dvec[5],
    )


def solution(mesh):
    P = jax.sharding.PartitionSpec
    return jax.shard_map(
        functools.partial(per_device, fsdp=mesh.shape["fsdp"], tp=mesh.shape["tp"]),
        mesh=mesh,
        in_specs=(
            P("fsdp", None, None),
            P("fsdp"),
            P("fsdp"),
            P("fsdp", None, "tp"),
            P(None, "tp"),
            P(None, "tp"),
            P("tp", "fsdp"),
            P("fsdp"),
            P("fsdp"),
            P("fsdp"),
            P("fsdp", "tp"),
            P("tp"),
            P("tp", "fsdp"),
            P("fsdp"),
            P("fsdp"),
            P("fsdp", None, None),
        ),
        out_specs=(
            P("fsdp", None, None),
            P("fsdp", None, None),
            P("fsdp"),
            P("fsdp"),
            P("fsdp", None, "tp"),
            P(None, "tp"),
            P(None, "tp"),
            P("tp", "fsdp"),
            P("fsdp"),
            P("fsdp"),
            P("fsdp"),
            P("fsdp", "tp"),
            P("tp"),
            P("tp", "fsdp"),
            P("fsdp"),
        ),
        check_vma=False,
    )
```

```python
import functools
import jax
import jax.numpy as jnp
import numpy as np
from jax import lax
from jax.experimental import pallas as pl
from jax.experimental.pallas import tpu as pltpu

HD = 32
WIN = 7
SHIFT = 3
SIDE = 14
AREA = WIN * WIN
ROWS = 64
GROUP = 4
EPSILON = 1e-05
F32 = jnp.float32
BF16 = jnp.bfloat16
PADDED = -1e30
MESH = pl.DeviceIdType.MESH


def window_constants():
    offsets = np.arange(WIN)
    rows, cols = np.repeat(offsets, WIN), np.tile(offsets, WIN)
    relative = (rows[:, None] - rows[None, :] + WIN - 1) * (2 * WIN - 1) + (
        cols[:, None] - cols[None, :] + WIN - 1
    )
    span = (2 * WIN - 1) ** 2
    index = np.full((ROWS, ROWS), span, np.int32)
    index[:AREA, :AREA] = relative.T
    region = np.zeros((SIDE, SIDE), np.int32)
    bounds = ((0, SIDE - WIN), (SIDE - WIN, SIDE - SHIFT), (SIDE - SHIFT, SIDE))
    for a, rr in enumerate(bounds):
        for b, cc in enumerate(bounds):
            region[rr[0] : rr[1], cc[0] : cc[1]] = 3 * a + b
    across = SIDE // WIN
    cut = region.reshape(across, WIN, across, WIN).transpose(0, 2, 1, 3).reshape(across * across, AREA)
    mask = np.zeros((across * across, ROWS, ROWS), np.float32)
    mask[:, :AREA, :AREA] = np.where(cut[:, :, None] == cut[:, None, :], 0.0, -100.0)
    mask[:, AREA:, :] = PADDED
    mask = np.tile(mask, (1, 1, GROUP))
    perm = np.zeros((across * across * ROWS, SIDE * SIDE), np.float32)
    for w in range(across * across):
        for s in range(AREA):
            r = ((w // across) * WIN + s // WIN + SHIFT) % SIDE
            c = ((w % across) * WIN + s % WIN + SHIFT) % SIDE
            perm[w * ROWS + s, r * SIDE + c] = 1.0
    return index, mask, perm


def dot(a, b, dims=((1,), (0,))):
    return lax.dot_general(a, b, (dims, ((), ())), preferred_element_type=F32)


NT = ((1,), (1,))
TN = ((0,), (0,))


def standardize(x):
    c = x - jnp.mean(x, axis=-1, keepdims=True)
    inv = lax.rsqrt(jnp.mean(c * c, axis=-1, keepdims=True) + EPSILON)
    return c * inv, inv


def head_masks(dtype):
    lane = lax.broadcasted_iota(jnp.int32, (1, GROUP * HD), 1) // HD
    return [(lane == h).astype(F32).astype(dtype) for h in range(GROUP)]


def spread(x, masks):
    return jnp.concatenate([x * m for m in masks], axis=0)


def gather_heads(y, masks):
    out = y[:ROWS] * masks[0]
    for h in range(1, GROUP):
        out = out + y[h * ROWS : (h + 1) * ROWS] * masks[h]
    return out


def bits_of(n):
    return [1 << b for b in reversed(range(n.bit_length() - 1))]

class Cube:
    def __init__(self, fsdp, tp):
        self.f, self.t = lax.axis_index("fsdp"), lax.axis_index("tp")
        self.digits = [("tp", b) for b in bits_of(tp)] + [("fsdp", b) for b in bits_of(fsdp)]
        self.own = [lax.rem((self.t if a == "tp" else self.f) // b, 2) for a, b in self.digits]
        self.count = len(self.digits)
        self.n_t = len(bits_of(tp))

    def partner(self, k):
        axis, b = self.digits[k]
        step = b * (1 - 2 * self.own[k])
        if axis == "tp":
            return (self.f, self.t + step)
        return (self.f + step, self.t)

    def at(self, free, flip=None):
        out = []
        for k in range(self.count):
            if k in free:
                out.append(slice(None))
            else:
                out.append(1 - self.own[k] if k == flip else self.own[k])
        return tuple(out)


def greet(cube, digits):
    bar = pltpu.get_barrier_semaphore()
    for k in digits:
        pl.semaphore_signal(bar, inc=1, device_id=cube.partner(k), device_id_type=MESH)
    pl.semaphore_wait(bar, len(digits))


def gather_orders(cube):
    t, f = list(range(cube.n_t)), list(range(cube.n_t, cube.count))
    return (f + t, f[:-1] + t[:-1] + f[-1:] + t[-1:])


class Gather:
    def __init__(self, cube, full, chunks, send, recv):
        self.cube, self.full, self.chunks, self.send, self.recv = cube, full, chunks, send, recv
        self.orders = gather_orders(cube)

    def copies(self, c, s):
        lo, hi = self.chunks[c]
        rows = self.full.shape[self.cube.count]
        half = rows // 2
        for h, order in enumerate(self.orders):
            ref = self.full.at[self.cube.at(order[:s]) + (pl.ds(h * half, half), pl.ds(lo, hi - lo))]
            i = (c * self.cube.count + s) * 2 + h
            yield pltpu.make_async_remote_copy(ref, ref, self.send.at[i], self.recv.at[i],
                device_id=self.cube.partner(order[s]), device_id_type=MESH)

    def start(self, c, s):
        for copy in self.copies(c, s):
            copy.start()

    def wait(self, c, s):
        for copy in self.copies(c, s):
            copy.wait()

    def plan(self):
        n = self.cube.count
        return sorted(((c, s) for c in range(len(self.chunks)) for s in range(n + 1)), key=lambda e: (e[0] + e[1], e[0]))

    def advance(self, c, s):
        if s > 0:
            self.wait(c, s - 1)
        if s < self.cube.count:
            self.start(c, s)


def ag_kernel(pack_ref, full_ref, local, send, recv, *, fsdp, tp, chunks):
    cube = Cube(fsdp, tp)
    own = pltpu.make_async_copy(pack_ref, full_ref.at[cube.at(())], local)
    own.start()
    greet(cube, range(cube.count))
    own.wait()
    g = Gather(cube, full_ref, chunks, send, recv)
    for c, s in g.plan():
        g.advance(c, s)


def all_gather(pack, fsdp, tp, chunks):
    digits = len(bits_of(fsdp)) + len(bits_of(tp))
    n = len(chunks) * digits * 2
    return pl.pallas_call(
        functools.partial(ag_kernel, fsdp=fsdp, tp=tp, chunks=chunks),
        in_specs=[pl.BlockSpec(memory_space=pl.ANY)],
        out_specs=pl.BlockSpec(memory_space=pl.ANY),
        out_shape=jax.ShapeDtypeStruct((2,) * digits + pack.shape, pack.dtype),
        scratch_shapes=[pltpu.SemaphoreType.DMA, pltpu.SemaphoreType.DMA((n,)), pltpu.SemaphoreType.DMA((n,))],
        compiler_params=pltpu.CompilerParams(collective_id=1, has_side_effects=True),
        name="weights",
    )(pack)
def attn_fwd_kernel(img_ref, w_ref, b_ref, vec_ref, tab_ref, mask_ref, perm_ref, permt_ref, qkv_ref, p_ref, mix_ref, bias_scr, o_scr):
    n_win = mask_ref.shape[0]
    n_grp = w_ref.shape[0]
    gw = GROUP * HD

    @pl.when(pl.program_id(0) == 0)
    def _():
        for g in range(n_grp):
            full = jnp.concatenate([tab_ref[g * GROUP + h] for h in range(GROUP)], axis=1)
            for w in range(n_win):
                bias_scr[g, w] = full + mask_ref[w]

    x = img_ref[0].astype(F32)
    xhat, _ = standardize(x)
    normed = (xhat * vec_ref[0:1] + vec_ref[1:2]).astype(BF16)
    xp = dot(perm_ref[...], normed).astype(BF16)
    mb, mf = head_masks(BF16), head_masks(F32)
    for g in range(n_grp):
        c0 = g * 3 * gw
        acc = dot(xp, w_ref[g]) + b_ref[0:1, c0 : c0 + 3 * gw]
        qkv_ref[0, :, c0 : c0 + gw] = (acc[:, :gw] * (HD ** -0.5)).astype(BF16)
        qkv_ref[0, :, c0 + gw : c0 + 3 * gw] = acc[:, gw:].astype(BF16)

    def part(g, w, j):
        return qkv_ref[0, w * ROWS : (w + 1) * ROWS, (3 * g + j) * gw : (3 * g + j + 1) * gw]

    def score(g, w):
        return dot(part(g, w, 1), spread(part(g, w, 0), mb), NT) + bias_scr[g, w]

    def store(g, w, o):
        o_scr[w * ROWS : (w + 1) * ROWS, g * gw : (g + 1) * gw] = gather_heads(o, mf).astype(BF16)

    units = [(g, w) for g in range(n_grp) for w in range(n_win)]
    ahead, behind = score(*units[0]), None
    for at, (g, w) in enumerate(units):
        s = ahead
        if at + 1 < len(units):
            ahead = score(*units[at + 1])
        e = jnp.exp(s - jnp.max(s, axis=0, keepdims=True))
        p = (e * (1.0 / jnp.sum(e, axis=0, keepdims=True))).astype(BF16)
        p_ref[0, g, w] = p
        o = dot(p, part(g, w, 2), TN)
        if behind is not None:
            store(*behind)
        behind = (g, w, o)
    store(*behind)
    mix_ref[0] = dot(permt_ref[...], o_scr[...]).astype(BF16)


def attn_fwd(images, w_all, bqkv, vecs, table, consts):
    mask, perm, permt = consts
    n = images.shape[0]
    t, c = images.shape[1:]
    n_win, n_grp = mask.shape[0], w_all.shape[0]
    cols = n_grp * 3 * GROUP * HD
    rows = n_win * ROWS
    whole = lambda a: pl.BlockSpec(a.shape, lambda i: (0,) * a.ndim)
    return pl.pallas_call(
        attn_fwd_kernel,
        grid=(n,),
        in_specs=[pl.BlockSpec((1, t, c), lambda i: (i, 0, 0)), pl.BlockSpec((n_grp, c, 3 * GROUP * HD), lambda i: (0, 0, 0))]
        + [whole(a) for a in (bqkv, vecs, table, mask, perm, permt)],
        out_specs=[
            pl.BlockSpec((1, rows, cols), lambda i: (i, 0, 0)),
            pl.BlockSpec((1, n_grp, n_win, ROWS, GROUP * ROWS), lambda i: (i, 0, 0, 0, 0)),
            pl.BlockSpec((1, t, c), lambda i: (i, 0, 0)),
        ],
        out_shape=[
            jax.ShapeDtypeStruct((n, rows, cols), BF16),
            jax.ShapeDtypeStruct((n, n_grp, n_win, ROWS, GROUP * ROWS), BF16),
            jax.ShapeDtypeStruct((n, t, c), BF16),
        ],
        scratch_shapes=[
            pltpu.VMEM((n_grp, n_win, ROWS, GROUP * ROWS), F32),
            pltpu.VMEM((rows, c), BF16),
        ],
        compiler_params=pltpu.CompilerParams(vmem_limit_bytes=48 << 20),
        name="attn_fwd",
    )(images, w_all, bqkv, vecs, table, mask, perm, permt)


SQRT_HALF = float(np.sqrt(0.5))
INV_SQRT_2PI = float(1.0 / np.sqrt(2.0 * np.pi))
LANES = GROUP * HD
W_PROJ = 4 * LANES


class Spread:
    def __init__(self, cube, full, send, recv):
        self.cube, self.full, self.send, self.recv = cube, full, send, recv
        self.stages = cube.n_t

    def ref(self, s, i):
        own = self.cube.own
        return self.full.at[tuple(slice(None) if k < s else own[k] for k in range(self.stages)) + (i,)]

    def copy(self, s, i):
        ref = self.ref(s, i)
        return pltpu.make_async_remote_copy(
            ref, ref, self.send.at[s, i], self.recv.at[s, i], device_id=self.cube.partner(s), device_id_type=MESH
        )


def blocks_of(n, body):
    if n == 0:
        body(())
        return

    def one(i, carry):
        body(tuple(lax.rem(lax.div(i, 2 ** (n - 1 - k)), 2) for k in range(n)))
        return carry

    lax.fori_loop(0, 2**n, one, 0)


class Reduce:
    def __init__(self, cube, acc, order, bufs, send, recv, n_digits, out):
        self.cube, self.acc, self.order, self.bufs = cube, acc, order, bufs
        self.send, self.recv, self.n_digits, self.out = send, recv, n_digits, out
        self.stages = len(order)

    def at(self, free, flip=None):
        own = self.cube.own
        return tuple(
            slice(None) if k in free else (1 - own[k] if k == flip else own[k]) for k in range(self.n_digits)
        )

    def left(self, s):
        return sorted(k for k in self.order[s + 1 :] if k < self.n_digits)

    def copy(self, s):
        return pltpu.make_async_remote_copy(
            self.acc.at[self.at(self.left(s), self.order[s])],
            self.bufs[s],
            self.send.at[s],
            self.recv.at[s],
            device_id=self.cube.partner(self.order[s]),
            device_id_type=MESH,
        )

    def start(self):
        self.copy(0).start()

    def advance(self, s):
        self.copy(s).wait()
        free = self.left(s)
        own = self.cube.own

        def add(index):
            at = dict(zip(free, index))
            dst = tuple(at.get(k, own[k]) for k in range(self.n_digits))
            if s + 1 == self.stages:
                self.out(self.acc[dst].astype(F32) + self.bufs[s][index].astype(F32))
            else:
                self.acc[dst] = self.acc[dst] + self.bufs[s][index]

        blocks_of(len(free), add)
        if s + 1 < self.stages:
            self.copy(s + 1).start()


def reduce_orders(n_t, n):
    t, f = list(range(n_t)), list(range(n_t, n))
    t_in, f_in = t[1:][::-1], f[::-1]
    early = (t_in + f_in + t[:1], t_in + f[:-1][::-1] + f[-1:] + t[:1])
    late = (t_in + f[-1:] + t[:1] + f[:-1][::-1], t_in + t[:1] + f_in)
    return early, late, t[::-1] + f_in


def digits_of(value, n):
    return tuple((value >> (n - 1 - k)) & 1 for k in range(n))


def layer_kernel(live_ref, img_hbm, cot_hbm, mix_ref, w_hbm, vec_ref, b1_ref, qkv_ref, p_ref, perm_ref, permt_ref,
                 out_ref, gin_ref, dqkv_ref, dw1_ref, dw2_ref, dwp_ref, small_ref,
                 img_ref, cot_ref, w1_ref, w2_ref, wq_ref, wp, act, slope, normed_two, up_scr, gres_scr,
                 db1, dvec, dqkv_scr, dw, db, dtab, res_scr, acc, acc_p, late_a, late_b, small, *rest,
                 fsdp, tp, per, n_q):
    step = pl.program_id(0)
    cube = Cube(fsdp, tp)
    n, n_t, n_f = cube.count, cube.n_t, cube.count - cube.n_t
    n_img, n_tok, c = img_ref.shape
    n_grp, n_win = p_ref.shape[1:3]
    gw = LANES
    cut = c // fsdp
    fwd_steps = n_img // per
    bwd_at = fwd_steps
    att_at = bwd_at + n_q
    last_step = att_at + n_img - 1

    early, late, both = reduce_orders(n_t, n)
    bufs, rest = rest[: 5 * n], rest[5 * n :]
    load, local, send, recv, local_in, send_in, recv_in, rs_send, rs_recv = rest

    columns_at = lambda lo, width: w_hbm.at[:, :, pl.ds(lo, width)]
    wide_q = n_q * gw
    loads = [
        pltpu.make_async_copy(columns_at(lo, ref.shape[2]), ref, load.at[k])
        for k, (lo, ref) in enumerate(
            ((W_PROJ + gw, w1_ref), (W_PROJ + gw + wide_q, w2_ref), (0, wq_ref))
        )
    ]
    loads += [pltpu.make_async_copy(img_hbm, img_ref, load.at[3]), pltpu.make_async_copy(cot_hbm, cot_ref, load.at[4])]
    loads += [
        pltpu.make_async_copy(
            w_hbm.at[g, :, pl.ds(W_PROJ, gw)], wp.at[:, pl.ds(g * gw, gw)], load.at[5 + g]
        )
        for g in range(n_grp)
    ]
    gmix_scr = cot_ref

    def result_of(q):
        def out(total):
            dw1_ref[:, q * gw : (q + 1) * gw] = total[:, :gw]
            dw2_ref[q * gw : (q + 1) * gw] = total[:, gw:].T

        return out

    def result_p(total):
        dwp_ref[...] = total.T

    def result_a(total):
        dqkv_ref[:, : 2 * gw] = total

    def result_b(total):
        dqkv_ref[:, 2 * gw :] = total

    def result_s(total):
        small_ref[...] = total

    plans = [
        (acc.at[q], [ref.at[q] for ref in bufs[:n]], early[q % 2], n, result_of(q)) for q in range(n_q)
    ]
    plans += [
        (acc_p, bufs[n : 2 * n], early[0], n, result_p),
        (late_a, bufs[2 * n : 3 * n], late[0], n, result_a),
        (late_b, bufs[3 * n : 4 * n], late[1], n, result_b),
        (small, bufs[4 * n :], both, n_t, result_s),
    ]
    reduces = [
        Reduce(cube, ref, order, buf, rs_send.at[k], rs_recv.at[k], d, out)
        for k, (ref, buf, order, d, out) in enumerate(plans)
    ]
    n_early = n_q + 1
    spread_out = Spread(cube, out_ref, send, recv)
    spread_in = Spread(cube, gin_ref, send_in, recv_in)

    def keep_out(i):
        return pltpu.make_async_copy(res_scr.at[pl.ds(i * per, per)], spread_out.ref(0, i), local.at[i])

    def keep_in(i):
        return pltpu.make_async_copy(res_scr.at[i], spread_in.ref(0, i), local_in.at[i])

    events = {}

    def plan(at, work):
        events.setdefault(at, []).append(work)

    def point(k):
        for at in sorted(events):
            if at[1] == k:

                @pl.when(step == at[0])
                def _(at=at):
                    for work in events[at]:
                        work()

    def send_out(i):
        keep_out(i).wait()
        spread_out.copy(0, i).start()

    def pass_out(i, s):
        spread_out.copy(s - 1, i).wait()
        spread_out.copy(s, i).start()

    def send_in_(i):
        keep_in(i).wait()
        spread_in.copy(0, i).start()

    def pass_in(i, s):
        spread_in.copy(s - 1, i).wait()
        spread_in.copy(s, i).start()

    for i in range(fwd_steps):
        plan((i + 1, 0), functools.partial(send_out, i))
    later = [att_at - 1 + 3 * i for i in range(fwd_steps)]
    for s in range(1, n_t):
        for i in range(fwd_steps):
            plan((min(later[i] + s - 1, last_step), 0), functools.partial(pass_out, i, s))
    for i in range(n_img - 1):
        plan((att_at + i + 1, 0), functools.partial(send_in_, i))
    tail = []
    for i in range(n_img):
        for s in range(1, n_t):
            at = att_at + i + 3 + s
            if at <= last_step:
                plan((at, 0), functools.partial(pass_in, i, s))
            else:
                tail.append(functools.partial(pass_in, i, s))
    ends = []
    for k in range(n_early):
        begin = (bwd_at + k + 1, 1) if k + 1 < n_q else (att_at, 0)
        plan(begin, reduces[k].start)
        slots = SLOTS[k] if k < len(SLOTS) else ()
        for s in range(n):
            work = functools.partial(reduces[k].advance, s)
            if s < len(slots):
                plan((bwd_at + slots[s][0], slots[s][1]), work)
            else:
                ends.append(work)

    @pl.when(step == 0)
    def _():
        for ld in loads:
            ld.start()
        greet(cube, range(n))
        dw[...] = jnp.zeros_like(dw)
        dvec[...] = jnp.zeros_like(dvec)
        db[...] = jnp.zeros_like(db)
        db1[...] = jnp.zeros_like(db1)
        dtab[...] = jnp.zeros_like(dtab)
        for ld in loads:
            ld.wait()

    def columns(ref, q):
        at = pl.ds(pl.multiple_of(q * gw, gw), gw)
        return jnp.concatenate([ref[g, :, at] for g in range(n_grp)], axis=1)

    def rows_of(ref, b):
        return jnp.concatenate([ref[b * per + i] for i in range(per)], axis=0)

    def middle(b):
        mixed = rows_of(mix_ref, b)
        res = rows_of(img_ref, b).astype(F32) + (dot(mixed, wp[...], NT) + vec_ref[2:3])
        return (mixed, res) + standardize(res)

    @pl.when(step < bwd_at)
    def _():
        point(0)
        live = jnp.concatenate(
            [jnp.full((n_tok, 1), 1.0, F32) * live_ref[step * per + i] for i in range(per)], axis=0
        )
        up = rows_of(cot_ref, step).astype(F32) * live
        up_scr[step] = up.astype(BF16)
        dvec[5:6] += jnp.sum(up, axis=0, keepdims=True)
        mixed, res, xhat, _ = middle(step)
        normed_two[step] = (xhat * vec_ref[3:4] + vec_ref[4:5]).astype(BF16)

        def hidden_part(q, branch):
            hid = dot(normed_two[step], columns(w1_ref, q)) + b1_ref[pl.ds(q, 1)]
            cdf = 0.5 * (1.0 + lax.erf(hid * SQRT_HALF))
            a = (hid * cdf).astype(BF16)
            act[step, q] = a
            slope[step, q] = (cdf + hid * (jnp.exp(-0.5 * hid * hid) * INV_SQRT_2PI)).astype(BF16)
            return branch + dot(a, columns(w2_ref, q), NT)

        total = lax.fori_loop(0, n_q, hidden_part, res + vec_ref[5:6])
        out = (live * total).astype(BF16)
        for i in range(per):
            res_scr[step * per + i] = out[i * n_tok : (i + 1) * n_tok]
        keep_out(step).start()

    @pl.when(jnp.logical_and(step >= bwd_at, step < att_at))
    def _():
        q = step - bwd_at
        point(0)
        w2 = columns(w2_ref, q)
        d_one = d_two = None
        for b in range(fwd_steps):
            if b == 1:
                point(1)
            up = up_scr[b]
            dh = (dot(up, w2) * slope[b, q].astype(F32)).astype(BF16)
            slope[b, q] = dh
            db1[pl.ds(q, 1)] += jnp.sum(dh.astype(F32), axis=0, keepdims=True)
            one, two = dot(normed_two[b], dh, TN), dot(up, act[b, q], TN)
            d_one, d_two = (one, two) if b == 0 else (d_one + one, d_two + two)
        for t in range(n_grp):
            for f in range(fsdp):
                at = (q,) + digits_of(t, n_t) + digits_of(f, n_f)
                r, l = slice(f * cut, (f + 1) * cut), slice(t * gw, (t + 1) * gw)
                acc[at + (slice(None), slice(0, gw))] = d_one[r, l].astype(BF16)
                acc[at + (slice(None), slice(gw, 2 * gw))] = d_two[r, l].astype(BF16)

    @pl.when(step == att_at - 1)
    def _():
        def back(b, d_proj):
            dn = dot(slope[b, 0], columns(w1_ref, 0), NT)
            for k in range(1, n_q):
                dn = dn + dot(slope[b, k], columns(w1_ref, k), NT)
            mixed, _, xhat, inv = middle(b)
            d = dn * vec_ref[3:4]
            gres = up_scr[b].astype(F32) + inv * (
                d - jnp.mean(d, axis=-1, keepdims=True) - xhat * jnp.mean(d * xhat, axis=-1, keepdims=True)
            )
            gatt = gres.astype(BF16)
            gmix = dot(gatt, wp[...]).astype(BF16)
            for i in range(per):
                r = slice(i * n_tok, (i + 1) * n_tok)
                gres_scr[b * per + i] = gres[r]
                gmix_scr[b * per + i] = gmix[r]
            dvec[2:3] += jnp.sum(gatt.astype(F32), axis=0, keepdims=True)
            dvec[3:4] += jnp.sum(dn * xhat, axis=0, keepdims=True)
            dvec[4:5] += jnp.sum(dn, axis=0, keepdims=True)
            return d_proj + dot(gatt, mixed, TN)

        d_proj = lax.fori_loop(0, fwd_steps, back, jnp.zeros((c, c), F32))
        for t in range(n_grp):
            for f in range(fsdp):
                at = digits_of(t, n_t) + digits_of(f, n_f)
                acc_p[at] = d_proj[f * cut : (f + 1) * cut, t * gw : (t + 1) * gw].astype(BF16)

    @pl.when(step >= att_at)
    def _():
        j = step - att_at
        mb, mf = head_masks(BF16), head_masks(F32)
        point(0)
        x = img_ref[j].astype(F32)
        xhat, inv = standardize(x)
        normed = (xhat * vec_ref[0:1] + vec_ref[1:2]).astype(BF16)
        xp = dot(perm_ref[...], normed).astype(BF16)
        gm = dot(perm_ref[...], gmix_scr[j]).astype(BF16)
        dn = jnp.zeros((n_win * ROWS, c), F32)
        for g in range(n_grp):
            if g > 0:
                point(g)
            c0 = g * 3 * gw
            tab = jnp.zeros((ROWS, GROUP * ROWS), F32)
            cuts = [slice(w * ROWS, (w + 1) * ROWS) for w in range(n_win)]
            dos = [spread(gm[r, g * gw : (g + 1) * gw], mb) for r in cuts]
            dps = [dot(qkv_ref[0, r, c0 + 2 * gw : c0 + 3 * gw], do, NT) for r, do in zip(cuts, dos)]
            ps = [p_ref[0, g, w] for w in range(n_win)]
            dvs = [dot(p, do) for p, do in zip(ps, dos)]
            dss = []
            for p, dp in zip(ps, dps):
                pf = p.astype(F32)
                ds = pf * (dp - jnp.sum(pf * dp, axis=0, keepdims=True))
                tab = tab + ds
                dss.append(ds.astype(BF16))
            dks = [dot(ds, spread(qkv_ref[0, r, c0 : c0 + gw], mb)) for r, ds in zip(cuts, dss)]
            dqs = [dot(ds, qkv_ref[0, r, c0 + gw : c0 + 2 * gw], TN) for r, ds in zip(cuts, dss)]
            for r, dq, dk, dv in zip(cuts, dqs, dks, dvs):
                dqkv_scr[r, :gw] = (gather_heads(dq, mf) * (HD ** -0.5)).astype(BF16)
                dqkv_scr[r, gw : 2 * gw] = dk.astype(BF16)
                dqkv_scr[r, 2 * gw :] = dv.astype(BF16)
            dtab[g] += tab
            dqkv = dqkv_scr[...]
            db[0:1, c0 : c0 + 3 * gw] += jnp.sum(dqkv.astype(F32), axis=0, keepdims=True)
            dw[g] += dot(xp, dqkv, TN)
            dn = dn + dot(dqkv, wq_ref[g], NT)
        hi = dn.astype(BF16)
        lo = (dn - hi.astype(F32)).astype(BF16)
        dn = dot(permt_ref[...], hi) + dot(permt_ref[...], lo)
        d = dn * vec_ref[0:1]
        gin = inv * (
            d - jnp.mean(d, axis=-1, keepdims=True) - xhat * jnp.mean(d * xhat, axis=-1, keepdims=True)
        )
        res_scr[j] = (gres_scr[j] + gin).astype(BF16)
        keep_in(j).start()
        dvec[0:1] += jnp.sum(dn * xhat, axis=0, keepdims=True)
        dvec[1:2] += jnp.sum(dn, axis=0, keepdims=True)

    @pl.when(step == last_step)
    def _():
        def fill(index):
            t, f = index[:n_t], index[n_t:]
            at = lambda part: functools.reduce(lambda a, b: 2 * a + b, part)
            rows = pl.ds(pl.multiple_of(at(f) * cut, cut), cut)
            late_a[index] = dw[at(t), rows, : 2 * gw].astype(BF16)
            late_b[index] = dw[at(t), rows, 2 * gw :].astype(BF16)

        blocks_of(n, fill)
        for red in reduces[n_early : n_early + 2]:
            red.start()
        wide = GROUP * ROWS
        for g in range(n_grp):
            panel = small.at[digits_of(g, n_t)]
            panel[:ROWS] = dtab[g]
            c0 = g * 3 * gw
            panel[ROWS : ROWS + 1] = db[0:1, c0 : c0 + wide]
            panel[ROWS + 1 : ROWS + 2] = jnp.concatenate(
                [db[0:1, c0 + wide : c0 + 3 * gw], jnp.zeros((1, 2 * wide - 3 * gw), F32)], axis=1
            )
            r = ROWS + 2
            for q in range(0, n_q, 2):
                pair = [db1[q + k : q + k + 1, g * gw : (g + 1) * gw] for k in range(2)]
                panel[r : r + 1] = jnp.concatenate(pair, axis=1)
                r = r + 1
            for i in range(6):
                for k in range(c // wide):
                    panel[r : r + 1] = dvec[i : i + 1, k * wide : (k + 1) * wide]
                    r = r + 1
        reduces[n_early + 2].start()
        send_in_(n_img - 1)
        for work in ends:
            work()
        for s in range(n):
            for red in reduces[n_early:]:
                red.advance(s)
            if s == 0:
                for work in tail[: len(tail) // 2]:
                    work()
        for work in tail[len(tail) // 2 :]:
            work()
        for i in range(fwd_steps):
            spread_out.copy(n_t - 1, i).wait()
        for i in range(n_img):
            spread_in.copy(n_t - 1, i).wait()


SLOTS = (
    ((2, 0), (3, 1), (4, 0), (5, 2), (8, 0)),
    ((3, 0), (4, 0), (6, 0), (8, 0), (10, 0)),
    ((4, 0), (6, 2), (8, 2), (10, 2)),
    ((5, 2), (8, 0), (9, 3), (11, 2)),
    ((5, 2), (8, 0), (9, 3), (11, 2)),
)


def layer(live, images, out_grad, mixed, w_all, vecs, b1, qkv, p, perm, permt, fsdp, tp, per=4):
    n_img, t, c = mixed.shape
    rows, cols = qkv.shape[1:]
    n_grp, n_win = p.shape[1:3]
    gw, wide = LANES, GROUP * ROWS
    n_q = b1.shape[0]
    ff_cut = n_q * gw
    cut = c // fsdp
    n_t, n_f = len(bits_of(tp)), len(bits_of(fsdp))
    n = n_t + n_f
    digits = (2,) * n
    n_small = ROWS + 2 + ff_cut // wide + 6 * (c // wide)
    fwd_steps = n_img // per
    att_at = fwd_steps + n_q
    bufs = []
    for lead, width in (((n_q,), 2 * gw), ((), gw), ((), 2 * gw), ((), gw)):
        bufs += [pltpu.VMEM(lead + (2,) * (n - 1 - s) + (cut, width), BF16) for s in range(n)]
    bufs += [pltpu.VMEM((2,) * max(n_t - 1 - s, 0) + (n_small, wide), F32) for s in range(n)]
    whole = lambda s: pl.BlockSpec(s, lambda i: (0,) * len(s))
    once = lambda s: pl.BlockSpec(s, lambda i: (0,) * len(s), pipeline_mode=pl.Buffered(1))
    image = lambda i: jnp.clip(i - att_at, 0, n_img - 1)
    any_spec = pl.BlockSpec(memory_space=pl.ANY)
    hidden = (fwd_steps, n_q, per * t, n_grp * gw)
    return pl.pallas_call(
        functools.partial(layer_kernel, fsdp=fsdp, tp=tp, per=per, n_q=n_q),
        grid=(att_at + n_img,),
        in_specs=[
            pl.BlockSpec(memory_space=pltpu.SMEM),
            any_spec,
            any_spec,
            once(mixed.shape),
            any_spec,
            once(vecs.shape),
            once(b1.shape),
            pl.BlockSpec((1, rows, cols), lambda i: (image(i), 0, 0)),
            pl.BlockSpec((1,) + p.shape[1:], lambda i: (image(i), 0, 0, 0, 0)),
            once(perm.shape),
            once(permt.shape),
        ],
        out_specs=[any_spec, any_spec]
        + [whole(s) for s in ((cut, 3 * gw), (cut, ff_cut), (ff_cut, cut), (gw, cut), (n_small, wide))],
        out_shape=[
            jax.ShapeDtypeStruct((2,) * n_t + (fwd_steps, per, t, c), BF16),
            jax.ShapeDtypeStruct((2,) * n_t + (n_img, t, c), BF16),
            jax.ShapeDtypeStruct((cut, 3 * gw), F32),
            jax.ShapeDtypeStruct((cut, ff_cut), F32),
            jax.ShapeDtypeStruct((ff_cut, cut), F32),
            jax.ShapeDtypeStruct((gw, cut), F32),
            jax.ShapeDtypeStruct((n_small, wide), F32),
        ],
        scratch_shapes=[
            pltpu.VMEM((n_img, t, c), BF16),
            pltpu.VMEM((n_img, t, c), BF16),
            pltpu.VMEM((n_grp, c, ff_cut), BF16),
            pltpu.VMEM((n_grp, c, ff_cut), BF16),
            pltpu.VMEM((n_grp, c, 3 * gw), BF16),
            pltpu.VMEM((c, c), BF16),
            pltpu.VMEM(hidden, BF16),
            pltpu.VMEM(hidden, BF16),
            pltpu.VMEM((fwd_steps, per * t, c), BF16),
            pltpu.VMEM((fwd_steps, per * t, c), BF16),
            pltpu.VMEM((n_img, t, c), F32),
            pltpu.VMEM((8, n_grp * gw), F32),
            pltpu.VMEM((8, c), F32),
            pltpu.VMEM((rows, 3 * gw), BF16),
            pltpu.VMEM((n_grp, c, 3 * gw), F32),
            pltpu.VMEM((1, cols), F32),
            pltpu.VMEM((n_grp, ROWS, wide), F32),
            pltpu.VMEM((n_img, t, c), BF16),
            pltpu.VMEM((n_q,) + digits + (cut, 2 * gw), BF16),
            pltpu.VMEM(digits + (cut, gw), BF16),
            pltpu.VMEM(digits + (cut, 2 * gw), BF16),
            pltpu.VMEM(digits + (cut, gw), BF16),
            pltpu.VMEM((2,) * n_t + (n_small, wide), F32),
            *bufs,
            pltpu.SemaphoreType.DMA((5 + n_grp,)),
            pltpu.SemaphoreType.DMA((fwd_steps,)),
            pltpu.SemaphoreType.DMA((n_t, fwd_steps)),
            pltpu.SemaphoreType.DMA((n_t, fwd_steps)),
            pltpu.SemaphoreType.DMA((n_img,)),
            pltpu.SemaphoreType.DMA((n_t, n_img)),
            pltpu.SemaphoreType.DMA((n_t, n_img)),
            pltpu.SemaphoreType.DMA((n_q + 4, n)),
            pltpu.SemaphoreType.DMA((n_q + 4, n)),
        ],
        compiler_params=pltpu.CompilerParams(
            vmem_limit_bytes=60 << 20, collective_id=2, has_side_effects=True
        ),
        name="layer",
    )(live, images, out_grad, mixed, w_all, vecs, b1, qkv, p, perm, permt)


def per_device(
    images,
    attn_norm_gain,
    attn_norm_bias,
    qkv_weight,
    qkv_bias,
    position_table,
    proj_weight,
    proj_bias,
    mlp_norm_gain,
    mlp_norm_bias,
    fc1_weight,
    fc1_bias,
    fc2_weight,
    fc2_bias,
    image_count,
    out_grad,
    *,
    fsdp,
    tp,
):
    index, mask, perm = window_constants()
    span = position_table.shape[0]
    hot = jnp.asarray(index)[None] == jnp.arange(span, dtype=jnp.int32)[:, None, None]
    perm16 = jnp.asarray(perm).astype(BF16)
    consts = (jnp.asarray(mask), perm16, perm16.T)
    gw = GROUP * HD
    cut = qkv_weight.shape[0]
    width = cut * fsdp
    ff_cut = fc1_bias.shape[0]
    n_slots, n_tok, _ = images.shape
    mine = n_slots // tp
    first = lax.axis_index("tp") * mine
    img = lax.dynamic_slice_in_dim(images, first, mine, 0)
    cot = lax.dynamic_slice_in_dim(out_grad, first, mine, 0)
    live = (first + jnp.arange(mine, dtype=jnp.int32) < image_count[0]).astype(F32)

    vectors = (attn_norm_gain, attn_norm_bias, proj_bias, mlp_norm_gain, mlp_norm_bias, fc2_bias)
    flat = jnp.concatenate(vectors + (qkv_bias.reshape(-1), fc1_bias, position_table.reshape(-1)))
    lines = -(-flat.size // gw)
    flat = jnp.pad(flat, (0, lines * gw - flat.size)).reshape(lines, gw)
    pack = jnp.concatenate(
        [
            qkv_weight.reshape(cut, 3 * gw),
            jnp.pad(flat, ((0, cut - lines), (0, 0))),
            proj_weight.T,
            fc1_weight,
            fc2_weight.T,
        ],
        axis=1,
    )
    first_cols, cols = 4 * gw, pack.shape[1]
    chunks = ((0, first_cols), (first_cols, first_cols + gw + ff_cut), (first_cols + gw + ff_cut, cols))
    w_all = all_gather(pack, fsdp, tp, chunks)
    w_all = w_all.reshape(tp, width, cols)
    small = w_all[:, :, 3 * gw : 4 * gw].reshape(tp, fsdp, cut, gw)[:, :, :lines].reshape(tp, fsdp, lines * gw)
    vecs = small[0, :, : 6 * cut].reshape(fsdp, 6, cut).transpose(1, 0, 2).reshape(6, width).astype(F32)
    vecs = jnp.pad(vecs, ((0, 2), (0, 0)))
    rest = small[:, 0, 6 * cut :]
    n_qkv = qkv_bias.size
    b_qkv = rest[:, :n_qkv].reshape(1, tp * n_qkv).astype(F32)
    b_one = rest[:, n_qkv : n_qkv + ff_cut].reshape(1, tp * ff_cut).astype(F32)
    table = rest[:, n_qkv + ff_cut : n_qkv + ff_cut + position_table.size].reshape((tp,) + position_table.shape)
    table = table.transpose(0, 2, 1).reshape(-1, span)
    table = jnp.dot(table, hot.astype(BF16).reshape(span, -1), preferred_element_type=F32)
    table = table.reshape(-1, ROWS, ROWS)

    qkv, probs, mixed = attn_fwd(img, w_all, b_qkv, vecs, table, consts)
    b_one = b_one.reshape(tp, -1, gw).transpose(1, 0, 2).reshape(-1, tp * gw)
    output, images_grad, d_qkv, d_one, d_two, d_proj, small = layer(
        live, img, cot, mixed, w_all, vecs, b_one, qkv, probs, consts[1], consts[2], fsdp, tp
    )
    wide = GROUP * ROWS
    d_tab = jnp.einsum(
        "jhi,rji->rh",
        small[:ROWS].reshape(ROWS, GROUP, ROWS),
        hot.astype(F32),
        precision=lax.Precision.HIGHEST,
    )
    at = ROWS + 2
    dqkv_bias = small[ROWS:at].reshape(-1)[:n_qkv].reshape(qkv_bias.shape)
    dfc1_bias = small[at : at + ff_cut // wide].reshape(-1)
    dvec = small[at + ff_cut // wide :].reshape(6, width)
    dvec = lax.dynamic_slice_in_dim(dvec, lax.axis_index("fsdp") * cut, cut, 1)
    return (
        output.reshape(images.shape),
        images_grad.reshape(images.shape),
        dvec[0],
        dvec[1],
        d_qkv.reshape(qkv_weight.shape),
        dqkv_bias,
        d_tab,
        d_proj,
        dvec[2],
        dvec[3],
        dvec[4],
        d_one,
        dfc1_bias,
        d_two,
        dvec[5],
    )


def solution(mesh):
    P = jax.sharding.PartitionSpec
    return jax.shard_map(
        functools.partial(per_device, fsdp=mesh.shape["fsdp"], tp=mesh.shape["tp"]),
        mesh=mesh,
        in_specs=(
            P("fsdp", None, None),
            P("fsdp"),
            P("fsdp"),
            P("fsdp", None, "tp"),
            P(None, "tp"),
            P(None, "tp"),
            P("tp", "fsdp"),
            P("fsdp"),
            P("fsdp"),
            P("fsdp"),
            P("fsdp", "tp"),
            P("tp"),
            P("tp", "fsdp"),
            P("fsdp"),
            P("fsdp"),
            P("fsdp", None, None),
        ),
        out_specs=(
            P("fsdp", None, None),
            P("fsdp", None, None),
            P("fsdp"),
            P("fsdp"),
            P("fsdp", None, "tp"),
            P(None, "tp"),
            P(None, "tp"),
            P("tp", "fsdp"),
            P("fsdp"),
            P("fsdp"),
            P("fsdp"),
            P("fsdp", "tp"),
            P("tp"),
            P("tp", "fsdp"),
            P("fsdp"),
        ),
        check_vma=False,
    )
```

```python
import functools
import jax
import jax.numpy as jnp
import numpy as np
from jax import lax
from jax.experimental import pallas as pl
from jax.experimental.pallas import tpu as pltpu

HD = 32
WIN = 7
SHIFT = 3
SIDE = 14
AREA = WIN * WIN
ROWS = 64
GROUP = 4
EPSILON = 1e-05
F32 = jnp.float32
BF16 = jnp.bfloat16
PADDED = -1e30
MESH = pl.DeviceIdType.MESH


def window_constants():
    offsets = np.arange(WIN)
    rows, cols = np.repeat(offsets, WIN), np.tile(offsets, WIN)
    relative = (rows[:, None] - rows[None, :] + WIN - 1) * (2 * WIN - 1) + (
        cols[:, None] - cols[None, :] + WIN - 1
    )
    span = (2 * WIN - 1) ** 2
    index = np.full((ROWS, ROWS), span, np.int32)
    index[:AREA, :AREA] = relative.T
    region = np.zeros((SIDE, SIDE), np.int32)
    bounds = ((0, SIDE - WIN), (SIDE - WIN, SIDE - SHIFT), (SIDE - SHIFT, SIDE))
    for a, rr in enumerate(bounds):
        for b, cc in enumerate(bounds):
            region[rr[0] : rr[1], cc[0] : cc[1]] = 3 * a + b
    across = SIDE // WIN
    cut = region.reshape(across, WIN, across, WIN).transpose(0, 2, 1, 3).reshape(across * across, AREA)
    mask = np.zeros((across * across, ROWS, ROWS), np.float32)
    mask[:, :AREA, :AREA] = np.where(cut[:, :, None] == cut[:, None, :], 0.0, -100.0)
    mask[:, AREA:, :] = PADDED
    mask = np.tile(mask, (1, 1, GROUP))
    perm = np.zeros((across * across * ROWS, SIDE * SIDE), np.float32)
    for w in range(across * across):
        for s in range(AREA):
            r = ((w // across) * WIN + s // WIN + SHIFT) % SIDE
            c = ((w % across) * WIN + s % WIN + SHIFT) % SIDE
            perm[w * ROWS + s, r * SIDE + c] = 1.0
    return index, mask, perm


def dot(a, b, dims=((1,), (0,))):
    return lax.dot_general(a, b, (dims, ((), ())), preferred_element_type=F32)


NT = ((1,), (1,))
TN = ((0,), (0,))


def standardize(x):
    c = x - jnp.mean(x, axis=-1, keepdims=True)
    inv = lax.rsqrt(jnp.mean(c * c, axis=-1, keepdims=True) + EPSILON)
    return c * inv, inv


def head_masks(dtype):
    lane = lax.broadcasted_iota(jnp.int32, (1, GROUP * HD), 1) // HD
    return [(lane == h).astype(F32).astype(dtype) for h in range(GROUP)]


def spread(x, masks):
    return jnp.concatenate([x * m for m in masks], axis=0)


def gather_heads(y, masks):
    out = y[:ROWS] * masks[0]
    for h in range(1, GROUP):
        out = out + y[h * ROWS : (h + 1) * ROWS] * masks[h]
    return out


def bits_of(n):
    return [1 << b for b in reversed(range(n.bit_length() - 1))]

class Cube:
    def __init__(self, fsdp, tp):
        self.f, self.t = lax.axis_index("fsdp"), lax.axis_index("tp")
        self.digits = [("tp", b) for b in bits_of(tp)] + [("fsdp", b) for b in bits_of(fsdp)]
        self.own = [lax.rem((self.t if a == "tp" else self.f) // b, 2) for a, b in self.digits]
        self.count = len(self.digits)
        self.n_t = len(bits_of(tp))

    def partner(self, k):
        axis, b = self.digits[k]
        step = b * (1 - 2 * self.own[k])
        if axis == "tp":
            return (self.f, self.t + step)
        return (self.f + step, self.t)

    def at(self, free, flip=None):
        out = []
        for k in range(self.count):
            if k in free:
                out.append(slice(None))
            else:
                out.append(1 - self.own[k] if k == flip else self.own[k])
        return tuple(out)


def greet(cube, digits):
    bar = pltpu.get_barrier_semaphore()
    for k in digits:
        pl.semaphore_signal(bar, inc=1, device_id=cube.partner(k), device_id_type=MESH)
    pl.semaphore_wait(bar, len(digits))


def gather_orders(cube):
    t, f = list(range(cube.n_t)), list(range(cube.n_t, cube.count))
    return (f + t, f[:-1] + t[:-1] + f[-1:] + t[-1:])


LAG = 1


class Gather:
    def __init__(self, cube, full, chunks, send, recv):
        self.cube, self.full, self.chunks, self.send, self.recv = cube, full, chunks, send, recv
        self.orders = gather_orders(cube)

    def copies(self, c, s):
        lo, hi = self.chunks[c]
        rows = self.full.shape[self.cube.count]
        half = rows // 2
        for h, order in enumerate(self.orders):
            ref = self.full.at[self.cube.at(order[:s]) + (pl.ds(h * half, half), pl.ds(lo, hi - lo))]
            i = (c * self.cube.count + s) * 2 + h
            yield pltpu.make_async_remote_copy(ref, ref, self.send.at[i], self.recv.at[i],
                device_id=self.cube.partner(order[s]), device_id_type=MESH)

    def start(self, c, s):
        for copy in self.copies(c, s):
            copy.start()

    def wait(self, c, s):
        for copy in self.copies(c, s):
            copy.wait()

    def plan(self):
        n = self.cube.count
        return sorted(((c, s) for c in range(len(self.chunks)) for s in range(n + 1)), key=lambda e: (LAG * e[0] + e[1], e[0]))

    def advance(self, c, s):
        if s > 0:
            self.wait(c, s - 1)
        if s < self.cube.count:
            self.start(c, s)


LANES = GROUP * HD
SMALL = 16
W_SMALL = 3 * LANES
W_PROJ = 5 * LANES
W_ONE = 6 * LANES


def digits_of(value, n):
    return tuple((value >> (n - 1 - k)) & 1 for k in range(n))


def front_kernel(*refs, fsdp, tp, chunks):
    vectors, refs = refs[:6], refs[6:]
    (bq_in, b1_in, tab_in, wq_in, wp_in, w1_in, w2_in, img_ref, rel_ref, mask_ref, perm_ref, permt_ref,
     full_ref, qkv_ref, p_ref, mix_ref, vec_ref, b1_ref,
     pack, wq, few, bq, tab, table, bias_scr, o_scr, local, send, recv) = refs
    step, steps = pl.program_id(0), pl.num_programs(0)
    cube = Cube(fsdp, tp)
    n, n_t, n_f = cube.count, cube.n_t, cube.count - cube.n_t
    n_win, n_grp = mask_ref.shape[0], tp
    gw = LANES
    cut, ff_cut = w1_in.shape
    heads, span = tab_in.shape
    gather = Gather(cube, full_ref, chunks, send, recv)
    order = gather.plan()
    ready = order.index((0, n)) + 1
    everything = (slice(None),) * n

    @pl.when(step == 0)
    def _():
        pack[:, W_SMALL:W_PROJ] = jnp.zeros((cut, W_PROJ - W_SMALL), BF16)
        for i, ref in enumerate(vectors):
            pack[i : i + 1, W_SMALL : W_SMALL + cut] = ref[...]
        for k in range(3):
            pack[:, k * gw : (k + 1) * gw] = wq_in[k]
            pack[6 + k : 7 + k, W_SMALL : W_SMALL + gw] = bq_in[k : k + 1]
        for k in range(ff_cut // gw):
            pack[9 + k : 10 + k, W_SMALL : W_SMALL + gw] = b1_in[0:1, k * gw : (k + 1) * gw]
        pack[0:heads, W_SMALL + gw : W_PROJ] = tab_in[:, :gw]
        pack[heads : 2 * heads, W_SMALL + gw : W_SMALL + span] = tab_in[:, gw:]
        pack[:, W_PROJ:W_ONE] = wp_in[...]
        pack[:, W_ONE : W_ONE + ff_cut] = w1_in[...]
        pack[:, W_ONE + ff_cut :] = w2_in[...]
        own = pltpu.make_async_copy(pack, full_ref.at[cube.at(())], local.at[0])
        own.start()
        greet(cube, range(n))
        own.wait()
        for c, s in order[:ready]:
            gather.advance(c, s)
        loads = [
            pltpu.make_async_copy(full_ref.at[everything + (slice(None), pl.ds(0, 3 * gw))], wq, local.at[0]),
            pltpu.make_async_copy(
                full_ref.at[everything + (pl.ds(0, SMALL), pl.ds(W_SMALL, W_PROJ - W_SMALL))], few, local.at[1]
            ),
        ]
        for ld in loads:
            ld.start()
        for ld in loads:
            ld.wait()
        vec_ref[...] = jnp.zeros_like(vec_ref)
        for f in range(fsdp):
            part = few[(0,) * n_t + digits_of(f, n_f)].astype(F32)
            vec_ref[0:6, f * cut : (f + 1) * cut] = part[0:6, :cut]
        for t in range(tp):
            part = few[digits_of(t, n_t) + (0,) * n_f].astype(F32)
            for k in range(3):
                at = (3 * t + k) * gw
                bq[0:1, at : at + gw] = part[6 + k : 7 + k, :gw]
            for k in range(ff_cut // gw):
                b1_ref[k : k + 1, t * gw : (t + 1) * gw] = part[9 + k : 10 + k, :gw]
            tab[t * heads : (t + 1) * heads, :gw] = part[0:heads, gw:]
            tab[t * heads : (t + 1) * heads, gw:] = part[heads : 2 * heads, gw:]
        table_rows = tab[...].astype(BF16)
        wide = 8 * ROWS
        for k in range(ROWS * ROWS // wide):
            entry = lax.broadcasted_iota(jnp.int32, (2 * gw, wide), 0)
            hot = (entry == rel_ref[0:1, k * wide : (k + 1) * wide]).astype(F32).astype(BF16)
            value = dot(table_rows, hot)
            for j in range(8):
                table[:, k * 8 + j, :] = value[:, j * ROWS : (j + 1) * ROWS]
        for g in range(n_grp):
            full = jnp.concatenate([table[g * GROUP + h] for h in range(GROUP)], axis=1)
            for w in range(n_win):
                bias_scr[g, w] = full + mask_ref[w]

    rest = order[ready:]
    for i, (c, s) in enumerate(rest):
        at = 1 + 2 * (i // 2)

        @pl.when(step == jnp.minimum(at, steps - 1))
        def _(c=c, s=s):
            gather.advance(c, s)

    x = img_ref[0].astype(F32)
    xhat, _ = standardize(x)
    normed = (xhat * vec_ref[0:1] + vec_ref[1:2]).astype(BF16)
    xp = dot(perm_ref[...], normed).astype(BF16)
    mb, mf = head_masks(BF16), head_masks(F32)
    for g in range(n_grp):
        c0 = g * 3 * gw
        weight = wq[digits_of(g, n_t)].reshape(fsdp * cut, 3 * gw)
        acc = dot(xp, weight) + bq[0:1, c0 : c0 + 3 * gw]
        qkv_ref[0, :, c0 : c0 + gw] = (acc[:, :gw] * (HD ** -0.5)).astype(BF16)
        qkv_ref[0, :, c0 + gw : c0 + 3 * gw] = acc[:, gw:].astype(BF16)

    def part(g, w, j):
        return qkv_ref[0, w * ROWS : (w + 1) * ROWS, (3 * g + j) * gw : (3 * g + j + 1) * gw]

    def score(g, w):
        return dot(part(g, w, 1), spread(part(g, w, 0), mb), NT) + bias_scr[g, w]

    def store(g, w, o):
        o_scr[w * ROWS : (w + 1) * ROWS, g * gw : (g + 1) * gw] = gather_heads(o, mf).astype(BF16)

    units = [(g, w) for g in range(n_grp) for w in range(n_win)]
    ahead, behind = score(*units[0]), None
    for at, (g, w) in enumerate(units):
        s = ahead
        if at + 1 < len(units):
            ahead = score(*units[at + 1])
        e = jnp.exp(s - jnp.max(s, axis=0, keepdims=True))
        p = (e * (1.0 / jnp.sum(e, axis=0, keepdims=True))).astype(BF16)
        p_ref[0, g, w] = p
        o = dot(p, part(g, w, 2), TN)
        if behind is not None:
            store(*behind)
        behind = (g, w, o)
    store(*behind)
    mix_ref[0] = dot(permt_ref[...], o_scr[...]).astype(BF16)


def front(vectors, b_qkv, b_one, table, w_qkv, w_proj, w_one, w_two, images, consts, fsdp, tp):
    rel, mask, perm, permt = consts
    n_img, t, c = images.shape
    cut, ff_cut = w_one.shape
    gw = LANES
    n_win = mask.shape[0]
    rows, cols = n_win * ROWS, W_ONE + 2 * ff_cut
    heads = tp * table.shape[0]
    n_t, n_f = len(bits_of(tp)), len(bits_of(fsdp))
    n = n_t + n_f
    chunks = ((0, W_PROJ), (W_PROJ, W_ONE + ff_cut), (W_ONE + ff_cut, cols))
    n_sem = len(chunks) * n * 2
    once = lambda a: pl.BlockSpec(a.shape, lambda i: (0,) * a.ndim, pipeline_mode=pl.Buffered(1))
    whole = lambda s: pl.BlockSpec(s, lambda i: (0,) * len(s))
    small = tuple(vectors) + (b_qkv, b_one, table, w_qkv, w_proj, w_one, w_two)
    return pl.pallas_call(
        functools.partial(front_kernel, fsdp=fsdp, tp=tp, chunks=chunks),
        grid=(n_img,),
        in_specs=[once(a) for a in small]
        + [pl.BlockSpec((1, t, c), lambda i: (i, 0, 0))]
        + [once(a) for a in (rel, mask, perm, permt)],
        out_specs=[
            pl.BlockSpec(memory_space=pl.ANY),
            pl.BlockSpec((1, rows, 3 * tp * gw), lambda i: (i, 0, 0)),
            pl.BlockSpec((1, tp, n_win, ROWS, GROUP * ROWS), lambda i: (i, 0, 0, 0, 0)),
            pl.BlockSpec((1, t, c), lambda i: (i, 0, 0)),
            whole((8, c)),
            whole((ff_cut // gw, tp * gw)),
        ],
        out_shape=[
            jax.ShapeDtypeStruct((2,) * n + (cut, cols), BF16),
            jax.ShapeDtypeStruct((n_img, rows, 3 * tp * gw), BF16),
            jax.ShapeDtypeStruct((n_img, tp, n_win, ROWS, GROUP * ROWS), BF16),
            jax.ShapeDtypeStruct((n_img, t, c), BF16),
            jax.ShapeDtypeStruct((8, c), F32),
            jax.ShapeDtypeStruct((ff_cut // gw, tp * gw), F32),
        ],
        scratch_shapes=[
            pltpu.VMEM((cut, cols), BF16),
            pltpu.VMEM((2,) * n + (cut, 3 * gw), BF16),
            pltpu.VMEM((2,) * n + (SMALL, W_PROJ - W_SMALL), BF16),
            pltpu.VMEM((1, 3 * tp * gw), F32),
            pltpu.VMEM((heads, 2 * gw), F32),
            pltpu.VMEM((heads, ROWS, ROWS), F32),
            pltpu.VMEM((tp, n_win, ROWS, GROUP * ROWS), F32),
            pltpu.VMEM((rows, c), BF16),
            pltpu.SemaphoreType.DMA((2,)),
            pltpu.SemaphoreType.DMA((n_sem,)),
            pltpu.SemaphoreType.DMA((n_sem,)),
        ],
        compiler_params=pltpu.CompilerParams(
            vmem_limit_bytes=60 << 20, collective_id=1, has_side_effects=True
        ),
        name="front",
    )(*small, images, rel, mask, perm, permt)


SQRT_HALF = float(np.sqrt(0.5))
INV_SQRT_2PI = float(1.0 / np.sqrt(2.0 * np.pi))


class Spread:
    def __init__(self, cube, full, send, recv):
        self.cube, self.full, self.send, self.recv = cube, full, send, recv
        self.stages = cube.n_t

    def ref(self, s, i):
        own = self.cube.own
        return self.full.at[tuple(slice(None) if k < s else own[k] for k in range(self.stages)) + (i,)]

    def copy(self, s, i):
        ref = self.ref(s, i)
        return pltpu.make_async_remote_copy(
            ref, ref, self.send.at[s, i], self.recv.at[s, i], device_id=self.cube.partner(s), device_id_type=MESH
        )


def blocks_of(n, body):
    if n == 0:
        body(())
        return

    def one(i, carry):
        body(tuple(lax.rem(lax.div(i, 2 ** (n - 1 - k)), 2) for k in range(n)))
        return carry

    lax.fori_loop(0, 2**n, one, 0)


class Reduce:
    def __init__(self, cube, acc, order, bufs, send, recv, n_digits, out):
        self.cube, self.acc, self.order, self.bufs = cube, acc, order, bufs
        self.send, self.recv, self.n_digits, self.out = send, recv, n_digits, out
        self.stages = len(order)

    def at(self, free, flip=None):
        own = self.cube.own
        return tuple(
            slice(None) if k in free else (1 - own[k] if k == flip else own[k]) for k in range(self.n_digits)
        )

    def left(self, s):
        return sorted(k for k in self.order[s + 1 :] if k < self.n_digits)

    def copy(self, s):
        return pltpu.make_async_remote_copy(
            self.acc.at[self.at(self.left(s), self.order[s])],
            self.bufs[s],
            self.send.at[s],
            self.recv.at[s],
            device_id=self.cube.partner(self.order[s]),
            device_id_type=MESH,
        )

    def start(self):
        self.copy(0).start()

    def advance(self, s):
        self.copy(s).wait()
        free = self.left(s)
        own = self.cube.own

        def add(index):
            at = dict(zip(free, index))
            dst = tuple(at.get(k, own[k]) for k in range(self.n_digits))
            if s + 1 == self.stages:
                self.out(self.acc[dst].astype(F32) + self.bufs[s][index].astype(F32))
            else:
                self.acc[dst] = self.acc[dst] + self.bufs[s][index]

        blocks_of(len(free), add)
        if s + 1 < self.stages:
            self.copy(s + 1).start()


def reduce_orders(n_t, n):
    t, f = list(range(n_t)), list(range(n_t, n))
    t_in, f_in = t[1:][::-1], f[::-1]
    early = (t_in + f_in + t[:1], t_in + f[:-1][::-1] + f[-1:] + t[:1])
    late = (t_in + f[-1:] + t[:1] + f[:-1][::-1], t_in + t[:1] + f_in)
    return early, late, t[::-1] + f_in


def layer_kernel(live_ref, img_hbm, cot_hbm, mix_ref, w_hbm, vec_ref, b1_ref, qkv_ref, p_ref, perm_ref, permt_ref,
                 out_ref, gin_ref, dqkv_ref, dw1_ref, dw2_ref, dwp_ref, small_ref,
                 img_ref, cot_ref, w1_ref, w2_ref, wq_ref, wp, act, slope, normed_two, up_scr, gres_scr,
                 db1, dvec, dqkv_scr, dw, db, dtab, res_scr, acc, acc_p, late_a, late_b, small, *rest,
                 fsdp, tp, per, n_q):
    step = pl.program_id(0)
    cube = Cube(fsdp, tp)
    n, n_t, n_f = cube.count, cube.n_t, cube.count - cube.n_t
    n_img, n_tok, c = img_ref.shape
    n_grp, n_win = p_ref.shape[1:3]
    gw = LANES
    cut = c // fsdp
    fwd_steps = n_img // per
    bwd_at = fwd_steps
    att_at = bwd_at + n_q
    last_step = att_at + n_img - 1

    early, late, both = reduce_orders(n_t, n)
    bufs, rest = rest[: 5 * n], rest[5 * n :]
    load, local, send, recv, local_in, send_in, recv_in, rs_send, rs_recv = rest

    columns_at = lambda lo, width: w_hbm.at[:, :, pl.ds(lo, width)]
    wide_q = n_q * gw
    loads = [
        pltpu.make_async_copy(columns_at(lo, ref.shape[2]), ref, load.at[k])
        for k, (lo, ref) in enumerate(
            ((W_PROJ + gw, w1_ref), (W_PROJ + gw + wide_q, w2_ref), (0, wq_ref))
        )
    ]
    loads += [pltpu.make_async_copy(img_hbm, img_ref, load.at[3]), pltpu.make_async_copy(cot_hbm, cot_ref, load.at[4])]
    loads += [
        pltpu.make_async_copy(
            w_hbm.at[g, :, pl.ds(W_PROJ, gw)], wp.at[:, pl.ds(g * gw, gw)], load.at[5 + g]
        )
        for g in range(n_grp)
    ]
    gmix_scr = cot_ref

    def result_of(q):
        def out(total):
            dw1_ref[:, q * gw : (q + 1) * gw] = total[:, :gw]
            dw2_ref[:, q * gw : (q + 1) * gw] = total[:, gw:]

        return out

    def result_p(total):
        dwp_ref[...] = total

    def result_a(total):
        dqkv_ref[:, : 2 * gw] = total

    def result_b(total):
        dqkv_ref[:, 2 * gw :] = total

    def result_s(total):
        small_ref[...] = total

    plans = [
        (acc.at[q], [ref.at[q] for ref in bufs[:n]], early[q % 2], n, result_of(q)) for q in range(n_q)
    ]
    plans += [
        (acc_p, bufs[n : 2 * n], early[0], n, result_p),
        (late_a, bufs[2 * n : 3 * n], late[0], n, result_a),
        (late_b, bufs[3 * n : 4 * n], late[1], n, result_b),
        (small, bufs[4 * n :], both, n_t, result_s),
    ]
    reduces = [
        Reduce(cube, ref, order, buf, rs_send.at[k], rs_recv.at[k], d, out)
        for k, (ref, buf, order, d, out) in enumerate(plans)
    ]
    n_early = n_q + 1
    spread_out = Spread(cube, out_ref, send, recv)
    spread_in = Spread(cube, gin_ref, send_in, recv_in)

    def keep_out(i):
        return pltpu.make_async_copy(res_scr.at[pl.ds(i * per, per)], spread_out.ref(0, i), local.at[i])

    def keep_in(i):
        return pltpu.make_async_copy(res_scr.at[i], spread_in.ref(0, i), local_in.at[i])

    events = {}

    def plan(at, work):
        events.setdefault(at, []).append(work)

    def point(k):
        for at in sorted(events):
            if at[1] == k:

                @pl.when(step == at[0])
                def _(at=at):
                    for work in events[at]:
                        work()

    def send_out(i):
        keep_out(i).wait()
        spread_out.copy(0, i).start()

    def pass_out(i, s):
        spread_out.copy(s - 1, i).wait()
        spread_out.copy(s, i).start()

    def send_in_(i):
        keep_in(i).wait()
        spread_in.copy(0, i).start()

    def pass_in(i, s):
        spread_in.copy(s - 1, i).wait()
        spread_in.copy(s, i).start()

    for i in range(fwd_steps):
        plan((i + 1, 0), functools.partial(send_out, i))
    later = [att_at - 1 + 3 * i for i in range(fwd_steps)]
    for s in range(1, n_t):
        for i in range(fwd_steps):
            plan((min(later[i] + s - 1, last_step), 0), functools.partial(pass_out, i, s))
    for i in range(n_img - 1):
        plan((att_at + i + 1, 0), functools.partial(send_in_, i))
    tail = []
    for i in range(n_img):
        for s in range(1, n_t):
            at = att_at + i + 3 + s
            if at <= last_step:
                plan((at, 0), functools.partial(pass_in, i, s))
            else:
                tail.append(functools.partial(pass_in, i, s))
    ends = []
    for k in range(n_early):
        begin = (bwd_at + k + 1, 1) if k + 1 < n_q else (att_at, 0)
        plan(begin, reduces[k].start)
        slots = SLOTS[k] if k < len(SLOTS) else ()
        for s in range(n):
            work = functools.partial(reduces[k].advance, s)
            if s < len(slots):
                plan((bwd_at + slots[s][0], slots[s][1]), work)
            else:
                ends.append(work)

    @pl.when(step == 0)
    def _():
        for ld in loads:
            ld.start()
        greet(cube, range(n))
        dw[...] = jnp.zeros_like(dw)
        dvec[...] = jnp.zeros_like(dvec)
        db[...] = jnp.zeros_like(db)
        db1[...] = jnp.zeros_like(db1)
        dtab[...] = jnp.zeros_like(dtab)
        for ld in loads:
            ld.wait()

    def columns(ref, q):
        at = pl.ds(pl.multiple_of(q * gw, gw), gw)
        return jnp.concatenate([ref[g, :, at] for g in range(n_grp)], axis=1)

    def rows_of(ref, b):
        return jnp.concatenate([ref[b * per + i] for i in range(per)], axis=0)

    def middle(b):
        mixed = rows_of(mix_ref, b)
        res = rows_of(img_ref, b).astype(F32) + (dot(mixed, wp[...], NT) + vec_ref[2:3])
        return (mixed, res) + standardize(res)

    @pl.when(step < bwd_at)
    def _():
        point(0)
        live = jnp.concatenate(
            [jnp.full((n_tok, 1), 1.0, F32) * live_ref[step * per + i] for i in range(per)], axis=0
        )
        up = rows_of(cot_ref, step).astype(F32) * live
        up_scr[step] = up.astype(BF16)
        dvec[5:6] += jnp.sum(up, axis=0, keepdims=True)
        mixed, res, xhat, _ = middle(step)
        normed_two[step] = (xhat * vec_ref[3:4] + vec_ref[4:5]).astype(BF16)

        def hidden_part(q, branch):
            hid = dot(normed_two[step], columns(w1_ref, q)) + b1_ref[pl.ds(q, 1)]
            cdf = 0.5 * (1.0 + lax.erf(hid * SQRT_HALF))
            a = (hid * cdf).astype(BF16)
            act[step, q] = a
            slope[step, q] = (cdf + hid * (jnp.exp(-0.5 * hid * hid) * INV_SQRT_2PI)).astype(BF16)
            return branch + dot(a, columns(w2_ref, q), NT)

        total = lax.fori_loop(0, n_q, hidden_part, res + vec_ref[5:6])
        out = (live * total).astype(BF16)
        for i in range(per):
            res_scr[step * per + i] = out[i * n_tok : (i + 1) * n_tok]
        keep_out(step).start()

    @pl.when(jnp.logical_and(step >= bwd_at, step < att_at))
    def _():
        q = step - bwd_at
        point(0)
        w2 = columns(w2_ref, q)
        d_one = d_two = None
        for b in range(fwd_steps):
            if b == 1:
                point(1)
            up = up_scr[b]
            dh = (dot(up, w2) * slope[b, q].astype(F32)).astype(BF16)
            slope[b, q] = dh
            db1[pl.ds(q, 1)] += jnp.sum(dh.astype(F32), axis=0, keepdims=True)
            one, two = dot(normed_two[b], dh, TN), dot(up, act[b, q], TN)
            d_one, d_two = (one, two) if b == 0 else (d_one + one, d_two + two)
        for t in range(n_grp):
            for f in range(fsdp):
                at = (q,) + digits_of(t, n_t) + digits_of(f, n_f)
                r, l = slice(f * cut, (f + 1) * cut), slice(t * gw, (t + 1) * gw)
                acc[at + (slice(None), slice(0, gw))] = d_one[r, l].astype(BF16)
                acc[at + (slice(None), slice(gw, 2 * gw))] = d_two[r, l].astype(BF16)

    @pl.when(step == att_at - 1)
    def _():
        def back(b, d_proj):
            dn = dot(slope[b, 0], columns(w1_ref, 0), NT)
            for k in range(1, n_q):
                dn = dn + dot(slope[b, k], columns(w1_ref, k), NT)
            mixed, _, xhat, inv = middle(b)
            d = dn * vec_ref[3:4]
            gres = up_scr[b].astype(F32) + inv * (
                d - jnp.mean(d, axis=-1, keepdims=True) - xhat * jnp.mean(d * xhat, axis=-1, keepdims=True)
            )
            gatt = gres.astype(BF16)
            gmix = dot(gatt, wp[...]).astype(BF16)
            for i in range(per):
                r = slice(i * n_tok, (i + 1) * n_tok)
                gres_scr[b * per + i] = gres[r]
                gmix_scr[b * per + i] = gmix[r]
            dvec[2:3] += jnp.sum(gatt.astype(F32), axis=0, keepdims=True)
            dvec[3:4] += jnp.sum(dn * xhat, axis=0, keepdims=True)
            dvec[4:5] += jnp.sum(dn, axis=0, keepdims=True)
            return d_proj + dot(gatt, mixed, TN)

        d_proj = lax.fori_loop(0, fwd_steps, back, jnp.zeros((c, c), F32))
        for t in range(n_grp):
            for f in range(fsdp):
                at = digits_of(t, n_t) + digits_of(f, n_f)
                acc_p[at] = d_proj[f * cut : (f + 1) * cut, t * gw : (t + 1) * gw].astype(BF16)

    @pl.when(step >= att_at)
    def _():
        j = step - att_at
        mb, mf = head_masks(BF16), head_masks(F32)
        point(0)
        x = img_ref[j].astype(F32)
        xhat, inv = standardize(x)
        normed = (xhat * vec_ref[0:1] + vec_ref[1:2]).astype(BF16)
        xp = dot(perm_ref[...], normed).astype(BF16)
        gm = dot(perm_ref[...], gmix_scr[j]).astype(BF16)
        dn = jnp.zeros((n_win * ROWS, c), F32)
        for g in range(n_grp):
            if g > 0:
                point(g)
            c0 = g * 3 * gw
            tab = jnp.zeros((ROWS, GROUP * ROWS), F32)
            cuts = [slice(w * ROWS, (w + 1) * ROWS) for w in range(n_win)]
            dos = [spread(gm[r, g * gw : (g + 1) * gw], mb) for r in cuts]
            dps = [dot(qkv_ref[0, r, c0 + 2 * gw : c0 + 3 * gw], do, NT) for r, do in zip(cuts, dos)]
            ps = [p_ref[0, g, w] for w in range(n_win)]
            dvs = [dot(p, do) for p, do in zip(ps, dos)]
            dss = []
            for p, dp in zip(ps, dps):
                pf = p.astype(F32)
                ds = pf * (dp - jnp.sum(pf * dp, axis=0, keepdims=True))
                tab = tab + ds
                dss.append(ds.astype(BF16))
            dks = [dot(ds, spread(qkv_ref[0, r, c0 : c0 + gw], mb)) for r, ds in zip(cuts, dss)]
            dqs = [dot(ds, qkv_ref[0, r, c0 + gw : c0 + 2 * gw], TN) for r, ds in zip(cuts, dss)]
            for r, dq, dk, dv in zip(cuts, dqs, dks, dvs):
                dqkv_scr[r, :gw] = (gather_heads(dq, mf) * (HD ** -0.5)).astype(BF16)
                dqkv_scr[r, gw : 2 * gw] = dk.astype(BF16)
                dqkv_scr[r, 2 * gw :] = dv.astype(BF16)
            dtab[g] += tab
            dqkv = dqkv_scr[...]
            db[0:1, c0 : c0 + 3 * gw] += jnp.sum(dqkv.astype(F32), axis=0, keepdims=True)
            dw[g] += dot(xp, dqkv, TN)
            dn = dn + dot(dqkv, wq_ref[g], NT)
        hi = dn.astype(BF16)
        lo = (dn - hi.astype(F32)).astype(BF16)
        dn = dot(permt_ref[...], hi) + dot(permt_ref[...], lo)
        d = dn * vec_ref[0:1]
        gin = inv * (
            d - jnp.mean(d, axis=-1, keepdims=True) - xhat * jnp.mean(d * xhat, axis=-1, keepdims=True)
        )
        res_scr[j] = (gres_scr[j] + gin).astype(BF16)
        keep_in(j).start()
        dvec[0:1] += jnp.sum(dn * xhat, axis=0, keepdims=True)
        dvec[1:2] += jnp.sum(dn, axis=0, keepdims=True)

    @pl.when(step == last_step)
    def _():
        def fill(index):
            t, f = index[:n_t], index[n_t:]
            at = lambda part: functools.reduce(lambda a, b: 2 * a + b, part)
            rows = pl.ds(pl.multiple_of(at(f) * cut, cut), cut)
            late_a[index] = dw[at(t), rows, : 2 * gw].astype(BF16)
            late_b[index] = dw[at(t), rows, 2 * gw :].astype(BF16)

        blocks_of(n, fill)
        for red in reduces[n_early : n_early + 2]:
            red.start()
        wide = GROUP * ROWS
        for g in range(n_grp):
            panel = small.at[digits_of(g, n_t)]
            panel[:ROWS] = dtab[g]
            c0 = g * 3 * gw
            panel[ROWS : ROWS + 1] = db[0:1, c0 : c0 + wide]
            panel[ROWS + 1 : ROWS + 2] = jnp.concatenate(
                [db[0:1, c0 + wide : c0 + 3 * gw], jnp.zeros((1, 2 * wide - 3 * gw), F32)], axis=1
            )
            r = ROWS + 2
            for q in range(0, n_q, 2):
                pair = [db1[q + k : q + k + 1, g * gw : (g + 1) * gw] for k in range(2)]
                panel[r : r + 1] = jnp.concatenate(pair, axis=1)
                r = r + 1
            for i in range(6):
                for k in range(c // wide):
                    panel[r : r + 1] = dvec[i : i + 1, k * wide : (k + 1) * wide]
                    r = r + 1
        reduces[n_early + 2].start()
        send_in_(n_img - 1)
        for work in ends:
            work()
        for s in range(n):
            for red in reduces[n_early:]:
                red.advance(s)
            if s == 0:
                for work in tail[: len(tail) // 2]:
                    work()
        for work in tail[len(tail) // 2 :]:
            work()
        for i in range(fwd_steps):
            spread_out.copy(n_t - 1, i).wait()
        for i in range(n_img):
            spread_in.copy(n_t - 1, i).wait()


SLOTS = (
    ((2, 0), (3, 1), (4, 0), (5, 2), (8, 0)),
    ((3, 0), (4, 0), (6, 0), (8, 0), (10, 0)),
    ((4, 0), (6, 2), (8, 2), (10, 2)),
    ((5, 2), (8, 0), (9, 3), (11, 2)),
    ((5, 2), (8, 0), (9, 3), (11, 2)),
)


def layer(live, images, out_grad, mixed, w_all, vecs, b1, qkv, p, perm, permt, fsdp, tp, per=4):
    n_img, t, c = mixed.shape
    rows, cols = qkv.shape[1:]
    n_grp, n_win = p.shape[1:3]
    gw, wide = LANES, GROUP * ROWS
    n_q = b1.shape[0]
    ff_cut = n_q * gw
    cut = c // fsdp
    n_t, n_f = len(bits_of(tp)), len(bits_of(fsdp))
    n = n_t + n_f
    digits = (2,) * n
    n_small = ROWS + 2 + ff_cut // wide + 6 * (c // wide)
    fwd_steps = n_img // per
    att_at = fwd_steps + n_q
    bufs = []
    for lead, width in (((n_q,), 2 * gw), ((), gw), ((), 2 * gw), ((), gw)):
        bufs += [pltpu.VMEM(lead + (2,) * (n - 1 - s) + (cut, width), BF16) for s in range(n)]
    bufs += [pltpu.VMEM((2,) * max(n_t - 1 - s, 0) + (n_small, wide), F32) for s in range(n)]
    whole = lambda s: pl.BlockSpec(s, lambda i: (0,) * len(s))
    once = lambda s: pl.BlockSpec(s, lambda i: (0,) * len(s), pipeline_mode=pl.Buffered(1))
    image = lambda i: jnp.clip(i - att_at, 0, n_img - 1)
    any_spec = pl.BlockSpec(memory_space=pl.ANY)
    hidden = (fwd_steps, n_q, per * t, n_grp * gw)
    return pl.pallas_call(
        functools.partial(layer_kernel, fsdp=fsdp, tp=tp, per=per, n_q=n_q),
        grid=(att_at + n_img,),
        in_specs=[
            pl.BlockSpec(memory_space=pltpu.SMEM),
            any_spec,
            any_spec,
            once(mixed.shape),
            any_spec,
            once(vecs.shape),
            once(b1.shape),
            pl.BlockSpec((1, rows, cols), lambda i: (image(i), 0, 0)),
            pl.BlockSpec((1,) + p.shape[1:], lambda i: (image(i), 0, 0, 0, 0)),
            once(perm.shape),
            once(permt.shape),
        ],
        out_specs=[any_spec, any_spec]
        + [whole(s) for s in ((cut, 3 * gw), (cut, ff_cut), (cut, ff_cut), (cut, gw), (n_small, wide))],
        out_shape=[
            jax.ShapeDtypeStruct((2,) * n_t + (fwd_steps, per, t, c), BF16),
            jax.ShapeDtypeStruct((2,) * n_t + (n_img, t, c), BF16),
            jax.ShapeDtypeStruct((cut, 3 * gw), F32),
            jax.ShapeDtypeStruct((cut, ff_cut), F32),
            jax.ShapeDtypeStruct((cut, ff_cut), F32),
            jax.ShapeDtypeStruct((cut, gw), F32),
            jax.ShapeDtypeStruct((n_small, wide), F32),
        ],
        scratch_shapes=[
            pltpu.VMEM((n_img, t, c), BF16),
            pltpu.VMEM((n_img, t, c), BF16),
            pltpu.VMEM((n_grp, c, ff_cut), BF16),
            pltpu.VMEM((n_grp, c, ff_cut), BF16),
            pltpu.VMEM((n_grp, c, 3 * gw), BF16),
            pltpu.VMEM((c, c), BF16),
            pltpu.VMEM(hidden, BF16),
            pltpu.VMEM(hidden, BF16),
            pltpu.VMEM((fwd_steps, per * t, c), BF16),
            pltpu.VMEM((fwd_steps, per * t, c), BF16),
            pltpu.VMEM((n_img, t, c), F32),
            pltpu.VMEM((8, n_grp * gw), F32),
            pltpu.VMEM((8, c), F32),
            pltpu.VMEM((rows, 3 * gw), BF16),
            pltpu.VMEM((n_grp, c, 3 * gw), F32),
            pltpu.VMEM((1, cols), F32),
            pltpu.VMEM((n_grp, ROWS, wide), F32),
            pltpu.VMEM((n_img, t, c), BF16),
            pltpu.VMEM((n_q,) + digits + (cut, 2 * gw), BF16),
            pltpu.VMEM(digits + (cut, gw), BF16),
            pltpu.VMEM(digits + (cut, 2 * gw), BF16),
            pltpu.VMEM(digits + (cut, gw), BF16),
            pltpu.VMEM((2,) * n_t + (n_small, wide), F32),
            *bufs,
            pltpu.SemaphoreType.DMA((5 + n_grp,)),
            pltpu.SemaphoreType.DMA((fwd_steps,)),
            pltpu.SemaphoreType.DMA((n_t, fwd_steps)),
            pltpu.SemaphoreType.DMA((n_t, fwd_steps)),
            pltpu.SemaphoreType.DMA((n_img,)),
            pltpu.SemaphoreType.DMA((n_t, n_img)),
            pltpu.SemaphoreType.DMA((n_t, n_img)),
            pltpu.SemaphoreType.DMA((n_q + 4, n)),
            pltpu.SemaphoreType.DMA((n_q + 4, n)),
        ],
        compiler_params=pltpu.CompilerParams(
            vmem_limit_bytes=60 << 20, collective_id=2, has_side_effects=True
        ),
        name="layer",
    )(live, images, out_grad, mixed, w_all, vecs, b1, qkv, p, perm, permt)


def per_device(
    images,
    attn_norm_gain,
    attn_norm_bias,
    qkv_weight,
    qkv_bias,
    position_table,
    proj_weight,
    proj_bias,
    mlp_norm_gain,
    mlp_norm_bias,
    fc1_weight,
    fc1_bias,
    fc2_weight,
    fc2_bias,
    image_count,
    out_grad,
    *,
    fsdp,
    tp,
):
    index, mask, perm = window_constants()
    span = position_table.shape[0]
    gw = LANES
    cut = qkv_weight.shape[0]
    width = cut * fsdp
    ff_cut = fc1_bias.shape[0]
    n_qkv = qkv_bias.size
    mine = images.shape[0] // tp
    first = lax.axis_index("tp") * mine
    img = lax.dynamic_slice_in_dim(images, first, mine, 0)
    cot = lax.dynamic_slice_in_dim(out_grad, first, mine, 0)
    live = (first + jnp.arange(mine, dtype=jnp.int32) < image_count[0]).astype(F32)
    perm16 = jnp.asarray(perm).astype(BF16)
    consts = (jnp.asarray(index).reshape(1, -1), jnp.asarray(mask), perm16, perm16.T)
    vectors = (attn_norm_gain, attn_norm_bias, proj_bias, mlp_norm_gain, mlp_norm_bias, fc2_bias)
    w_all, qkv, probs, mixed, vecs, b_one = front(
        [v.reshape(1, cut) for v in vectors],
        qkv_bias,
        fc1_bias.reshape(1, ff_cut),
        position_table.T,
        qkv_weight.transpose(1, 0, 2),
        proj_weight.T,
        fc1_weight,
        fc2_weight.T,
        img,
        consts,
        fsdp,
        tp,
    )
    w_all = w_all.reshape(tp, width, w_all.shape[-1])
    output, images_grad, d_qkv, d_one, d_two, d_proj, small = layer(
        live, img, cot, mixed, w_all, vecs, b_one, qkv, probs, consts[2], consts[3], fsdp, tp
    )
    wide = GROUP * ROWS
    hot = (jnp.asarray(index)[None] == jnp.arange(span, dtype=jnp.int32)[:, None, None]).astype(F32)
    d_tab = jnp.einsum(
        "jhi,rji->rh",
        small[:ROWS].reshape(ROWS, GROUP, ROWS),
        hot,
        precision=lax.Precision.HIGHEST,
    )
    at = ROWS + 2
    dqkv_bias = small[ROWS:at].reshape(-1)[:n_qkv].reshape(qkv_bias.shape)
    dfc1_bias = small[at : at + ff_cut // wide].reshape(-1)
    dvec = small[at + ff_cut // wide :].reshape(6, width)
    dvec = lax.dynamic_slice_in_dim(dvec, lax.axis_index("fsdp") * cut, cut, 1)
    return (
        output.reshape(images.shape),
        images_grad.reshape(images.shape),
        dvec[0],
        dvec[1],
        d_qkv.reshape(qkv_weight.shape),
        dqkv_bias,
        d_tab,
        d_proj.T,
        dvec[2],
        dvec[3],
        dvec[4],
        d_one,
        dfc1_bias,
        d_two.T,
        dvec[5],
    )


def solution(mesh):
    P = jax.sharding.PartitionSpec
    return jax.shard_map(
        functools.partial(per_device, fsdp=mesh.shape["fsdp"], tp=mesh.shape["tp"]),
        mesh=mesh,
        in_specs=(
            P("fsdp", None, None),
            P("fsdp"),
            P("fsdp"),
            P("fsdp", None, "tp"),
            P(None, "tp"),
            P(None, "tp"),
            P("tp", "fsdp"),
            P("fsdp"),
            P("fsdp"),
            P("fsdp"),
            P("fsdp", "tp"),
            P("tp"),
            P("tp", "fsdp"),
            P("fsdp"),
            P("fsdp"),
            P("fsdp", None, None),
        ),
        out_specs=(
            P("fsdp", None, None),
            P("fsdp", None, None),
            P("fsdp"),
            P("fsdp"),
            P("fsdp", None, "tp"),
            P(None, "tp"),
            P(None, "tp"),
            P("tp", "fsdp"),
            P("fsdp"),
            P("fsdp"),
            P("fsdp"),
            P("fsdp", "tp"),
            P("tp"),
            P("tp", "fsdp"),
            P("fsdp"),
        ),
        check_vma=False,
    )
```

```python
import functools
import jax
import jax.numpy as jnp
import numpy as np
from jax import lax
from jax.experimental import pallas as pl
from jax.experimental.pallas import tpu as pltpu

HD = 32
WIN = 7
SHIFT = 3
SIDE = 14
AREA = WIN * WIN
ROWS = 64
GROUP = 4
EPSILON = 1e-05
F32 = jnp.float32
BF16 = jnp.bfloat16
PADDED = -1e30
MESH = pl.DeviceIdType.MESH


def window_constants():
    offsets = np.arange(WIN)
    rows, cols = np.repeat(offsets, WIN), np.tile(offsets, WIN)
    relative = (rows[:, None] - rows[None, :] + WIN - 1) * (2 * WIN - 1) + (
        cols[:, None] - cols[None, :] + WIN - 1
    )
    span = (2 * WIN - 1) ** 2
    index = np.full((ROWS, ROWS), span, np.int32)
    index[:AREA, :AREA] = relative.T
    region = np.zeros((SIDE, SIDE), np.int32)
    bounds = ((0, SIDE - WIN), (SIDE - WIN, SIDE - SHIFT), (SIDE - SHIFT, SIDE))
    for a, rr in enumerate(bounds):
        for b, cc in enumerate(bounds):
            region[rr[0] : rr[1], cc[0] : cc[1]] = 3 * a + b
    across = SIDE // WIN
    cut = region.reshape(across, WIN, across, WIN).transpose(0, 2, 1, 3).reshape(across * across, AREA)
    mask = np.zeros((across * across, ROWS, ROWS), np.float32)
    mask[:, :AREA, :AREA] = np.where(cut[:, :, None] == cut[:, None, :], 0.0, -100.0)
    mask[:, AREA:, :] = PADDED
    mask = np.tile(mask, (1, 1, GROUP))
    perm = np.zeros((across * across * ROWS, SIDE * SIDE), np.float32)
    for w in range(across * across):
        for s in range(AREA):
            r = ((w // across) * WIN + s // WIN + SHIFT) % SIDE
            c = ((w % across) * WIN + s % WIN + SHIFT) % SIDE
            perm[w * ROWS + s, r * SIDE + c] = 1.0
    return index, mask, perm


def dot(a, b, dims=((1,), (0,))):
    return lax.dot_general(a, b, (dims, ((), ())), preferred_element_type=F32)


NT = ((1,), (1,))
TN = ((0,), (0,))


def standardize(x):
    c = x - jnp.mean(x, axis=-1, keepdims=True)
    inv = lax.rsqrt(jnp.mean(c * c, axis=-1, keepdims=True) + EPSILON)
    return c * inv, inv


def head_masks(dtype):
    lane = lax.broadcasted_iota(jnp.int32, (1, GROUP * HD), 1) // HD
    return [(lane == h).astype(F32).astype(dtype) for h in range(GROUP)]


def spread(x, masks):
    return jnp.concatenate([x * m for m in masks], axis=0)


def gather_heads(y, masks):
    out = y[:ROWS] * masks[0]
    for h in range(1, GROUP):
        out = out + y[h * ROWS : (h + 1) * ROWS] * masks[h]
    return out


def bits_of(n):
    return [1 << b for b in reversed(range(n.bit_length() - 1))]

class Cube:
    def __init__(self, fsdp, tp):
        self.f, self.t = lax.axis_index("fsdp"), lax.axis_index("tp")
        self.digits = [("tp", b) for b in bits_of(tp)] + [("fsdp", b) for b in bits_of(fsdp)]
        self.own = [lax.rem((self.t if a == "tp" else self.f) // b, 2) for a, b in self.digits]
        self.count = len(self.digits)
        self.n_t = len(bits_of(tp))

    def partner(self, k):
        axis, b = self.digits[k]
        step = b * (1 - 2 * self.own[k])
        if axis == "tp":
            return (self.f, self.t + step)
        return (self.f + step, self.t)

    def at(self, free, flip=None):
        out = []
        for k in range(self.count):
            if k in free:
                out.append(slice(None))
            else:
                out.append(1 - self.own[k] if k == flip else self.own[k])
        return tuple(out)


def greet(cube, digits):
    bar = pltpu.get_barrier_semaphore()
    for k in digits:
        pl.semaphore_signal(bar, inc=1, device_id=cube.partner(k), device_id_type=MESH)
    pl.semaphore_wait(bar, len(digits))


def gather_orders(cube):
    t, f = list(range(cube.n_t)), list(range(cube.n_t, cube.count))
    return (f + t, f[:-1] + t[:-1] + f[-1:] + t[-1:])


class Gather:
    def __init__(self, cube, chunks, send, recv):
        self.cube, self.chunks, self.send, self.recv = cube, chunks, send, recv
        self.lanes = [sum(len(k) for k in chunks[:c]) for c in range(len(chunks))]

    def copies(self, c, s):
        for h, (ref, part, order) in enumerate(self.chunks[c]):
            ref = ref.at[self.cube.at(order[:s]) + part]
            i = (self.lanes[c] + h) * self.cube.count + s
            yield pltpu.make_async_remote_copy(
                ref,
                ref,
                self.send.at[i],
                self.recv.at[i],
                device_id=self.cube.partner(order[s]),
                device_id_type=MESH,
            )

    def plan(self):
        n = self.cube.count
        events = ((c, s) for c in range(len(self.chunks)) for s in range(n + 1))
        return sorted(events, key=lambda e: (LAGS[e[0]] + e[1], e[0]))

    def advance(self, c, s):
        if s > 0:
            for copy in self.copies(c, s - 1):
                copy.wait()
        if s < self.cube.count:
            for copy in self.copies(c, s):
                copy.start()


LAGS = (0, 1, 2)


LANES = GROUP * HD
SMALL = 16
PASSES = (3, 3, 5, 5, 7)
W_ONE = LANES


def digits_of(value, n):
    return tuple((value >> (n - 1 - k)) & 1 for k in range(n))


def front_kernel(*refs, fsdp, tp):
    vectors, refs = refs[:6], refs[6:]
    (bq_in, b1_in, tab_in, wq_in, wp_in, w1_in, w2_in, img_ref, rel_ref, mask_ref, perm_ref, permt_ref,
     full_ref, wq_out, qkv_ref, p_ref, mix_ref, vec_ref, b1_ref,
     pack, wq, few, bq, tab, table, bias_scr, o_scr, local, send, recv) = refs
    step, steps = pl.program_id(0), pl.num_programs(0)
    cube = Cube(fsdp, tp)
    n, n_t, n_f = cube.count, cube.n_t, cube.count - cube.n_t
    n_win, n_grp = mask_ref.shape[0], tp
    gw = LANES
    cut, ff_cut = w1_in.shape
    heads, span = tab_in.shape
    halves = [pl.ds(h * (cut // 2), cut // 2) for h in range(2)]
    orders = gather_orders(cube)
    split = lambda ref, cols: [(ref, (rows, cols), order) for rows, order in zip(halves, orders)]
    chunks = [
        split(wq, slice(None)) + [(few, (slice(None), slice(None)), orders[0])],
        split(full_ref, pl.ds(0, W_ONE + ff_cut)),
        split(full_ref, pl.ds(W_ONE + ff_cut, ff_cut)),
    ]
    gather = Gather(cube, chunks, send, recv)
    order = gather.plan()
    ready = order.index((0, n)) + 1
    keep = pltpu.make_async_copy(wq, wq_out, local.at[1])

    @pl.when(step == 0)
    def _():
        pack[:, :W_ONE] = wp_in[...]
        pack[:, W_ONE : W_ONE + ff_cut] = w1_in[...]
        pack[:, W_ONE + ff_cut :] = w2_in[...]
        own = pltpu.make_async_copy(pack, full_ref.at[cube.at(())], local.at[0])
        own.start()
        here = cube.at(())
        few[here] = jnp.zeros((SMALL, 2 * gw), BF16)
        for i, ref in enumerate(vectors):
            few[here + (slice(i, i + 1), slice(0, cut))] = ref[...]
        for k in range(3):
            wq[here + (slice(None), slice(k * gw, (k + 1) * gw))] = wq_in[k]
            few[here + (slice(6 + k, 7 + k), slice(0, gw))] = bq_in[k : k + 1]
        for k in range(ff_cut // gw):
            few[here + (slice(9 + k, 10 + k), slice(0, gw))] = b1_in[0:1, k * gw : (k + 1) * gw]
        few[here + (slice(0, heads), slice(gw, 2 * gw))] = tab_in[:, :gw]
        few[here + (slice(heads, 2 * heads), slice(gw, span))] = tab_in[:, gw:]
        greet(cube, range(n))
        own.wait()
        for c, s in order[:ready]:
            gather.advance(c, s)
        keep.start()
        vec_ref[...] = jnp.zeros_like(vec_ref)
        for f in range(fsdp):
            part = few[(0,) * n_t + digits_of(f, n_f)].astype(F32)
            vec_ref[0:6, f * cut : (f + 1) * cut] = part[0:6, :cut]
        for t in range(tp):
            part = few[digits_of(t, n_t) + (0,) * n_f].astype(F32)
            for k in range(3):
                at = (3 * t + k) * gw
                bq[0:1, at : at + gw] = part[6 + k : 7 + k, :gw]
            for k in range(ff_cut // gw):
                b1_ref[k : k + 1, t * gw : (t + 1) * gw] = part[9 + k : 10 + k, :gw]
            tab[t * heads : (t + 1) * heads, :gw] = part[0:heads, gw:]
            tab[t * heads : (t + 1) * heads, gw:] = part[heads : 2 * heads, gw:]
        table_rows = tab[...].astype(BF16)
        wide = 8 * ROWS
        for k in range(ROWS * ROWS // wide):
            entry = lax.broadcasted_iota(jnp.int32, (2 * gw, wide), 0)
            hot = (entry == rel_ref[0:1, k * wide : (k + 1) * wide]).astype(F32).astype(BF16)
            value = dot(table_rows, hot)
            for j in range(8):
                table[:, k * 8 + j, :] = value[:, j * ROWS : (j + 1) * ROWS]
        for g in range(n_grp):
            full = jnp.concatenate([table[g * GROUP + h] for h in range(GROUP)], axis=1)
            for w in range(n_win):
                bias_scr[g, w] = full + mask_ref[w]

    rest = order[ready:]
    for i, (c, s) in enumerate(rest):
        at = PASSES[min(i, len(PASSES) - 1)]

        @pl.when(step == jnp.minimum(at, steps - 1))
        def _(c=c, s=s):
            gather.advance(c, s)

    @pl.when(step == steps - 1)
    def _():
        keep.wait()

    x = img_ref[0].astype(F32)
    xhat, _ = standardize(x)
    normed = (xhat * vec_ref[0:1] + vec_ref[1:2]).astype(BF16)
    xp = dot(perm_ref[...], normed).astype(BF16)
    mb, mf = head_masks(BF16), head_masks(F32)
    for g in range(n_grp):
        c0 = g * 3 * gw
        weight = wq[digits_of(g, n_t)].reshape(fsdp * cut, 3 * gw)
        acc = dot(xp, weight) + bq[0:1, c0 : c0 + 3 * gw]
        qkv_ref[0, :, c0 : c0 + gw] = (acc[:, :gw] * (HD ** -0.5)).astype(BF16)
        qkv_ref[0, :, c0 + gw : c0 + 3 * gw] = acc[:, gw:].astype(BF16)

    def part(g, w, j):
        return qkv_ref[0, w * ROWS : (w + 1) * ROWS, (3 * g + j) * gw : (3 * g + j + 1) * gw]

    def score(g, w):
        return dot(part(g, w, 1), spread(part(g, w, 0), mb), NT) + bias_scr[g, w]

    def store(g, w, o):
        o_scr[w * ROWS : (w + 1) * ROWS, g * gw : (g + 1) * gw] = gather_heads(o, mf).astype(BF16)

    units = [(g, w) for g in range(n_grp) for w in range(n_win)]
    ahead, behind = score(*units[0]), None
    for at, (g, w) in enumerate(units):
        s = ahead
        if at + 1 < len(units):
            ahead = score(*units[at + 1])
        e = jnp.exp(s - jnp.max(s, axis=0, keepdims=True))
        p = (e * (1.0 / jnp.sum(e, axis=0, keepdims=True))).astype(BF16)
        p_ref[0, g, w] = p
        o = dot(p, part(g, w, 2), TN)
        if behind is not None:
            store(*behind)
        behind = (g, w, o)
    store(*behind)
    mix_ref[0] = dot(permt_ref[...], o_scr[...]).astype(BF16)


def front(vectors, b_qkv, b_one, table, w_qkv, w_proj, w_one, w_two, images, consts, fsdp, tp):
    rel, mask, perm, permt = consts
    n_img, t, c = images.shape
    cut, ff_cut = w_one.shape
    gw = LANES
    n_win = mask.shape[0]
    rows, cols = n_win * ROWS, W_ONE + 2 * ff_cut
    heads = tp * table.shape[0]
    n_t, n_f = len(bits_of(tp)), len(bits_of(fsdp))
    n = n_t + n_f
    n_sem = 7 * n
    once = lambda a: pl.BlockSpec(a.shape, lambda i: (0,) * a.ndim, pipeline_mode=pl.Buffered(1))
    whole = lambda s: pl.BlockSpec(s, lambda i: (0,) * len(s))
    small = tuple(vectors) + (b_qkv, b_one, table, w_qkv, w_proj, w_one, w_two)
    return pl.pallas_call(
        functools.partial(front_kernel, fsdp=fsdp, tp=tp),
        grid=(n_img,),
        in_specs=[once(a) for a in small]
        + [pl.BlockSpec((1, t, c), lambda i: (i, 0, 0))]
        + [once(a) for a in (rel, mask, perm, permt)],
        out_specs=[
            pl.BlockSpec(memory_space=pl.ANY),
            pl.BlockSpec(memory_space=pl.ANY),
            pl.BlockSpec((1, rows, 3 * tp * gw), lambda i: (i, 0, 0)),
            pl.BlockSpec((1, tp, n_win, ROWS, GROUP * ROWS), lambda i: (i, 0, 0, 0, 0)),
            pl.BlockSpec((1, t, c), lambda i: (i, 0, 0)),
            whole((8, c)),
            whole((ff_cut // gw, tp * gw)),
        ],
        out_shape=[
            jax.ShapeDtypeStruct((2,) * n + (cut, cols), BF16),
            jax.ShapeDtypeStruct((2,) * n + (cut, 3 * gw), BF16),
            jax.ShapeDtypeStruct((n_img, rows, 3 * tp * gw), BF16),
            jax.ShapeDtypeStruct((n_img, tp, n_win, ROWS, GROUP * ROWS), BF16),
            jax.ShapeDtypeStruct((n_img, t, c), BF16),
            jax.ShapeDtypeStruct((8, c), F32),
            jax.ShapeDtypeStruct((ff_cut // gw, tp * gw), F32),
        ],
        scratch_shapes=[
            pltpu.VMEM((cut, cols), BF16),
            pltpu.VMEM((2,) * n + (cut, 3 * gw), BF16),
            pltpu.VMEM((2,) * n + (SMALL, 2 * gw), BF16),
            pltpu.VMEM((1, 3 * tp * gw), F32),
            pltpu.VMEM((heads, 2 * gw), F32),
            pltpu.VMEM((heads, ROWS, ROWS), F32),
            pltpu.VMEM((tp, n_win, ROWS, GROUP * ROWS), F32),
            pltpu.VMEM((rows, c), BF16),
            pltpu.SemaphoreType.DMA((2,)),
            pltpu.SemaphoreType.DMA((n_sem,)),
            pltpu.SemaphoreType.DMA((n_sem,)),
        ],
        compiler_params=pltpu.CompilerParams(
            vmem_limit_bytes=60 << 20, collective_id=1, has_side_effects=True
        ),
        name="front",
    )(*small, images, rel, mask, perm, permt)


SQRT_HALF = float(np.sqrt(0.5))
INV_SQRT_2PI = float(1.0 / np.sqrt(2.0 * np.pi))


class Spread:
    def __init__(self, cube, full, send, recv):
        self.cube, self.full, self.send, self.recv = cube, full, send, recv
        self.stages = cube.n_t

    def ref(self, s, i):
        own = self.cube.own
        return self.full.at[tuple(slice(None) if k < s else own[k] for k in range(self.stages)) + (i,)]

    def copy(self, s, i):
        ref = self.ref(s, i)
        return pltpu.make_async_remote_copy(
            ref, ref, self.send.at[s, i], self.recv.at[s, i], device_id=self.cube.partner(s), device_id_type=MESH
        )


def blocks_of(n, body):
    if n == 0:
        body(())
        return

    def one(i, carry):
        body(tuple(lax.rem(lax.div(i, 2 ** (n - 1 - k)), 2) for k in range(n)))
        return carry

    lax.fori_loop(0, 2**n, one, 0)


class Reduce:
    def __init__(self, cube, acc, order, bufs, send, recv, n_digits, out):
        self.cube, self.acc, self.order, self.bufs = cube, acc, order, bufs
        self.send, self.recv, self.n_digits, self.out = send, recv, n_digits, out
        self.stages = len(order)

    def at(self, free, flip=None):
        own = self.cube.own
        return tuple(
            slice(None) if k in free else (1 - own[k] if k == flip else own[k]) for k in range(self.n_digits)
        )

    def left(self, s):
        return sorted(k for k in self.order[s + 1 :] if k < self.n_digits)

    def copy(self, s):
        return pltpu.make_async_remote_copy(
            self.acc.at[self.at(self.left(s), self.order[s])],
            self.bufs[s],
            self.send.at[s],
            self.recv.at[s],
            device_id=self.cube.partner(self.order[s]),
            device_id_type=MESH,
        )

    def start(self):
        self.copy(0).start()

    def advance(self, s):
        self.copy(s).wait()
        free = self.left(s)
        own = self.cube.own

        def add(index):
            at = dict(zip(free, index))
            dst = tuple(at.get(k, own[k]) for k in range(self.n_digits))
            if s + 1 == self.stages:
                self.out(self.acc[dst].astype(F32) + self.bufs[s][index].astype(F32))
            else:
                self.acc[dst] = self.acc[dst] + self.bufs[s][index]

        blocks_of(len(free), add)
        if s + 1 < self.stages:
            self.copy(s + 1).start()


def reduce_orders(n_t, n):
    t, f = list(range(n_t)), list(range(n_t, n))
    t_in, f_in = t[1:][::-1], f[::-1]
    early = (t_in + f_in + t[:1], t_in + f[:-1][::-1] + f[-1:] + t[:1])
    late = (t_in + f[-1:] + t[:1] + f[:-1][::-1], t_in + t[:1] + f_in)
    return early, late, t[::-1] + f_in


def layer_kernel(live_ref, img_hbm, cot_hbm, mix_ref, w_hbm, wq_hbm, vec_ref, b1_ref, qkv_ref, p_ref, perm_ref, permt_ref,
                 out_ref, gin_ref, dqkv_ref, dw1_ref, dw2_ref, dwp_ref, small_ref,
                 img_ref, cot_ref, w1_ref, w2_ref, wq_ref, wp, act, slope, normed_two, up_scr, gres_scr,
                 db1, dvec, dqkv_scr, dw, db, dtab, res_scr, acc, acc_p, late_a, late_b, small, *rest,
                 fsdp, tp, per, n_q):
    step = pl.program_id(0)
    cube = Cube(fsdp, tp)
    n, n_t, n_f = cube.count, cube.n_t, cube.count - cube.n_t
    n_img, n_tok, c = img_ref.shape
    n_grp, n_win = p_ref.shape[1:3]
    gw = LANES
    cut = c // fsdp
    fwd_steps = n_img // per
    bwd_at = fwd_steps
    att_at = bwd_at + n_q
    last_step = att_at + n_img - 1

    early, late, both = reduce_orders(n_t, n)
    bufs, rest = rest[: 5 * n], rest[5 * n :]
    load, local, send, recv, local_in, send_in, recv_in, rs_send, rs_recv = rest

    wide_q = n_q * gw
    loads = [
        pltpu.make_async_copy(w_hbm.at[:, :, pl.ds(W_ONE, wide_q)], w1_ref, load.at[0]),
        pltpu.make_async_copy(w_hbm.at[:, :, pl.ds(W_ONE + wide_q, wide_q)], w2_ref, load.at[1]),
        pltpu.make_async_copy(img_hbm, img_ref, load.at[2]),
        pltpu.make_async_copy(cot_hbm, cot_ref, load.at[3]),
    ]
    loads += [
        pltpu.make_async_copy(w_hbm.at[g, :, pl.ds(0, gw)], wp.at[:, pl.ds(g * gw, gw)], load.at[5 + g])
        for g in range(n_grp)
    ]
    load_wq = pltpu.make_async_copy(wq_hbm, wq_ref, load.at[4])
    gmix_scr = cot_ref

    def result_of(q):
        def out(total):
            dw1_ref[:, q * gw : (q + 1) * gw] = total[:, :gw]
            dw2_ref[:, q * gw : (q + 1) * gw] = total[:, gw:]

        return out

    def result_p(total):
        dwp_ref[...] = total

    def result_a(total):
        dqkv_ref[: cut // 2] = total

    def result_b(total):
        dqkv_ref[cut // 2 :] = total

    def result_s(total):
        small_ref[...] = total

    plans = [
        (acc.at[q], [ref.at[q] for ref in bufs[:n]], early[q % 2], n, result_of(q)) for q in range(n_q)
    ]
    plans += [
        (acc_p, bufs[n : 2 * n], early[0], n, result_p),
        (late_a, bufs[2 * n : 3 * n], late[0], n, result_a),
        (late_b, bufs[3 * n : 4 * n], late[1], n, result_b),
        (small, bufs[4 * n :], both, n_t, result_s),
    ]
    reduces = [
        Reduce(cube, ref, order, buf, rs_send.at[k], rs_recv.at[k], d, out)
        for k, (ref, buf, order, d, out) in enumerate(plans)
    ]
    n_early = n_q + 1
    spread_out = Spread(cube, out_ref, send, recv)
    spread_in = Spread(cube, gin_ref, send_in, recv_in)

    def keep_out(i):
        return pltpu.make_async_copy(res_scr.at[pl.ds(i * per, per)], spread_out.ref(0, i), local.at[i])

    def keep_in(i):
        return pltpu.make_async_copy(res_scr.at[i], spread_in.ref(0, i), local_in.at[i])

    events = {}

    def plan(at, work):
        events.setdefault(at, []).append(work)

    def point(k):
        for at in sorted(events):
            if at[1] == k:

                @pl.when(step == at[0])
                def _(at=at):
                    for work in events[at]:
                        work()

    def send_out(i):
        keep_out(i).wait()
        spread_out.copy(0, i).start()

    def pass_out(i, s):
        spread_out.copy(s - 1, i).wait()
        spread_out.copy(s, i).start()

    def send_in_(i):
        keep_in(i).wait()
        spread_in.copy(0, i).start()

    def pass_in(i, s):
        spread_in.copy(s - 1, i).wait()
        spread_in.copy(s, i).start()

    for i in range(fwd_steps):
        plan((i + 1, 0), functools.partial(send_out, i))
    later = [att_at - 1 + 3 * i for i in range(fwd_steps)]
    for s in range(1, n_t):
        for i in range(fwd_steps):
            plan((min(later[i] + s - 1, last_step), 0), functools.partial(pass_out, i, s))
    for i in range(n_img - 1):
        plan((att_at + i + 1, 0), functools.partial(send_in_, i))
    tail = []
    for i in range(n_img):
        for s in range(1, n_t):
            at = att_at + i + 3 + s
            if at <= last_step:
                plan((at, 0), functools.partial(pass_in, i, s))
            else:
                tail.append(functools.partial(pass_in, i, s))
    ends = []
    for k in range(n_early):
        begin = (bwd_at + k + 1, 1) if k + 1 < n_q else (att_at, 0)
        plan(begin, reduces[k].start)
        slots = SLOTS[k] if k < len(SLOTS) else ()
        for s in range(n):
            work = functools.partial(reduces[k].advance, s)
            if s < len(slots):
                plan((bwd_at + slots[s][0], slots[s][1]), work)
            else:
                ends.append(work)

    @pl.when(step == 0)
    def _():
        for ld in loads + [load_wq]:
            ld.start()
        greet(cube, range(n))
        dw[...] = jnp.zeros_like(dw)
        dvec[...] = jnp.zeros_like(dvec)
        db[...] = jnp.zeros_like(db)
        db1[...] = jnp.zeros_like(db1)
        dtab[...] = jnp.zeros_like(dtab)
        for ld in loads:
            ld.wait()

    def columns(ref, q):
        at = pl.ds(pl.multiple_of(q * gw, gw), gw)
        return jnp.concatenate([ref[g, :, at] for g in range(n_grp)], axis=1)

    def rows_of(ref, b):
        return jnp.concatenate([ref[b * per + i] for i in range(per)], axis=0)

    def middle(b):
        mixed = rows_of(mix_ref, b)
        res = rows_of(img_ref, b).astype(F32) + (dot(mixed, wp[...], NT) + vec_ref[2:3])
        return (mixed, res) + standardize(res)

    @pl.when(step < bwd_at)
    def _():
        point(0)
        live = jnp.concatenate(
            [jnp.full((n_tok, 1), 1.0, F32) * live_ref[step * per + i] for i in range(per)], axis=0
        )
        up = rows_of(cot_ref, step).astype(F32) * live
        up_scr[step] = up.astype(BF16)
        dvec[5:6] += jnp.sum(up, axis=0, keepdims=True)
        mixed, res, xhat, _ = middle(step)
        normed_two[step] = (xhat * vec_ref[3:4] + vec_ref[4:5]).astype(BF16)

        def hidden_part(q, branch):
            hid = dot(normed_two[step], columns(w1_ref, q)) + b1_ref[pl.ds(q, 1)]
            cdf = 0.5 * (1.0 + lax.erf(hid * SQRT_HALF))
            a = (hid * cdf).astype(BF16)
            act[step, q] = a
            slope[step, q] = (cdf + hid * (jnp.exp(-0.5 * hid * hid) * INV_SQRT_2PI)).astype(BF16)
            return branch + dot(a, columns(w2_ref, q), NT)

        total = lax.fori_loop(0, n_q, hidden_part, res + vec_ref[5:6])
        out = (live * total).astype(BF16)
        for i in range(per):
            res_scr[step * per + i] = out[i * n_tok : (i + 1) * n_tok]
        keep_out(step).start()

    @pl.when(jnp.logical_and(step >= bwd_at, step < att_at))
    def _():
        q = step - bwd_at
        point(0)
        w2 = columns(w2_ref, q)
        d_one = d_two = None
        for b in range(fwd_steps):
            if b == 1:
                point(1)
            up = up_scr[b]
            dh = (dot(up, w2) * slope[b, q].astype(F32)).astype(BF16)
            slope[b, q] = dh
            db1[pl.ds(q, 1)] += jnp.sum(dh.astype(F32), axis=0, keepdims=True)
            one, two = dot(normed_two[b], dh, TN), dot(up, act[b, q], TN)
            d_one, d_two = (one, two) if b == 0 else (d_one + one, d_two + two)
        for t in range(n_grp):
            block = (2,) * n_f + (cut, gw)
            at = (q,) + digits_of(t, n_t) + (slice(None),) * (n_f + 1)
            l = slice(t * gw, (t + 1) * gw)
            acc[at + (slice(0, gw),)] = d_one[:, l].astype(BF16).reshape(block)
            acc[at + (slice(gw, 2 * gw),)] = d_two[:, l].astype(BF16).reshape(block)

    @pl.when(step == att_at - 1)
    def _():
        point(2)

        def back(b, d_proj):
            dn = dot(slope[b, 0], columns(w1_ref, 0), NT)
            for k in range(1, n_q):
                dn = dn + dot(slope[b, k], columns(w1_ref, k), NT)
            mixed, _, xhat, inv = middle(b)
            d = dn * vec_ref[3:4]
            gres = up_scr[b].astype(F32) + inv * (
                d - jnp.mean(d, axis=-1, keepdims=True) - xhat * jnp.mean(d * xhat, axis=-1, keepdims=True)
            )
            gatt = gres.astype(BF16)
            gmix = dot(gatt, wp[...]).astype(BF16)
            for i in range(per):
                r = slice(i * n_tok, (i + 1) * n_tok)
                gres_scr[b * per + i] = gres[r]
                gmix_scr[b * per + i] = gmix[r]
            dvec[2:3] += jnp.sum(gatt.astype(F32), axis=0, keepdims=True)
            dvec[3:4] += jnp.sum(dn * xhat, axis=0, keepdims=True)
            dvec[4:5] += jnp.sum(dn, axis=0, keepdims=True)
            return d_proj + dot(gatt, mixed, TN)

        d_proj = lax.fori_loop(0, fwd_steps, back, jnp.zeros((c, c), F32))
        for t in range(n_grp):
            acc_p[digits_of(t, n_t)] = (
                d_proj[:, t * gw : (t + 1) * gw].astype(BF16).reshape((2,) * n_f + (cut, gw))
            )

    @pl.when(step == att_at)
    def _():
        load_wq.wait()

    @pl.when(step >= att_at)
    def _():
        j = step - att_at
        mb, mf = head_masks(BF16), head_masks(F32)
        point(0)
        x = img_ref[j].astype(F32)
        xhat, inv = standardize(x)
        normed = (xhat * vec_ref[0:1] + vec_ref[1:2]).astype(BF16)
        xp = dot(perm_ref[...], normed).astype(BF16)
        gm = dot(perm_ref[...], gmix_scr[j]).astype(BF16)
        dn = jnp.zeros((n_win * ROWS, c), F32)
        for g in range(n_grp):
            if g > 0:
                point(g)
            c0 = g * 3 * gw
            tab = jnp.zeros((ROWS, GROUP * ROWS), F32)
            cuts = [slice(w * ROWS, (w + 1) * ROWS) for w in range(n_win)]
            dos = [spread(gm[r, g * gw : (g + 1) * gw], mb) for r in cuts]
            dps = [dot(qkv_ref[0, r, c0 + 2 * gw : c0 + 3 * gw], do, NT) for r, do in zip(cuts, dos)]
            ps = [p_ref[0, g, w] for w in range(n_win)]
            dvs = [dot(p, do) for p, do in zip(ps, dos)]
            dss = []
            for p, dp in zip(ps, dps):
                pf = p.astype(F32)
                ds = pf * (dp - jnp.sum(pf * dp, axis=0, keepdims=True))
                tab = tab + ds
                dss.append(ds.astype(BF16))
            dks = [dot(ds, spread(qkv_ref[0, r, c0 : c0 + gw], mb)) for r, ds in zip(cuts, dss)]
            dqs = [dot(ds, qkv_ref[0, r, c0 + gw : c0 + 2 * gw], TN) for r, ds in zip(cuts, dss)]
            for r, dq, dk, dv in zip(cuts, dqs, dks, dvs):
                dqkv_scr[r, :gw] = (gather_heads(dq, mf) * (HD ** -0.5)).astype(BF16)
                dqkv_scr[r, gw : 2 * gw] = dk.astype(BF16)
                dqkv_scr[r, 2 * gw :] = dv.astype(BF16)
            dtab[g] += tab
            dqkv = dqkv_scr[...]
            db[0:1, c0 : c0 + 3 * gw] += jnp.sum(dqkv.astype(F32), axis=0, keepdims=True)
            dw[g] += dot(xp, dqkv, TN)
            dn = dn + dot(dqkv, wq_ref[g], NT)
        hi = dn.astype(BF16)
        lo = (dn - hi.astype(F32)).astype(BF16)
        dn = dot(permt_ref[...], hi) + dot(permt_ref[...], lo)
        d = dn * vec_ref[0:1]
        gin = inv * (
            d - jnp.mean(d, axis=-1, keepdims=True) - xhat * jnp.mean(d * xhat, axis=-1, keepdims=True)
        )
        res_scr[j] = (gres_scr[j] + gin).astype(BF16)
        keep_in(j).start()
        dvec[0:1] += jnp.sum(dn * xhat, axis=0, keepdims=True)
        dvec[1:2] += jnp.sum(dn, axis=0, keepdims=True)

    @pl.when(step == last_step)
    def _():
        for g in range(n_grp):
            value = dw[g].astype(BF16).reshape((2,) * n_f + (cut, 3 * gw))
            late_a[digits_of(g, n_t)] = value[..., : cut // 2, :]
            late_b[digits_of(g, n_t)] = value[..., cut // 2 :, :]
        for red in reduces[n_early : n_early + 2]:
            red.start()
        wide = GROUP * ROWS
        for g in range(n_grp):
            panel = small.at[digits_of(g, n_t)]
            panel[:ROWS] = dtab[g]
            c0 = g * 3 * gw
            panel[ROWS : ROWS + 1] = db[0:1, c0 : c0 + wide]
            panel[ROWS + 1 : ROWS + 2] = jnp.concatenate(
                [db[0:1, c0 + wide : c0 + 3 * gw], jnp.zeros((1, 2 * wide - 3 * gw), F32)], axis=1
            )
            r = ROWS + 2
            for q in range(0, n_q, 2):
                pair = [db1[q + k : q + k + 1, g * gw : (g + 1) * gw] for k in range(2)]
                panel[r : r + 1] = jnp.concatenate(pair, axis=1)
                r = r + 1
            for i in range(6):
                for k in range(c // wide):
                    panel[r : r + 1] = dvec[i : i + 1, k * wide : (k + 1) * wide]
                    r = r + 1
        reduces[n_early + 2].start()
        send_in_(n_img - 1)
        for s in range(n):
            for red in reduces[n_early:]:
                red.advance(s)
            if s == TAIL_AT:
                for work in tail:
                    work()
        for work in ends:
            work()
        for i in range(fwd_steps):
            spread_out.copy(n_t - 1, i).wait()
        for i in range(n_img):
            spread_in.copy(n_t - 1, i).wait()


SLOTS = (
    ((3, 0), (4, 2), (6, 0), (8, 0), (10, 0)),
    ((4, 0), (6, 0), (8, 0), (10, 0)),
    ((5, 0), (7, 0), (9, 0), (11, 0)),
    ((6, 0), (8, 2), (10, 2), (11, 3)),
    ((6, 0), (8, 2), (10, 2), (11, 3)),
)
TAIL_AT = 2


def layer(live, images, out_grad, mixed, w_all, w_qkv, vecs, b1, qkv, p, perm, permt, fsdp, tp, per=4):
    n_img, t, c = mixed.shape
    rows, cols = qkv.shape[1:]
    n_grp, n_win = p.shape[1:3]
    gw, wide = LANES, GROUP * ROWS
    n_q = b1.shape[0]
    ff_cut = n_q * gw
    cut = c // fsdp
    n_t, n_f = len(bits_of(tp)), len(bits_of(fsdp))
    n = n_t + n_f
    digits = (2,) * n
    n_small = ROWS + 2 + ff_cut // wide + 6 * (c // wide)
    fwd_steps = n_img // per
    att_at = fwd_steps + n_q
    bufs = []
    for lead, block in (
        ((n_q,), (cut, 2 * gw)),
        ((), (cut, gw)),
        ((), (cut // 2, 3 * gw)),
        ((), (cut // 2, 3 * gw)),
    ):
        bufs += [pltpu.VMEM(lead + (2,) * (n - 1 - s) + block, BF16) for s in range(n)]
    both = reduce_orders(n_t, n)[2]
    for s in range(n):
        left = sum(k < n_t for k in both[s + 1 :])
        bufs.append(pltpu.VMEM((2,) * left + (n_small, wide), F32))
    whole = lambda s: pl.BlockSpec(s, lambda i: (0,) * len(s))
    once = lambda s: pl.BlockSpec(s, lambda i: (0,) * len(s), pipeline_mode=pl.Buffered(1))
    image = lambda i: jnp.clip(i - att_at, 0, n_img - 1)
    any_spec = pl.BlockSpec(memory_space=pl.ANY)
    hidden = (fwd_steps, n_q, per * t, n_grp * gw)
    return pl.pallas_call(
        functools.partial(layer_kernel, fsdp=fsdp, tp=tp, per=per, n_q=n_q),
        grid=(att_at + n_img,),
        in_specs=[
            pl.BlockSpec(memory_space=pltpu.SMEM),
            any_spec,
            any_spec,
            once(mixed.shape),
            any_spec,
            any_spec,
            once(vecs.shape),
            once(b1.shape),
            pl.BlockSpec((1, rows, cols), lambda i: (image(i), 0, 0)),
            pl.BlockSpec((1,) + p.shape[1:], lambda i: (image(i), 0, 0, 0, 0)),
            once(perm.shape),
            once(permt.shape),
        ],
        out_specs=[any_spec, any_spec]
        + [whole(s) for s in ((cut, 3 * gw), (cut, ff_cut), (cut, ff_cut), (cut, gw), (n_small, wide))],
        out_shape=[
            jax.ShapeDtypeStruct((2,) * n_t + (fwd_steps, per, t, c), BF16),
            jax.ShapeDtypeStruct((2,) * n_t + (n_img, t, c), BF16),
            jax.ShapeDtypeStruct((cut, 3 * gw), F32),
            jax.ShapeDtypeStruct((cut, ff_cut), F32),
            jax.ShapeDtypeStruct((cut, ff_cut), F32),
            jax.ShapeDtypeStruct((cut, gw), F32),
            jax.ShapeDtypeStruct((n_small, wide), F32),
        ],
        scratch_shapes=[
            pltpu.VMEM((n_img, t, c), BF16),
            pltpu.VMEM((n_img, t, c), BF16),
            pltpu.VMEM((n_grp, c, ff_cut), BF16),
            pltpu.VMEM((n_grp, c, ff_cut), BF16),
            pltpu.VMEM((n_grp, c, 3 * gw), BF16),
            pltpu.VMEM((c, c), BF16),
            pltpu.VMEM(hidden, BF16),
            pltpu.VMEM(hidden, BF16),
            pltpu.VMEM((fwd_steps, per * t, c), BF16),
            pltpu.VMEM((fwd_steps, per * t, c), BF16),
            pltpu.VMEM((n_img, t, c), F32),
            pltpu.VMEM((8, n_grp * gw), F32),
            pltpu.VMEM((8, c), F32),
            pltpu.VMEM((rows, 3 * gw), BF16),
            pltpu.VMEM((n_grp, c, 3 * gw), F32),
            pltpu.VMEM((1, cols), F32),
            pltpu.VMEM((n_grp, ROWS, wide), F32),
            pltpu.VMEM((n_img, t, c), BF16),
            pltpu.VMEM((n_q,) + digits + (cut, 2 * gw), BF16),
            pltpu.VMEM(digits + (cut, gw), BF16),
            pltpu.VMEM(digits + (cut // 2, 3 * gw), BF16),
            pltpu.VMEM(digits + (cut // 2, 3 * gw), BF16),
            pltpu.VMEM((2,) * n_t + (n_small, wide), F32),
            *bufs,
            pltpu.SemaphoreType.DMA((5 + n_grp,)),
            pltpu.SemaphoreType.DMA((fwd_steps,)),
            pltpu.SemaphoreType.DMA((n_t, fwd_steps)),
            pltpu.SemaphoreType.DMA((n_t, fwd_steps)),
            pltpu.SemaphoreType.DMA((n_img,)),
            pltpu.SemaphoreType.DMA((n_t, n_img)),
            pltpu.SemaphoreType.DMA((n_t, n_img)),
            pltpu.SemaphoreType.DMA((n_q + 4, n)),
            pltpu.SemaphoreType.DMA((n_q + 4, n)),
        ],
        compiler_params=pltpu.CompilerParams(
            vmem_limit_bytes=60 << 20, collective_id=2, has_side_effects=True
        ),
        name="layer",
    )(live, images, out_grad, mixed, w_all, w_qkv, vecs, b1, qkv, p, perm, permt)


def per_device(
    images,
    attn_norm_gain,
    attn_norm_bias,
    qkv_weight,
    qkv_bias,
    position_table,
    proj_weight,
    proj_bias,
    mlp_norm_gain,
    mlp_norm_bias,
    fc1_weight,
    fc1_bias,
    fc2_weight,
    fc2_bias,
    image_count,
    out_grad,
    *,
    fsdp,
    tp,
):
    index, mask, perm = window_constants()
    span = position_table.shape[0]
    gw = LANES
    cut = qkv_weight.shape[0]
    width = cut * fsdp
    ff_cut = fc1_bias.shape[0]
    n_qkv = qkv_bias.size
    mine = images.shape[0] // tp
    first = lax.axis_index("tp") * mine
    img = lax.dynamic_slice_in_dim(images, first, mine, 0)
    cot = lax.dynamic_slice_in_dim(out_grad, first, mine, 0)
    live = (first + jnp.arange(mine, dtype=jnp.int32) < image_count[0]).astype(F32)
    perm16 = jnp.asarray(perm).astype(BF16)
    consts = (jnp.asarray(index).reshape(1, -1), jnp.asarray(mask), perm16, perm16.T)
    vectors = (attn_norm_gain, attn_norm_bias, proj_bias, mlp_norm_gain, mlp_norm_bias, fc2_bias)
    w_all, w_qkv, qkv, probs, mixed, vecs, b_one = front(
        [v.reshape(1, cut) for v in vectors],
        qkv_bias,
        fc1_bias.reshape(1, ff_cut),
        position_table.T,
        qkv_weight.transpose(1, 0, 2),
        proj_weight.T,
        fc1_weight,
        fc2_weight.T,
        img,
        consts,
        fsdp,
        tp,
    )
    w_all = w_all.reshape(tp, width, w_all.shape[-1])
    w_qkv = w_qkv.reshape(tp, width, 3 * gw)
    output, images_grad, d_qkv, d_one, d_two, d_proj, small = layer(
        live, img, cot, mixed, w_all, w_qkv, vecs, b_one, qkv, probs, consts[2], consts[3], fsdp, tp
    )
    wide = GROUP * ROWS
    hot = (jnp.asarray(index)[None] == jnp.arange(span, dtype=jnp.int32)[:, None, None]).astype(F32)
    d_tab = jnp.einsum(
        "jhi,rji->rh",
        small[:ROWS].reshape(ROWS, GROUP, ROWS),
        hot,
        precision=lax.Precision.HIGHEST,
    )
    at = ROWS + 2
    dqkv_bias = small[ROWS:at].reshape(-1)[:n_qkv].reshape(qkv_bias.shape)
    dfc1_bias = small[at : at + ff_cut // wide].reshape(-1)
    dvec = small[at + ff_cut // wide :].reshape(6, width)
    dvec = lax.dynamic_slice_in_dim(dvec, lax.axis_index("fsdp") * cut, cut, 1)
    return (
        output.reshape(images.shape),
        images_grad.reshape(images.shape),
        dvec[0],
        dvec[1],
        d_qkv.reshape(qkv_weight.shape),
        dqkv_bias,
        d_tab,
        d_proj.T,
        dvec[2],
        dvec[3],
        dvec[4],
        d_one,
        dfc1_bias,
        d_two.T,
        dvec[5],
    )


def solution(mesh):
    P = jax.sharding.PartitionSpec
    return jax.shard_map(
        functools.partial(per_device, fsdp=mesh.shape["fsdp"], tp=mesh.shape["tp"]),
        mesh=mesh,
        in_specs=(
            P("fsdp", None, None),
            P("fsdp"),
            P("fsdp"),
            P("fsdp", None, "tp"),
            P(None, "tp"),
            P(None, "tp"),
            P("tp", "fsdp"),
            P("fsdp"),
            P("fsdp"),
            P("fsdp"),
            P("fsdp", "tp"),
            P("tp"),
            P("tp", "fsdp"),
            P("fsdp"),
            P("fsdp"),
            P("fsdp", None, None),
        ),
        out_specs=(
            P("fsdp", None, None),
            P("fsdp", None, None),
            P("fsdp"),
            P("fsdp"),
            P("fsdp", None, "tp"),
            P(None, "tp"),
            P(None, "tp"),
            P("tp", "fsdp"),
            P("fsdp"),
            P("fsdp"),
            P("fsdp"),
            P("fsdp", "tp"),
            P("tp"),
            P("tp", "fsdp"),
            P("fsdp"),
        ),
        check_vma=False,
    )
```

```python
import functools
import jax
import jax.numpy as jnp
import numpy as np
from jax import lax
from jax.experimental import pallas as pl
from jax.experimental.pallas import tpu as pltpu

HD = 32
WIN = 7
SHIFT = 3
SIDE = 14
AREA = WIN * WIN
ROWS = 64
GROUP = 4
EPSILON = 1e-05
F32 = jnp.float32
BF16 = jnp.bfloat16
PADDED = -1e30
MESH = pl.DeviceIdType.MESH


def window_constants():
    offsets = np.arange(WIN)
    rows, cols = np.repeat(offsets, WIN), np.tile(offsets, WIN)
    relative = (rows[:, None] - rows[None, :] + WIN - 1) * (2 * WIN - 1) + (
        cols[:, None] - cols[None, :] + WIN - 1
    )
    span = (2 * WIN - 1) ** 2
    index = np.full((ROWS, ROWS), span, np.int32)
    index[:AREA, :AREA] = relative.T
    region = np.zeros((SIDE, SIDE), np.int32)
    bounds = ((0, SIDE - WIN), (SIDE - WIN, SIDE - SHIFT), (SIDE - SHIFT, SIDE))
    for a, rr in enumerate(bounds):
        for b, cc in enumerate(bounds):
            region[rr[0] : rr[1], cc[0] : cc[1]] = 3 * a + b
    across = SIDE // WIN
    cut = region.reshape(across, WIN, across, WIN).transpose(0, 2, 1, 3).reshape(across * across, AREA)
    mask = np.zeros((across * across, ROWS, ROWS), np.float32)
    mask[:, :AREA, :AREA] = np.where(cut[:, :, None] == cut[:, None, :], 0.0, -100.0)
    mask[:, AREA:, :] = PADDED
    mask = np.tile(mask, (1, 1, GROUP))
    perm = np.zeros((across * across * ROWS, SIDE * SIDE), np.float32)
    for w in range(across * across):
        for s in range(AREA):
            r = ((w // across) * WIN + s // WIN + SHIFT) % SIDE
            c = ((w % across) * WIN + s % WIN + SHIFT) % SIDE
            perm[w * ROWS + s, r * SIDE + c] = 1.0
    return index, mask, perm


def dot(a, b, dims=((1,), (0,))):
    return lax.dot_general(a, b, (dims, ((), ())), preferred_element_type=F32)


NT = ((1,), (1,))
TN = ((0,), (0,))


def standardize(x):
    c = x - jnp.mean(x, axis=-1, keepdims=True)
    inv = lax.rsqrt(jnp.mean(c * c, axis=-1, keepdims=True) + EPSILON)
    return c * inv, inv


def head_masks(dtype):
    lane = lax.broadcasted_iota(jnp.int32, (1, GROUP * HD), 1) // HD
    return [(lane == h).astype(F32).astype(dtype) for h in range(GROUP)]


def spread(x, masks):
    return jnp.concatenate([x * m for m in masks], axis=0)


def gather_heads(y, masks):
    out = y[:ROWS] * masks[0]
    for h in range(1, GROUP):
        out = out + y[h * ROWS : (h + 1) * ROWS] * masks[h]
    return out


def bits_of(n):
    return [1 << b for b in reversed(range(n.bit_length() - 1))]

class Cube:
    def __init__(self, fsdp, tp):
        self.f, self.t = lax.axis_index("fsdp"), lax.axis_index("tp")
        self.digits = [("tp", b) for b in bits_of(tp)] + [("fsdp", b) for b in bits_of(fsdp)]
        self.own = [lax.rem((self.t if a == "tp" else self.f) // b, 2) for a, b in self.digits]
        self.count = len(self.digits)
        self.n_t = len(bits_of(tp))

    def partner(self, k):
        axis, b = self.digits[k]
        step = b * (1 - 2 * self.own[k])
        if axis == "tp":
            return (self.f, self.t + step)
        return (self.f + step, self.t)

    def at(self, free, flip=None):
        out = []
        for k in range(self.count):
            if k in free:
                out.append(slice(None))
            else:
                out.append(1 - self.own[k] if k == flip else self.own[k])
        return tuple(out)


def greet(cube, digits):
    bar = pltpu.get_barrier_semaphore()
    for k in digits:
        pl.semaphore_signal(bar, inc=1, device_id=cube.partner(k), device_id_type=MESH)
    pl.semaphore_wait(bar, len(digits))


def gather_orders(cube):
    t, f = list(range(cube.n_t)), list(range(cube.n_t, cube.count))
    return (f + t, f[:-1] + t[:-1] + f[-1:] + t[-1:])


class Gather:
    def __init__(self, cube, chunks, send, recv):
        self.cube, self.chunks, self.send, self.recv = cube, chunks, send, recv
        self.lanes = [sum(len(k) for k in chunks[:c]) for c in range(len(chunks))]

    def copies(self, c, s):
        for h, (ref, part, order) in enumerate(self.chunks[c]):
            ref = ref.at[self.cube.at(order[:s]) + part]
            i = (self.lanes[c] + h) * self.cube.count + s
            yield pltpu.make_async_remote_copy(
                ref,
                ref,
                self.send.at[i],
                self.recv.at[i],
                device_id=self.cube.partner(order[s]),
                device_id_type=MESH,
            )

    def plan(self):
        n = self.cube.count
        events = ((c, s) for c in range(len(self.chunks)) for s in range(n + 1))
        return sorted(events, key=lambda e: (LAGS[e[0]] + e[1], e[0]))

    def advance(self, c, s):
        if s > 0:
            for copy in self.copies(c, s - 1):
                copy.wait()
        if s < self.cube.count:
            for copy in self.copies(c, s):
                copy.start()


LAGS = (0, 1, 2)


LANES = GROUP * HD
SMALL = 16
PASSES = (3, 3, 5, 5, 7)
W_ONE = LANES


def digits_of(value, n):
    return tuple((value >> (n - 1 - k)) & 1 for k in range(n))


def front_kernel(*refs, fsdp, tp):
    vectors, refs = refs[:6], refs[6:]
    (bq_in, b1_in, tab_in, wq_in, wp_in, w1_in, w2_in, img_ref, rel_ref, mask_ref, perm_ref, permt_ref,
     full_ref, wq_out, qkv_ref, p_ref, mix_ref, vec_ref, b1_ref,
     pack, wq, few, bq, tab, table, bias_scr, o_scr, local, send, recv) = refs
    step, steps = pl.program_id(0), pl.num_programs(0)
    cube = Cube(fsdp, tp)
    n, n_t, n_f = cube.count, cube.n_t, cube.count - cube.n_t
    n_win, n_grp = mask_ref.shape[0], tp
    gw = LANES
    cut, ff_cut = w1_in.shape
    heads, span = tab_in.shape
    halves = [pl.ds(h * (cut // 2), cut // 2) for h in range(2)]
    orders = gather_orders(cube)
    split = lambda ref, cols: [(ref, (rows, cols), order) for rows, order in zip(halves, orders)]
    chunks = [
        split(wq, slice(None)) + [(few, (slice(None), slice(None)), orders[0])],
        split(full_ref, pl.ds(0, W_ONE + ff_cut)),
        split(full_ref, pl.ds(W_ONE + ff_cut, ff_cut)),
    ]
    gather = Gather(cube, chunks, send, recv)
    order = gather.plan()
    ready = order.index((0, n)) + 1
    keep = pltpu.make_async_copy(wq, wq_out, local.at[1])

    @pl.when(step == 0)
    def _():
        pack[:, :W_ONE] = wp_in[...]
        pack[:, W_ONE : W_ONE + ff_cut] = w1_in[...]
        pack[:, W_ONE + ff_cut :] = w2_in[...]
        own = pltpu.make_async_copy(pack, full_ref.at[cube.at(())], local.at[0])
        own.start()
        here = cube.at(())
        few[here] = jnp.zeros((SMALL, 2 * gw), BF16)
        for i, ref in enumerate(vectors):
            few[here + (slice(i, i + 1), slice(0, cut))] = ref[...]
        for k in range(3):
            wq[here + (slice(None), slice(k * gw, (k + 1) * gw))] = wq_in[k]
            few[here + (slice(6 + k, 7 + k), slice(0, gw))] = bq_in[k : k + 1]
        for k in range(ff_cut // gw):
            few[here + (slice(9 + k, 10 + k), slice(0, gw))] = b1_in[0:1, k * gw : (k + 1) * gw]
        few[here + (slice(0, heads), slice(gw, 2 * gw))] = tab_in[:, :gw]
        few[here + (slice(heads, 2 * heads), slice(gw, span))] = tab_in[:, gw:]
        greet(cube, range(n))
        own.wait()
        for c, s in order[:ready]:
            gather.advance(c, s)
        keep.start()
        vec_ref[...] = jnp.zeros_like(vec_ref)
        for f in range(fsdp):
            part = few[(0,) * n_t + digits_of(f, n_f)].astype(F32)
            vec_ref[0:6, f * cut : (f + 1) * cut] = part[0:6, :cut]
        for t in range(tp):
            part = few[digits_of(t, n_t) + (0,) * n_f].astype(F32)
            for k in range(3):
                at = (3 * t + k) * gw
                bq[0:1, at : at + gw] = part[6 + k : 7 + k, :gw]
            for k in range(ff_cut // gw):
                b1_ref[k : k + 1, t * gw : (t + 1) * gw] = part[9 + k : 10 + k, :gw]
            tab[t * heads : (t + 1) * heads, :gw] = part[0:heads, gw:]
            tab[t * heads : (t + 1) * heads, gw:] = part[heads : 2 * heads, gw:]
        table_rows = tab[...].astype(BF16)
        wide = 8 * ROWS
        for k in range(ROWS * ROWS // wide):
            entry = lax.broadcasted_iota(jnp.int32, (2 * gw, wide), 0)
            hot = (entry == rel_ref[0:1, k * wide : (k + 1) * wide]).astype(F32).astype(BF16)
            value = dot(table_rows, hot)
            for j in range(8):
                table[:, k * 8 + j, :] = value[:, j * ROWS : (j + 1) * ROWS]
        for g in range(n_grp):
            full = jnp.concatenate([table[g * GROUP + h] for h in range(GROUP)], axis=1)
            for w in range(n_win):
                bias_scr[g, w] = full + mask_ref[w]

    rest = order[ready:]
    for i, (c, s) in enumerate(rest):
        at = PASSES[min(i, len(PASSES) - 1)]

        @pl.when(step == jnp.minimum(at, steps - 1))
        def _(c=c, s=s):
            gather.advance(c, s)

    @pl.when(step == steps - 1)
    def _():
        keep.wait()

    x = img_ref[0].astype(F32)
    xhat, _ = standardize(x)
    normed = (xhat * vec_ref[0:1] + vec_ref[1:2]).astype(BF16)
    xp = dot(perm_ref[...], normed).astype(BF16)
    mb, mf = head_masks(BF16), head_masks(F32)
    for g in range(n_grp):
        c0 = g * 3 * gw
        weight = wq[digits_of(g, n_t)].reshape(fsdp * cut, 3 * gw)
        acc = dot(xp, weight) + bq[0:1, c0 : c0 + 3 * gw]
        qkv_ref[0, :, c0 : c0 + gw] = (acc[:, :gw] * (HD ** -0.5)).astype(BF16)
        qkv_ref[0, :, c0 + gw : c0 + 3 * gw] = acc[:, gw:].astype(BF16)

    def part(g, w, j):
        return qkv_ref[0, w * ROWS : (w + 1) * ROWS, (3 * g + j) * gw : (3 * g + j + 1) * gw]

    def score(g, w):
        return dot(part(g, w, 1), spread(part(g, w, 0), mb), NT) + bias_scr[g, w]

    def store(g, w, o):
        o_scr[w * ROWS : (w + 1) * ROWS, g * gw : (g + 1) * gw] = gather_heads(o, mf).astype(BF16)

    units = [(g, w) for g in range(n_grp) for w in range(n_win)]
    ahead, behind = score(*units[0]), None
    for at, (g, w) in enumerate(units):
        s = ahead
        if at + 1 < len(units):
            ahead = score(*units[at + 1])
        e = jnp.exp(s - jnp.max(s, axis=0, keepdims=True))
        p = (e * (1.0 / jnp.sum(e, axis=0, keepdims=True))).astype(BF16)
        p_ref[0, g, w] = p
        o = dot(p, part(g, w, 2), TN)
        if behind is not None:
            store(*behind)
        behind = (g, w, o)
    store(*behind)
    mix_ref[0] = dot(permt_ref[...], o_scr[...]).astype(BF16)


def front(vectors, b_qkv, b_one, table, w_qkv, w_proj, w_one, w_two, images, consts, fsdp, tp):
    rel, mask, perm, permt = consts
    n_img, t, c = images.shape
    cut, ff_cut = w_one.shape
    gw = LANES
    n_win = mask.shape[0]
    rows, cols = n_win * ROWS, W_ONE + 2 * ff_cut
    heads = tp * table.shape[0]
    n_t, n_f = len(bits_of(tp)), len(bits_of(fsdp))
    n = n_t + n_f
    n_sem = 7 * n
    once = lambda a: pl.BlockSpec(a.shape, lambda i: (0,) * a.ndim, pipeline_mode=pl.Buffered(1))
    whole = lambda s: pl.BlockSpec(s, lambda i: (0,) * len(s))
    small = tuple(vectors) + (b_qkv, b_one, table, w_qkv, w_proj, w_one, w_two)
    return pl.pallas_call(
        functools.partial(front_kernel, fsdp=fsdp, tp=tp),
        grid=(n_img,),
        in_specs=[once(a) for a in small]
        + [pl.BlockSpec((1, t, c), lambda i: (i, 0, 0))]
        + [once(a) for a in (rel, mask, perm, permt)],
        out_specs=[
            pl.BlockSpec(memory_space=pl.ANY),
            pl.BlockSpec(memory_space=pl.ANY),
            pl.BlockSpec((1, rows, 3 * tp * gw), lambda i: (i, 0, 0)),
            pl.BlockSpec((1, tp, n_win, ROWS, GROUP * ROWS), lambda i: (i, 0, 0, 0, 0)),
            pl.BlockSpec((1, t, c), lambda i: (i, 0, 0)),
            whole((8, c)),
            whole((ff_cut // gw, tp * gw)),
        ],
        out_shape=[
            jax.ShapeDtypeStruct((2,) * n + (cut, cols), BF16),
            jax.ShapeDtypeStruct((2,) * n + (cut, 3 * gw), BF16),
            jax.ShapeDtypeStruct((n_img, rows, 3 * tp * gw), BF16),
            jax.ShapeDtypeStruct((n_img, tp, n_win, ROWS, GROUP * ROWS), BF16),
            jax.ShapeDtypeStruct((n_img, t, c), BF16),
            jax.ShapeDtypeStruct((8, c), F32),
            jax.ShapeDtypeStruct((ff_cut // gw, tp * gw), F32),
        ],
        scratch_shapes=[
            pltpu.VMEM((cut, cols), BF16),
            pltpu.VMEM((2,) * n + (cut, 3 * gw), BF16),
            pltpu.VMEM((2,) * n + (SMALL, 2 * gw), BF16),
            pltpu.VMEM((1, 3 * tp * gw), F32),
            pltpu.VMEM((heads, 2 * gw), F32),
            pltpu.VMEM((heads, ROWS, ROWS), F32),
            pltpu.VMEM((tp, n_win, ROWS, GROUP * ROWS), F32),
            pltpu.VMEM((rows, c), BF16),
            pltpu.SemaphoreType.DMA((2,)),
            pltpu.SemaphoreType.DMA((n_sem,)),
            pltpu.SemaphoreType.DMA((n_sem,)),
        ],
        compiler_params=pltpu.CompilerParams(
            vmem_limit_bytes=60 << 20, collective_id=1, has_side_effects=True
        ),
        name="front",
    )(*small, images, rel, mask, perm, permt)


SQRT_HALF = float(np.sqrt(0.5))
INV_SQRT_2PI = float(1.0 / np.sqrt(2.0 * np.pi))


class Spread:
    def __init__(self, cube, full, send, recv):
        self.cube, self.full, self.send, self.recv = cube, full, send, recv
        self.stages = cube.n_t

    def ref(self, s, i):
        own = self.cube.own
        return self.full.at[tuple(slice(None) if k < s else own[k] for k in range(self.stages)) + (i,)]

    def copy(self, s, i):
        ref = self.ref(s, i)
        return pltpu.make_async_remote_copy(
            ref, ref, self.send.at[s, i], self.recv.at[s, i], device_id=self.cube.partner(s), device_id_type=MESH
        )


class Reduce:
    def __init__(self, cube, acc, order, bufs, send, recv, n_digits, out):
        self.cube, self.acc, self.order, self.bufs = cube, acc, order, bufs
        self.send, self.recv, self.n_digits, self.out = send, recv, n_digits, out
        self.stages = len(order)

    def at(self, free, flip=None):
        own = self.cube.own
        return tuple(
            slice(None) if k in free else (1 - own[k] if k == flip else own[k]) for k in range(self.n_digits)
        )

    def left(self, s):
        return sorted(k for k in self.order[s + 1 :] if k < self.n_digits)

    def copy(self, s):
        return pltpu.make_async_remote_copy(
            self.acc.at[self.at(self.left(s), self.order[s])],
            self.bufs[s],
            self.send.at[s],
            self.recv.at[s],
            device_id=self.cube.partner(self.order[s]),
            device_id_type=MESH,
        )

    def start(self):
        self.copy(0).start()

    def advance(self, s):
        self.copy(s).wait()
        region = self.at(self.left(s))
        if s + 1 == self.stages:
            self.out(self.acc[region].astype(F32) + self.bufs[s][...].astype(F32))
        else:
            self.acc[region] = self.acc[region] + self.bufs[s][...]
        if s + 1 < self.stages:
            self.copy(s + 1).start()


def reduce_orders(n_t, n):
    t, f = list(range(n_t)), list(range(n_t, n))
    t_in, f_in = t[1:][::-1], f[::-1]
    early = (t_in + f_in + t[:1], t_in + f[:-1][::-1] + f[-1:] + t[:1])
    late = (t_in + f_in + t[:1], t_in + f[1:-1][::-1] + f[-1:] + t[:1] + f[:1])
    return early, late, t[::-1] + f_in


def layer_kernel(live_ref, img_hbm, cot_hbm, mix_ref, w_hbm, wq_hbm, vec_ref, b1_ref, qkv_ref, p_ref, perm_ref, permt_ref,
                 out_ref, gin_ref, dqkv_ref, dw1_ref, dw2_ref, dwp_ref, small_ref,
                 img_ref, cot_ref, w1_ref, w2_ref, wq_ref, wp, act, slope, normed_two, up_scr, gres_scr,
                 db1, dvec, dqkv_scr, dw, db, dtab, res_scr, acc, acc_p, late_a, late_b, small, *rest,
                 fsdp, tp, per, n_q):
    step = pl.program_id(0)
    cube = Cube(fsdp, tp)
    n, n_t, n_f = cube.count, cube.n_t, cube.count - cube.n_t
    n_img, n_tok, c = img_ref.shape
    n_grp, n_win = p_ref.shape[1:3]
    gw = LANES
    cut = c // fsdp
    fwd_steps = n_img // per
    bwd_at = fwd_steps
    att_at = bwd_at + n_q
    last_step = att_at + n_img - 1

    early, late, both = reduce_orders(n_t, n)
    bufs, rest = rest[: 5 * n], rest[5 * n :]
    load, local, send, recv, local_in, send_in, recv_in, rs_send, rs_recv = rest

    wide_q = n_q * gw
    loads = [
        pltpu.make_async_copy(w_hbm.at[:, :, pl.ds(W_ONE, wide_q)], w1_ref, load.at[0]),
        pltpu.make_async_copy(w_hbm.at[:, :, pl.ds(W_ONE + wide_q, wide_q)], w2_ref, load.at[1]),
        pltpu.make_async_copy(img_hbm, img_ref, load.at[2]),
        pltpu.make_async_copy(cot_hbm, cot_ref, load.at[3]),
    ]
    loads += [
        pltpu.make_async_copy(w_hbm.at[g, :, pl.ds(0, gw)], wp.at[:, pl.ds(g * gw, gw)], load.at[5 + g])
        for g in range(n_grp)
    ]
    load_wq = pltpu.make_async_copy(wq_hbm, wq_ref, load.at[4])
    gmix_scr = cot_ref

    def result_of(q):
        def out(total):
            dw1_ref[:, q * gw : (q + 1) * gw] = total[:, :gw]
            dw2_ref[:, q * gw : (q + 1) * gw] = total[:, gw:]

        return out

    def result_p(total):
        dwp_ref[...] = total

    def result_a(total):
        for k in range(3):
            dqkv_ref[k, : cut // 2] = total[:, k * gw : (k + 1) * gw]

    def result_b(total):
        for k in range(3):
            dqkv_ref[k, cut // 2 :] = total[:, k * gw : (k + 1) * gw]

    def result_s(total):
        small_ref[...] = total

    plans = [
        (acc.at[q], [ref.at[q] for ref in bufs[:n]], early[q % 2], n, result_of(q)) for q in range(n_q)
    ]
    plans += [
        (acc_p, bufs[n : 2 * n], early[0], n, result_p),
        (late_a, bufs[2 * n : 3 * n], late[0], n, result_a),
        (late_b, bufs[3 * n : 4 * n], late[1], n, result_b),
        (small, bufs[4 * n :], both, n_t, result_s),
    ]
    reduces = [
        Reduce(cube, ref, order, buf, rs_send.at[k], rs_recv.at[k], d, out)
        for k, (ref, buf, order, d, out) in enumerate(plans)
    ]
    n_early = n_q + 1
    spread_out = Spread(cube, out_ref, send, recv)
    spread_in = Spread(cube, gin_ref, send_in, recv_in)

    def keep_out(i):
        return pltpu.make_async_copy(res_scr.at[pl.ds(i * per, per)], spread_out.ref(0, i), local.at[i])

    def keep_in(i):
        return pltpu.make_async_copy(res_scr.at[i], spread_in.ref(0, i), local_in.at[i])

    events = {}

    def plan(at, work):
        events.setdefault(at, []).append(work)

    def point(k):
        for at in sorted(events):
            if at[1] == k:

                @pl.when(step == at[0])
                def _(at=at):
                    for work in events[at]:
                        work()

    def send_out(i):
        keep_out(i).wait()
        spread_out.copy(0, i).start()

    def pass_out(i, s):
        spread_out.copy(s - 1, i).wait()
        spread_out.copy(s, i).start()

    def send_in_(i):
        keep_in(i).wait()
        spread_in.copy(0, i).start()

    def pass_in(i, s):
        spread_in.copy(s - 1, i).wait()
        spread_in.copy(s, i).start()

    for i in range(fwd_steps):
        plan((i + 1, 0), functools.partial(send_out, i))
    later = [att_at - 1 + 3 * i for i in range(fwd_steps)]
    for s in range(1, n_t):
        for i in range(fwd_steps):
            plan((min(later[i] + s - 1, last_step), 0), functools.partial(pass_out, i, s))
    for i in range(n_img - 1):
        plan((att_at + i + 1, 0), functools.partial(send_in_, i))
    tail = []
    for i in range(n_img):
        for s in range(1, n_t):
            at = att_at + i + 3 + s
            if at <= last_step:
                plan((at, 0), functools.partial(pass_in, i, s))
            else:
                tail.append(functools.partial(pass_in, i, s))
    ends = []
    for k in range(n_early):
        begin = (bwd_at + k + 1, 1) if k + 1 < n_q else (att_at, 0)
        plan(begin, reduces[k].start)
        slots = SLOTS[k] if k < len(SLOTS) else ()
        for s in range(n):
            work = functools.partial(reduces[k].advance, s)
            if s < len(slots):
                plan((bwd_at + slots[s][0], slots[s][1]), work)
            else:
                ends.append(work)

    @pl.when(step == 0)
    def _():
        for ld in loads[2:] + loads[:2] + [load_wq]:
            ld.start()
        greet(cube, range(n))
        dw[...] = jnp.zeros_like(dw)
        dvec[...] = jnp.zeros_like(dvec)
        db[...] = jnp.zeros_like(db)
        db1[...] = jnp.zeros_like(db1)
        dtab[...] = jnp.zeros_like(dtab)
        for ld in loads[2:]:
            ld.wait()

    def columns(ref, q):
        at = pl.ds(pl.multiple_of(q * gw, gw), gw)
        return jnp.concatenate([ref[g, :, at] for g in range(n_grp)], axis=1)

    def rows_of(ref, b):
        return jnp.concatenate([ref[b * per + i] for i in range(per)], axis=0)

    def middle(b):
        mixed = rows_of(mix_ref, b)
        res = rows_of(img_ref, b).astype(F32) + (dot(mixed, wp[...], NT) + vec_ref[2:3])
        return (mixed, res) + standardize(res)

    @pl.when(step < bwd_at)
    def _():
        point(0)
        live = jnp.concatenate(
            [jnp.full((n_tok, 1), 1.0, F32) * live_ref[step * per + i] for i in range(per)], axis=0
        )
        up = rows_of(cot_ref, step).astype(F32) * live
        up_scr[step] = up.astype(BF16)
        dvec[5:6] += jnp.sum(up, axis=0, keepdims=True)
        mixed, res, xhat, _ = middle(step)
        normed_two[step] = (xhat * vec_ref[3:4] + vec_ref[4:5]).astype(BF16)

        @pl.when(step == 0)
        def _():
            for ld in loads[:2]:
                ld.wait()

        def hidden_part(q, branch):
            hid = dot(normed_two[step], columns(w1_ref, q)) + b1_ref[pl.ds(q, 1)]
            cdf = 0.5 * (1.0 + lax.erf(hid * SQRT_HALF))
            a = (hid * cdf).astype(BF16)
            act[step, q] = a
            slope[step, q] = (cdf + hid * (jnp.exp(-0.5 * hid * hid) * INV_SQRT_2PI)).astype(BF16)
            return branch + dot(a, columns(w2_ref, q), NT)

        total = lax.fori_loop(0, n_q, hidden_part, res + vec_ref[5:6])
        out = (live * total).astype(BF16)
        for i in range(per):
            res_scr[step * per + i] = out[i * n_tok : (i + 1) * n_tok]
        keep_out(step).start()

    @pl.when(jnp.logical_and(step >= bwd_at, step < att_at))
    def _():
        q = step - bwd_at
        point(0)
        w2 = columns(w2_ref, q)
        d_one = d_two = None
        for b in range(fwd_steps):
            if b == 1:
                point(1)
            up = up_scr[b]
            dh = (dot(up, w2) * slope[b, q].astype(F32)).astype(BF16)
            slope[b, q] = dh
            db1[pl.ds(q, 1)] += jnp.sum(dh.astype(F32), axis=0, keepdims=True)
            one, two = dot(normed_two[b], dh, TN), dot(up, act[b, q], TN)
            d_one, d_two = (one, two) if b == 0 else (d_one + one, d_two + two)
        for t in range(n_grp):
            block = (2,) * n_f + (cut, gw)
            at = (q,) + digits_of(t, n_t) + (slice(None),) * (n_f + 1)
            l = slice(t * gw, (t + 1) * gw)
            acc[at + (slice(0, gw),)] = d_one[:, l].astype(BF16).reshape(block)
            acc[at + (slice(gw, 2 * gw),)] = d_two[:, l].astype(BF16).reshape(block)

    @pl.when(step == att_at - 1)
    def _():
        point(2)

        def back(b, d_proj):
            dn = dot(slope[b, 0], columns(w1_ref, 0), NT)
            for k in range(1, n_q):
                dn = dn + dot(slope[b, k], columns(w1_ref, k), NT)
            mixed, _, xhat, inv = middle(b)
            d = dn * vec_ref[3:4]
            gres = up_scr[b].astype(F32) + inv * (
                d - jnp.mean(d, axis=-1, keepdims=True) - xhat * jnp.mean(d * xhat, axis=-1, keepdims=True)
            )
            gatt = gres.astype(BF16)
            gmix = dot(gatt, wp[...]).astype(BF16)
            for i in range(per):
                r = slice(i * n_tok, (i + 1) * n_tok)
                gres_scr[b * per + i] = gres[r]
                gmix_scr[b * per + i] = gmix[r]
            dvec[2:3] += jnp.sum(gatt.astype(F32), axis=0, keepdims=True)
            dvec[3:4] += jnp.sum(dn * xhat, axis=0, keepdims=True)
            dvec[4:5] += jnp.sum(dn, axis=0, keepdims=True)
            return d_proj + dot(gatt, mixed, TN)

        d_proj = lax.fori_loop(0, fwd_steps, back, jnp.zeros((c, c), F32))
        for t in range(n_grp):
            acc_p[digits_of(t, n_t)] = (
                d_proj[:, t * gw : (t + 1) * gw].astype(BF16).reshape((2,) * n_f + (cut, gw))
            )

    @pl.when(step == att_at)
    def _():
        load_wq.wait()

    @pl.when(step >= att_at)
    def _():
        j = step - att_at
        mb, mf = head_masks(BF16), head_masks(F32)
        point(0)
        x = img_ref[j].astype(F32)
        xhat, inv = standardize(x)
        normed = (xhat * vec_ref[0:1] + vec_ref[1:2]).astype(BF16)
        xp = dot(perm_ref[...], normed).astype(BF16)
        gm = dot(perm_ref[...], gmix_scr[j]).astype(BF16)
        dn = jnp.zeros((n_win * ROWS, c), F32)
        for g in range(n_grp):
            if g > 0:
                point(g)
            c0 = g * 3 * gw
            tab = jnp.zeros((ROWS, GROUP * ROWS), F32)
            cuts = [slice(w * ROWS, (w + 1) * ROWS) for w in range(n_win)]
            dos = [spread(gm[r, g * gw : (g + 1) * gw], mb) for r in cuts]
            dps = [dot(qkv_ref[0, r, c0 + 2 * gw : c0 + 3 * gw], do, NT) for r, do in zip(cuts, dos)]
            ps = [p_ref[0, g, w] for w in range(n_win)]
            dvs = [dot(p, do) for p, do in zip(ps, dos)]
            dss = []
            for p, dp in zip(ps, dps):
                pf = p.astype(F32)
                ds = pf * (dp - jnp.sum(pf * dp, axis=0, keepdims=True))
                tab = tab + ds
                dss.append(ds.astype(BF16))
            dks = [dot(ds, spread(qkv_ref[0, r, c0 : c0 + gw], mb)) for r, ds in zip(cuts, dss)]
            dqs = [dot(ds, qkv_ref[0, r, c0 + gw : c0 + 2 * gw], TN) for r, ds in zip(cuts, dss)]
            for r, dq, dk, dv in zip(cuts, dqs, dks, dvs):
                dqkv_scr[r, :gw] = (gather_heads(dq, mf) * (HD ** -0.5)).astype(BF16)
                dqkv_scr[r, gw : 2 * gw] = dk.astype(BF16)
                dqkv_scr[r, 2 * gw :] = dv.astype(BF16)
            dtab[g] += tab
            dqkv = dqkv_scr[...]
            db[0:1, c0 : c0 + 3 * gw] += jnp.sum(dqkv.astype(F32), axis=0, keepdims=True)
            dw[g] += dot(xp, dqkv, TN)
            dn = dn + dot(dqkv, wq_ref[g], NT)
        hi = dn.astype(BF16)
        lo = (dn - hi.astype(F32)).astype(BF16)
        dn = dot(permt_ref[...], hi) + dot(permt_ref[...], lo)
        d = dn * vec_ref[0:1]
        gin = inv * (
            d - jnp.mean(d, axis=-1, keepdims=True) - xhat * jnp.mean(d * xhat, axis=-1, keepdims=True)
        )
        res_scr[j] = (gres_scr[j] + gin).astype(BF16)
        keep_in(j).start()
        dvec[0:1] += jnp.sum(dn * xhat, axis=0, keepdims=True)
        dvec[1:2] += jnp.sum(dn, axis=0, keepdims=True)

    @pl.when(step == last_step)
    def _():
        for g in range(n_grp):
            value = dw[g].astype(BF16).reshape((2,) * n_f + (cut, 3 * gw))
            late_a[digits_of(g, n_t)] = value[..., : cut // 2, :]
            late_b[digits_of(g, n_t)] = value[..., cut // 2 :, :]
        for red in reduces[n_early : n_early + 2]:
            red.start()
        wide = GROUP * ROWS
        for g in range(n_grp):
            panel = small.at[digits_of(g, n_t)]
            panel[:ROWS] = dtab[g]
            c0 = g * 3 * gw
            panel[ROWS : ROWS + 1] = db[0:1, c0 : c0 + wide]
            panel[ROWS + 1 : ROWS + 2] = jnp.concatenate(
                [db[0:1, c0 + wide : c0 + 3 * gw], jnp.zeros((1, 2 * wide - 3 * gw), F32)], axis=1
            )
            r = ROWS + 2
            for q in range(0, n_q, 2):
                pair = [db1[q + k : q + k + 1, g * gw : (g + 1) * gw] for k in range(2)]
                panel[r : r + 1] = jnp.concatenate(pair, axis=1)
                r = r + 1
            for i in range(6):
                for k in range(c // wide):
                    panel[r : r + 1] = dvec[i : i + 1, k * wide : (k + 1) * wide]
                    r = r + 1
        reduces[n_early + 2].start()
        send_in_(n_img - 1)
        for s in range(n):
            for red in reduces[n_early:]:
                red.advance(s)
            if s == TAIL_AT:
                for work in tail:
                    work()
        for work in ends:
            work()
        for i in range(fwd_steps):
            spread_out.copy(n_t - 1, i).wait()
        for i in range(n_img):
            spread_in.copy(n_t - 1, i).wait()


SLOTS = (
    ((3, 0), (4, 2), (6, 0), (8, 0), (10, 0)),
    ((4, 0), (6, 0), (8, 0), (10, 0)),
    ((5, 0), (7, 0), (9, 0), (11, 0)),
    ((6, 0), (8, 2), (10, 2), (11, 3)),
    ((6, 0), (8, 2), (10, 2), (11, 3)),
)
TAIL_AT = 2


def layer(live, images, out_grad, mixed, w_all, w_qkv, vecs, b1, qkv, p, perm, permt, fsdp, tp, per=4):
    n_img, t, c = mixed.shape
    rows, cols = qkv.shape[1:]
    n_grp, n_win = p.shape[1:3]
    gw, wide = LANES, GROUP * ROWS
    n_q = b1.shape[0]
    ff_cut = n_q * gw
    cut = c // fsdp
    n_t, n_f = len(bits_of(tp)), len(bits_of(fsdp))
    n = n_t + n_f
    digits = (2,) * n
    n_small = ROWS + 2 + ff_cut // wide + 6 * (c // wide)
    fwd_steps = n_img // per
    att_at = fwd_steps + n_q
    bufs = []
    for lead, block in (
        ((n_q,), (cut, 2 * gw)),
        ((), (cut, gw)),
        ((), (cut // 2, 3 * gw)),
        ((), (cut // 2, 3 * gw)),
    ):
        bufs += [pltpu.VMEM(lead + (2,) * (n - 1 - s) + block, BF16) for s in range(n)]
    both = reduce_orders(n_t, n)[2]
    for s in range(n):
        left = sum(k < n_t for k in both[s + 1 :])
        bufs.append(pltpu.VMEM((2,) * left + (n_small, wide), F32))
    whole = lambda s: pl.BlockSpec(s, lambda i: (0,) * len(s))
    once = lambda s: pl.BlockSpec(s, lambda i: (0,) * len(s), pipeline_mode=pl.Buffered(1))
    image = lambda i: jnp.clip(i - att_at, 0, n_img - 1)
    any_spec = pl.BlockSpec(memory_space=pl.ANY)
    hidden = (fwd_steps, n_q, per * t, n_grp * gw)
    return pl.pallas_call(
        functools.partial(layer_kernel, fsdp=fsdp, tp=tp, per=per, n_q=n_q),
        grid=(att_at + n_img,),
        in_specs=[
            pl.BlockSpec(memory_space=pltpu.SMEM),
            any_spec,
            any_spec,
            once(mixed.shape),
            any_spec,
            any_spec,
            once(vecs.shape),
            once(b1.shape),
            pl.BlockSpec((1, rows, cols), lambda i: (image(i), 0, 0)),
            pl.BlockSpec((1,) + p.shape[1:], lambda i: (image(i), 0, 0, 0, 0)),
            once(perm.shape),
            once(permt.shape),
        ],
        out_specs=[any_spec, any_spec]
        + [whole(s) for s in ((3, cut, gw), (cut, ff_cut), (cut, ff_cut), (cut, gw), (n_small, wide))],
        out_shape=[
            jax.ShapeDtypeStruct((2,) * n_t + (fwd_steps, per, t, c), BF16),
            jax.ShapeDtypeStruct((2,) * n_t + (n_img, t, c), BF16),
            jax.ShapeDtypeStruct((3, cut, gw), F32),
            jax.ShapeDtypeStruct((cut, ff_cut), F32),
            jax.ShapeDtypeStruct((cut, ff_cut), F32),
            jax.ShapeDtypeStruct((cut, gw), F32),
            jax.ShapeDtypeStruct((n_small, wide), F32),
        ],
        scratch_shapes=[
            pltpu.VMEM((n_img, t, c), BF16),
            pltpu.VMEM((n_img, t, c), BF16),
            pltpu.VMEM((n_grp, c, ff_cut), BF16),
            pltpu.VMEM((n_grp, c, ff_cut), BF16),
            pltpu.VMEM((n_grp, c, 3 * gw), BF16),
            pltpu.VMEM((c, c), BF16),
            pltpu.VMEM(hidden, BF16),
            pltpu.VMEM(hidden, BF16),
            pltpu.VMEM((fwd_steps, per * t, c), BF16),
            pltpu.VMEM((fwd_steps, per * t, c), BF16),
            pltpu.VMEM((n_img, t, c), F32),
            pltpu.VMEM((8, n_grp * gw), F32),
            pltpu.VMEM((8, c), F32),
            pltpu.VMEM((rows, 3 * gw), BF16),
            pltpu.VMEM((n_grp, c, 3 * gw), F32),
            pltpu.VMEM((1, cols), F32),
            pltpu.VMEM((n_grp, ROWS, wide), F32),
            pltpu.VMEM((n_img, t, c), BF16),
            pltpu.VMEM((n_q,) + digits + (cut, 2 * gw), BF16),
            pltpu.VMEM(digits + (cut, gw), BF16),
            pltpu.VMEM(digits + (cut // 2, 3 * gw), BF16),
            pltpu.VMEM(digits + (cut // 2, 3 * gw), BF16),
            pltpu.VMEM((2,) * n_t + (n_small, wide), F32),
            *bufs,
            pltpu.SemaphoreType.DMA((5 + n_grp,)),
            pltpu.SemaphoreType.DMA((fwd_steps,)),
            pltpu.SemaphoreType.DMA((n_t, fwd_steps)),
            pltpu.SemaphoreType.DMA((n_t, fwd_steps)),
            pltpu.SemaphoreType.DMA((n_img,)),
            pltpu.SemaphoreType.DMA((n_t, n_img)),
            pltpu.SemaphoreType.DMA((n_t, n_img)),
            pltpu.SemaphoreType.DMA((n_q + 4, n)),
            pltpu.SemaphoreType.DMA((n_q + 4, n)),
        ],
        compiler_params=pltpu.CompilerParams(
            vmem_limit_bytes=60 << 20, collective_id=2, has_side_effects=True
        ),
        name="layer",
    )(live, images, out_grad, mixed, w_all, w_qkv, vecs, b1, qkv, p, perm, permt)


def per_device(
    images,
    attn_norm_gain,
    attn_norm_bias,
    qkv_weight,
    qkv_bias,
    position_table,
    proj_weight,
    proj_bias,
    mlp_norm_gain,
    mlp_norm_bias,
    fc1_weight,
    fc1_bias,
    fc2_weight,
    fc2_bias,
    image_count,
    out_grad,
    *,
    fsdp,
    tp,
):
    index, mask, perm = window_constants()
    span = position_table.shape[0]
    gw = LANES
    cut = qkv_weight.shape[0]
    width = cut * fsdp
    ff_cut = fc1_bias.shape[0]
    n_qkv = qkv_bias.size
    mine = images.shape[0] // tp
    first = lax.axis_index("tp") * mine
    img = lax.dynamic_slice_in_dim(images, first, mine, 0)
    cot = lax.dynamic_slice_in_dim(out_grad, first, mine, 0)
    live = (first + jnp.arange(mine, dtype=jnp.int32) < image_count[0]).astype(F32)
    perm16 = jnp.asarray(perm).astype(BF16)
    consts = (jnp.asarray(index).reshape(1, -1), jnp.asarray(mask), perm16, perm16.T)
    vectors = (attn_norm_gain, attn_norm_bias, proj_bias, mlp_norm_gain, mlp_norm_bias, fc2_bias)
    w_all, w_qkv, qkv, probs, mixed, vecs, b_one = front(
        [v.reshape(1, cut) for v in vectors],
        qkv_bias,
        fc1_bias.reshape(1, ff_cut),
        position_table.T,
        qkv_weight.transpose(1, 0, 2),
        proj_weight.T,
        fc1_weight,
        fc2_weight.T,
        img,
        consts,
        fsdp,
        tp,
    )
    w_all = w_all.reshape(tp, width, w_all.shape[-1])
    w_qkv = w_qkv.reshape(tp, width, 3 * gw)
    output, images_grad, d_qkv, d_one, d_two, d_proj, small = layer(
        live, img, cot, mixed, w_all, w_qkv, vecs, b_one, qkv, probs, consts[2], consts[3], fsdp, tp
    )
    wide = GROUP * ROWS
    hot = (jnp.asarray(index)[None] == jnp.arange(span, dtype=jnp.int32)[:, None, None]).astype(F32)
    d_tab = jnp.einsum(
        "jhi,rji->rh",
        small[:ROWS].reshape(ROWS, GROUP, ROWS),
        hot,
        precision=lax.Precision.HIGHEST,
    )
    at = ROWS + 2
    dqkv_bias = small[ROWS:at].reshape(-1)[:n_qkv].reshape(qkv_bias.shape)
    dfc1_bias = small[at : at + ff_cut // wide].reshape(-1)
    dvec = small[at + ff_cut // wide :].reshape(6, width)
    dvec = lax.dynamic_slice_in_dim(dvec, lax.axis_index("fsdp") * cut, cut, 1)
    return (
        output.reshape(images.shape),
        images_grad.reshape(images.shape),
        dvec[0],
        dvec[1],
        d_qkv.transpose(1, 0, 2),
        dqkv_bias,
        d_tab,
        d_proj.T,
        dvec[2],
        dvec[3],
        dvec[4],
        d_one,
        dfc1_bias,
        d_two.T,
        dvec[5],
    )


def solution(mesh):
    P = jax.sharding.PartitionSpec
    return jax.shard_map(
        functools.partial(per_device, fsdp=mesh.shape["fsdp"], tp=mesh.shape["tp"]),
        mesh=mesh,
        in_specs=(
            P("fsdp", None, None),
            P("fsdp"),
            P("fsdp"),
            P("fsdp", None, "tp"),
            P(None, "tp"),
            P(None, "tp"),
            P("tp", "fsdp"),
            P("fsdp"),
            P("fsdp"),
            P("fsdp"),
            P("fsdp", "tp"),
            P("tp"),
            P("tp", "fsdp"),
            P("fsdp"),
            P("fsdp"),
            P("fsdp", None, None),
        ),
        out_specs=(
            P("fsdp", None, None),
            P("fsdp", None, None),
            P("fsdp"),
            P("fsdp"),
            P("fsdp", None, "tp"),
            P(None, "tp"),
            P(None, "tp"),
            P("tp", "fsdp"),
            P("fsdp"),
            P("fsdp"),
            P("fsdp"),
            P("fsdp", "tp"),
            P("tp"),
            P("tp", "fsdp"),
            P("fsdp"),
        ),
        check_vma=False,
    )
```

```python
import functools
import jax
import jax.numpy as jnp
import numpy as np
from jax import lax
from jax.experimental import pallas as pl
from jax.experimental.pallas import tpu as pltpu

HD = 32
WIN = 7
SHIFT = 3
SIDE = 14
AREA = WIN * WIN
ROWS = 64
GROUP = 4
EPSILON = 1e-05
F32 = jnp.float32
BF16 = jnp.bfloat16
PADDED = -1e30
MESH = pl.DeviceIdType.MESH


def window_constants():
    offsets = np.arange(WIN)
    rows, cols = np.repeat(offsets, WIN), np.tile(offsets, WIN)
    relative = (rows[:, None] - rows[None, :] + WIN - 1) * (2 * WIN - 1) + (
        cols[:, None] - cols[None, :] + WIN - 1
    )
    span = (2 * WIN - 1) ** 2
    index = np.full((ROWS, ROWS), span, np.int32)
    index[:AREA, :AREA] = relative.T
    region = np.zeros((SIDE, SIDE), np.int32)
    bounds = ((0, SIDE - WIN), (SIDE - WIN, SIDE - SHIFT), (SIDE - SHIFT, SIDE))
    for a, rr in enumerate(bounds):
        for b, cc in enumerate(bounds):
            region[rr[0] : rr[1], cc[0] : cc[1]] = 3 * a + b
    across = SIDE // WIN
    cut = region.reshape(across, WIN, across, WIN).transpose(0, 2, 1, 3).reshape(across * across, AREA)
    mask = np.zeros((across * across, ROWS, ROWS), np.float32)
    mask[:, :AREA, :AREA] = np.where(cut[:, :, None] == cut[:, None, :], 0.0, -100.0)
    mask[:, AREA:, :] = PADDED
    mask = np.tile(mask, (1, 1, GROUP))
    perm = np.zeros((across * across * ROWS, SIDE * SIDE), np.float32)
    for w in range(across * across):
        for s in range(AREA):
            r = ((w // across) * WIN + s // WIN + SHIFT) % SIDE
            c = ((w % across) * WIN + s % WIN + SHIFT) % SIDE
            perm[w * ROWS + s, r * SIDE + c] = 1.0
    return index, mask, perm


def dot(a, b, dims=((1,), (0,))):
    return lax.dot_general(a, b, (dims, ((), ())), preferred_element_type=F32)


NT = ((1,), (1,))
TN = ((0,), (0,))


def standardize(x):
    c = x - jnp.mean(x, axis=-1, keepdims=True)
    inv = lax.rsqrt(jnp.mean(c * c, axis=-1, keepdims=True) + EPSILON)
    return c * inv, inv


def head_masks(dtype):
    lane = lax.broadcasted_iota(jnp.int32, (1, GROUP * HD), 1) // HD
    return [(lane == h).astype(F32).astype(dtype) for h in range(GROUP)]


def spread(x, masks):
    return jnp.concatenate([x * m for m in masks], axis=0)


def gather_heads(y, masks):
    out = y[:ROWS] * masks[0]
    for h in range(1, GROUP):
        out = out + y[h * ROWS : (h + 1) * ROWS] * masks[h]
    return out


def bits_of(n):
    return [1 << b for b in reversed(range(n.bit_length() - 1))]

class Cube:
    def __init__(self, fsdp, tp):
        self.f, self.t = lax.axis_index("fsdp"), lax.axis_index("tp")
        self.digits = [("tp", b) for b in bits_of(tp)] + [("fsdp", b) for b in bits_of(fsdp)]
        self.own = [lax.rem((self.t if a == "tp" else self.f) // b, 2) for a, b in self.digits]
        self.count = len(self.digits)
        self.n_t = len(bits_of(tp))

    def partner(self, k):
        axis, b = self.digits[k]
        step = b * (1 - 2 * self.own[k])
        if axis == "tp":
            return (self.f, self.t + step)
        return (self.f + step, self.t)

    def at(self, free, flip=None):
        out = []
        for k in range(self.count):
            if k in free:
                out.append(slice(None))
            else:
                out.append(1 - self.own[k] if k == flip else self.own[k])
        return tuple(out)


def greet(cube, digits):
    bar = pltpu.get_barrier_semaphore()
    for k in digits:
        pl.semaphore_signal(bar, inc=1, device_id=cube.partner(k), device_id_type=MESH)
    pl.semaphore_wait(bar, len(digits))


def gather_orders(cube):
    t, f = list(range(cube.n_t)), list(range(cube.n_t, cube.count))
    return (f + t, f[:-1] + t[:-1] + f[-1:] + t[-1:])


class Gather:
    def __init__(self, cube, chunks, send, recv):
        self.cube, self.chunks, self.send, self.recv = cube, chunks, send, recv
        self.lanes = [sum(len(k) for k in chunks[:c]) for c in range(len(chunks))]

    def copies(self, c, s):
        for h, (ref, part, order) in enumerate(self.chunks[c]):
            ref = ref.at[self.cube.at(order[:s]) + part]
            i = (self.lanes[c] + h) * self.cube.count + s
            yield pltpu.make_async_remote_copy(
                ref,
                ref,
                self.send.at[i],
                self.recv.at[i],
                device_id=self.cube.partner(order[s]),
                device_id_type=MESH,
            )

    def plan(self):
        n = self.cube.count
        events = ((c, s) for c in range(len(self.chunks)) for s in range(n + 1))
        return sorted(events, key=lambda e: (LAGS[e[0]] + e[1], e[0]))

    def advance(self, c, s):
        if s > 0:
            for copy in self.copies(c, s - 1):
                copy.wait()
        if s < self.cube.count:
            for copy in self.copies(c, s):
                copy.start()


LAGS = (0, 1, 2)


LANES = GROUP * HD
SMALL = 16
PASSES = (3, 3, 5, 5, 7)
W_ONE = LANES


def digits_of(value, n):
    return tuple((value >> (n - 1 - k)) & 1 for k in range(n))


def front_kernel(*refs, fsdp, tp):
    vectors, refs = refs[:6], refs[6:]
    (bq_in, b1_in, tab_in, wq_in, wp_in, w1_in, w2_in, img_ref, rel_ref, mask_ref, perm_ref, permt_ref,
     full_ref, wq_out, qkv_ref, p_ref, mix_ref, vec_ref, b1_ref,
     pack, wq, few, bq, tab, table, bias_scr, o_scr, local, send, recv) = refs
    step, steps = pl.program_id(0), pl.num_programs(0)
    cube = Cube(fsdp, tp)
    n, n_t, n_f = cube.count, cube.n_t, cube.count - cube.n_t
    n_win, n_grp = mask_ref.shape[0], tp
    gw = LANES
    cut, ff_cut = w1_in.shape
    heads, span = tab_in.shape
    halves = [pl.ds(h * (cut // 2), cut // 2) for h in range(2)]
    orders = gather_orders(cube)
    split = lambda ref, cols: [(ref, (rows, cols), order) for rows, order in zip(halves, orders)]
    chunks = [
        split(wq, slice(None)) + [(few, (slice(None), slice(None)), orders[0])],
        split(full_ref, pl.ds(0, W_ONE + ff_cut)),
        split(full_ref, pl.ds(W_ONE + ff_cut, ff_cut)),
    ]
    gather = Gather(cube, chunks, send, recv)
    order = gather.plan()
    ready = order.index((0, n)) + 1
    keep = pltpu.make_async_copy(wq, wq_out, local.at[1])

    @pl.when(step == 0)
    def _():
        pack[:, :W_ONE] = wp_in[...]
        pack[:, W_ONE : W_ONE + ff_cut] = w1_in[...]
        pack[:, W_ONE + ff_cut :] = w2_in[...]
        own = pltpu.make_async_copy(pack, full_ref.at[cube.at(())], local.at[0])
        own.start()
        here = cube.at(())
        few[here] = jnp.zeros((SMALL, 2 * gw), BF16)
        for i, ref in enumerate(vectors):
            few[here + (slice(i, i + 1), slice(0, cut))] = ref[...]
        for k in range(3):
            wq[here + (slice(None), slice(k * gw, (k + 1) * gw))] = wq_in[k]
            few[here + (slice(6 + k, 7 + k), slice(0, gw))] = bq_in[k : k + 1]
        for k in range(ff_cut // gw):
            few[here + (slice(9 + k, 10 + k), slice(0, gw))] = b1_in[0:1, k * gw : (k + 1) * gw]
        few[here + (slice(0, heads), slice(gw, 2 * gw))] = tab_in[:, :gw]
        few[here + (slice(heads, 2 * heads), slice(gw, span))] = tab_in[:, gw:]
        greet(cube, range(n))
        own.wait()
        for c, s in order[:ready]:
            gather.advance(c, s)
        keep.start()
        vec_ref[...] = jnp.zeros_like(vec_ref)
        for f in range(fsdp):
            part = few[(0,) * n_t + digits_of(f, n_f)].astype(F32)
            vec_ref[0:6, f * cut : (f + 1) * cut] = part[0:6, :cut]
        for t in range(tp):
            part = few[digits_of(t, n_t) + (0,) * n_f].astype(F32)
            for k in range(3):
                at = (3 * t + k) * gw
                bq[0:1, at : at + gw] = part[6 + k : 7 + k, :gw]
            for k in range(ff_cut // gw):
                b1_ref[k : k + 1, t * gw : (t + 1) * gw] = part[9 + k : 10 + k, :gw]
            tab[t * heads : (t + 1) * heads, :gw] = part[0:heads, gw:]
            tab[t * heads : (t + 1) * heads, gw:] = part[heads : 2 * heads, gw:]
        table_rows = tab[...].astype(BF16)
        wide = 8 * ROWS
        for k in range(ROWS * ROWS // wide):
            entry = lax.broadcasted_iota(jnp.int32, (2 * gw, wide), 0)
            hot = (entry == rel_ref[0:1, k * wide : (k + 1) * wide]).astype(F32).astype(BF16)
            value = dot(table_rows, hot)
            for j in range(8):
                table[:, k * 8 + j, :] = value[:, j * ROWS : (j + 1) * ROWS]
        for g in range(n_grp):
            full = jnp.concatenate([table[g * GROUP + h] for h in range(GROUP)], axis=1)
            for w in range(n_win):
                bias_scr[g, w] = full + mask_ref[w]

    rest = order[ready:]
    for i, (c, s) in enumerate(rest):
        at = PASSES[min(i, len(PASSES) - 1)]

        @pl.when(step == jnp.minimum(at, steps - 1))
        def _(c=c, s=s):
            gather.advance(c, s)

    @pl.when(step == steps - 1)
    def _():
        keep.wait()

    x = img_ref[0].astype(F32)
    xhat, _ = standardize(x)
    normed = (xhat * vec_ref[0:1] + vec_ref[1:2]).astype(BF16)
    xp = dot(perm_ref[...], normed).astype(BF16)
    mb, mf = head_masks(BF16), head_masks(F32)
    for g in range(n_grp):
        c0 = g * 3 * gw
        weight = wq[digits_of(g, n_t)].reshape(fsdp * cut, 3 * gw)
        acc = dot(xp, weight) + bq[0:1, c0 : c0 + 3 * gw]
        qkv_ref[0, :, c0 : c0 + gw] = (acc[:, :gw] * (HD ** -0.5)).astype(BF16)
        qkv_ref[0, :, c0 + gw : c0 + 3 * gw] = acc[:, gw:].astype(BF16)

    def part(g, w, j):
        return qkv_ref[0, w * ROWS : (w + 1) * ROWS, (3 * g + j) * gw : (3 * g + j + 1) * gw]

    def score(g, w):
        return dot(part(g, w, 1), spread(part(g, w, 0), mb), NT) + bias_scr[g, w]

    def store(g, w, o):
        o_scr[w * ROWS : (w + 1) * ROWS, g * gw : (g + 1) * gw] = gather_heads(o, mf).astype(BF16)

    units = [(g, w) for g in range(n_grp) for w in range(n_win)]
    ahead, behind = score(*units[0]), None
    for at, (g, w) in enumerate(units):
        s = ahead
        if at + 1 < len(units):
            ahead = score(*units[at + 1])
        e = jnp.exp(s - jnp.max(s, axis=0, keepdims=True))
        p = (e * (1.0 / jnp.sum(e, axis=0, keepdims=True))).astype(BF16)
        p_ref[0, g, w] = p
        o = dot(p, part(g, w, 2), TN)
        if behind is not None:
            store(*behind)
        behind = (g, w, o)
    store(*behind)
    mix_ref[0] = dot(permt_ref[...], o_scr[...]).astype(BF16)


def front(vectors, b_qkv, b_one, table, w_qkv, w_proj, w_one, w_two, images, consts, fsdp, tp):
    rel, mask, perm, permt = consts
    n_img, t, c = images.shape
    cut, ff_cut = w_one.shape
    gw = LANES
    n_win = mask.shape[0]
    rows, cols = n_win * ROWS, W_ONE + 2 * ff_cut
    heads = tp * table.shape[0]
    n_t, n_f = len(bits_of(tp)), len(bits_of(fsdp))
    n = n_t + n_f
    n_sem = 7 * n
    once = lambda a: pl.BlockSpec(a.shape, lambda i: (0,) * a.ndim, pipeline_mode=pl.Buffered(1))
    whole = lambda s: pl.BlockSpec(s, lambda i: (0,) * len(s))
    small = tuple(vectors) + (b_qkv, b_one, table, w_qkv, w_proj, w_one, w_two)
    return pl.pallas_call(
        functools.partial(front_kernel, fsdp=fsdp, tp=tp),
        grid=(n_img,),
        in_specs=[once(a) for a in small]
        + [pl.BlockSpec((1, t, c), lambda i: (i, 0, 0))]
        + [once(a) for a in (rel, mask, perm, permt)],
        out_specs=[
            pl.BlockSpec(memory_space=pl.ANY),
            pl.BlockSpec(memory_space=pl.ANY),
            pl.BlockSpec((1, rows, 3 * tp * gw), lambda i: (i, 0, 0)),
            pl.BlockSpec((1, tp, n_win, ROWS, GROUP * ROWS), lambda i: (i, 0, 0, 0, 0)),
            pl.BlockSpec((1, t, c), lambda i: (i, 0, 0)),
            whole((8, c)),
            whole((ff_cut // gw, tp * gw)),
        ],
        out_shape=[
            jax.ShapeDtypeStruct((2,) * n + (cut, cols), BF16),
            jax.ShapeDtypeStruct((2,) * n + (cut, 3 * gw), BF16),
            jax.ShapeDtypeStruct((n_img, rows, 3 * tp * gw), BF16),
            jax.ShapeDtypeStruct((n_img, tp, n_win, ROWS, GROUP * ROWS), BF16),
            jax.ShapeDtypeStruct((n_img, t, c), BF16),
            jax.ShapeDtypeStruct((8, c), F32),
            jax.ShapeDtypeStruct((ff_cut // gw, tp * gw), F32),
        ],
        scratch_shapes=[
            pltpu.VMEM((cut, cols), BF16),
            pltpu.VMEM((2,) * n + (cut, 3 * gw), BF16),
            pltpu.VMEM((2,) * n + (SMALL, 2 * gw), BF16),
            pltpu.VMEM((1, 3 * tp * gw), F32),
            pltpu.VMEM((heads, 2 * gw), F32),
            pltpu.VMEM((heads, ROWS, ROWS), F32),
            pltpu.VMEM((tp, n_win, ROWS, GROUP * ROWS), F32),
            pltpu.VMEM((rows, c), BF16),
            pltpu.SemaphoreType.DMA((2,)),
            pltpu.SemaphoreType.DMA((n_sem,)),
            pltpu.SemaphoreType.DMA((n_sem,)),
        ],
        compiler_params=pltpu.CompilerParams(
            vmem_limit_bytes=60 << 20, collective_id=1, has_side_effects=True
        ),
        name="front",
    )(*small, images, rel, mask, perm, permt)


SQRT_HALF = float(np.sqrt(0.5))
INV_SQRT_2PI = float(1.0 / np.sqrt(2.0 * np.pi))


class Spread:
    def __init__(self, cube, full, send, recv):
        self.cube, self.full, self.send, self.recv = cube, full, send, recv
        self.stages = cube.n_t

    def ref(self, s, i):
        own = self.cube.own
        return self.full.at[tuple(slice(None) if k < s else own[k] for k in range(self.stages)) + (i,)]

    def copy(self, s, i):
        ref = self.ref(s, i)
        return pltpu.make_async_remote_copy(
            ref, ref, self.send.at[s, i], self.recv.at[s, i], device_id=self.cube.partner(s), device_id_type=MESH
        )


class Reduce:
    def __init__(self, cube, acc, order, bufs, send, recv, n_digits, out):
        self.cube, self.acc, self.order, self.bufs = cube, acc, order, bufs
        self.send, self.recv, self.n_digits, self.out = send, recv, n_digits, out
        self.stages = len(order)

    def at(self, free, flip=None):
        own = self.cube.own
        return tuple(
            slice(None) if k in free else (1 - own[k] if k == flip else own[k]) for k in range(self.n_digits)
        )

    def left(self, s):
        return sorted(k for k in self.order[s + 1 :] if k < self.n_digits)

    def copy(self, s):
        return pltpu.make_async_remote_copy(
            self.acc.at[self.at(self.left(s), self.order[s])],
            self.bufs[s],
            self.send.at[s],
            self.recv.at[s],
            device_id=self.cube.partner(self.order[s]),
            device_id_type=MESH,
        )

    def start(self):
        self.copy(0).start()

    def advance(self, s):
        self.copy(s).wait()
        region = self.at(self.left(s))
        if s + 1 == self.stages:
            self.out(self.acc[region].astype(F32) + self.bufs[s][...].astype(F32))
        else:
            self.acc[region] = self.acc[region] + self.bufs[s][...]
        if s + 1 < self.stages:
            self.copy(s + 1).start()


def reduce_orders(n_t, n):
    t, f = list(range(n_t)), list(range(n_t, n))
    t_in, f_in = t[1:][::-1], f[::-1]
    early = (t_in + f_in + t[:1], t_in + f[:-1][::-1] + f[-1:] + t[:1])
    late = (t_in + f_in + t[:1], t_in + f[1:-1][::-1] + f[-1:] + t[:1] + f[:1])
    return early, late, t[::-1] + f_in


def layer_kernel(live_ref, img_hbm, cot_hbm, mix_ref, w_hbm, wq_hbm, vec_ref, b1_ref, qkv_ref, p_ref, perm_ref, permt_ref,
                 out_ref, gin_ref, dqkv_ref, dw1_ref, dw2_ref, dwp_ref, small_ref,
                 img_ref, cot_ref, w1_ref, w2_ref, wq_ref, wp, act, slope, normed_two, up_scr, gres_scr,
                 db1, dvec, dqkv_scr, dw, db, dtab, res_scr, acc, acc_p, late_a, late_b, small, *rest,
                 fsdp, tp, per, n_q):
    step = pl.program_id(0)
    cube = Cube(fsdp, tp)
    n, n_t, n_f = cube.count, cube.n_t, cube.count - cube.n_t
    n_img, n_tok, c = img_ref.shape
    n_grp, n_win = p_ref.shape[1:3]
    gw = LANES
    cut = c // fsdp
    fwd_steps = n_img // per
    bwd_at = fwd_steps
    att_at = bwd_at + n_q
    last_step = att_at + n_img - 1

    early, late, both = reduce_orders(n_t, n)
    bufs, rest = rest[: 5 * n], rest[5 * n :]
    load, local, send, recv, local_in, send_in, recv_in, rs_send, rs_recv = rest

    wide_q = n_q * gw
    loads = [
        pltpu.make_async_copy(w_hbm.at[:, :, pl.ds(W_ONE, wide_q)], w1_ref, load.at[0]),
        pltpu.make_async_copy(w_hbm.at[:, :, pl.ds(W_ONE + wide_q, wide_q)], w2_ref, load.at[1]),
        pltpu.make_async_copy(img_hbm, img_ref, load.at[2]),
        pltpu.make_async_copy(cot_hbm, cot_ref, load.at[3]),
    ]
    loads += [
        pltpu.make_async_copy(w_hbm.at[g, :, pl.ds(0, gw)], wp.at[:, pl.ds(g * gw, gw)], load.at[5 + g])
        for g in range(n_grp)
    ]
    load_wq = pltpu.make_async_copy(wq_hbm, wq_ref, load.at[4])
    gmix_scr = cot_ref

    def result_of(q):
        def out(total):
            dw1_ref[:, q * gw : (q + 1) * gw] = total[:, :gw]
            dw2_ref[:, q * gw : (q + 1) * gw] = total[:, gw:]

        return out

    def result_p(total):
        dwp_ref[...] = total

    def result_a(total):
        for k in range(3):
            dqkv_ref[k, : cut // 2] = total[:, k * gw : (k + 1) * gw]

    def result_b(total):
        for k in range(3):
            dqkv_ref[k, cut // 2 :] = total[:, k * gw : (k + 1) * gw]

    def result_s(total):
        small_ref[...] = total

    plans = [
        (acc.at[q], [ref.at[q] for ref in bufs[:n]], early[q % 2], n, result_of(q)) for q in range(n_q)
    ]
    plans += [
        (acc_p, bufs[n : 2 * n], early[0], n, result_p),
        (late_a, bufs[2 * n : 3 * n], late[0], n, result_a),
        (late_b, bufs[3 * n : 4 * n], late[1], n, result_b),
        (small, bufs[4 * n :], both, n_t, result_s),
    ]
    reduces = [
        Reduce(cube, ref, order, buf, rs_send.at[k], rs_recv.at[k], d, out)
        for k, (ref, buf, order, d, out) in enumerate(plans)
    ]
    n_early = n_q + 1
    spread_out = Spread(cube, out_ref, send, recv)
    spread_in = Spread(cube, gin_ref, send_in, recv_in)

    def keep_out(i):
        return pltpu.make_async_copy(res_scr.at[pl.ds(i * per, per)], spread_out.ref(0, i), local.at[i])

    def keep_in(i):
        return pltpu.make_async_copy(res_scr.at[i], spread_in.ref(0, i), local_in.at[i])

    events = {}

    def plan(at, work):
        events.setdefault(at, []).append(work)

    def point(k):
        for at in sorted(events):
            if at[1] == k:

                @pl.when(step == at[0])
                def _(at=at):
                    for work in events[at]:
                        work()

    def send_out(i):
        keep_out(i).wait()
        spread_out.copy(0, i).start()

    def pass_out(i, s):
        spread_out.copy(s - 1, i).wait()
        spread_out.copy(s, i).start()

    def send_in_(i):
        keep_in(i).wait()
        spread_in.copy(0, i).start()

    def pass_in(i, s):
        spread_in.copy(s - 1, i).wait()
        spread_in.copy(s, i).start()

    for i in range(fwd_steps):
        plan((i + 1, 0), functools.partial(send_out, i))
    later = [att_at - 1 + 3 * i for i in range(fwd_steps)]
    for s in range(1, n_t):
        for i in range(fwd_steps):
            plan((min(later[i] + s - 1, last_step), 0), functools.partial(pass_out, i, s))
    for i in range(n_img - 1):
        plan((att_at + i + 1, 0), functools.partial(send_in_, i))
    tail = []
    for i in range(n_img):
        for s in range(1, n_t):
            at = att_at + i + 3 + s
            if at <= last_step:
                plan((at, 0), functools.partial(pass_in, i, s))
            else:
                tail.append(functools.partial(pass_in, i, s))
    ends = []
    for k in range(n_early):
        begin = (bwd_at + k + 1, 1) if k + 1 < n_q else (att_at, 0)
        plan(begin, reduces[k].start)
        slots = SLOTS[k] if k < len(SLOTS) else ()
        for s in range(n):
            work = functools.partial(reduces[k].advance, s)
            if s < len(slots):
                plan((bwd_at + slots[s][0], slots[s][1]), work)
            else:
                ends.append(work)

    @pl.when(step == 0)
    def _():
        for ld in loads[2:] + loads[:2] + [load_wq]:
            ld.start()
        greet(cube, range(n))
        dw[...] = jnp.zeros_like(dw)
        dvec[...] = jnp.zeros_like(dvec)
        db[...] = jnp.zeros_like(db)
        db1[...] = jnp.zeros_like(db1)
        dtab[...] = jnp.zeros_like(dtab)
        for ld in loads[2:]:
            ld.wait()

    def columns(ref, q):
        at = pl.ds(pl.multiple_of(q * gw, gw), gw)
        return jnp.concatenate([ref[g, :, at] for g in range(n_grp)], axis=1)

    def rows_of(ref, b):
        return jnp.concatenate([ref[b * per + i] for i in range(per)], axis=0)

    def middle(b):
        mixed = rows_of(mix_ref, b)
        res = rows_of(img_ref, b).astype(F32) + (dot(mixed, wp[...], NT) + vec_ref[2:3])
        return (mixed, res) + standardize(res)

    @pl.when(step < bwd_at)
    def _():
        point(0)
        live = jnp.concatenate(
            [jnp.full((n_tok, 1), 1.0, F32) * live_ref[step * per + i] for i in range(per)], axis=0
        )
        up = rows_of(cot_ref, step).astype(F32) * live
        up_scr[step] = up.astype(BF16)
        dvec[5:6] += jnp.sum(up, axis=0, keepdims=True)
        mixed, res, xhat, _ = middle(step)
        normed_two[step] = (xhat * vec_ref[3:4] + vec_ref[4:5]).astype(BF16)

        @pl.when(step == 0)
        def _():
            for ld in loads[:2]:
                ld.wait()

        def hidden_part(q, branch):
            hid = dot(normed_two[step], columns(w1_ref, q)) + b1_ref[pl.ds(q, 1)]
            cdf = 0.5 * (1.0 + lax.erf(hid * SQRT_HALF))
            a = (hid * cdf).astype(BF16)
            act[step, q] = a
            slope[step, q] = (cdf + hid * (jnp.exp(-0.5 * hid * hid) * INV_SQRT_2PI)).astype(BF16)
            return branch + dot(a, columns(w2_ref, q), NT)

        total = lax.fori_loop(0, n_q, hidden_part, res + vec_ref[5:6])
        out = (live * total).astype(BF16)
        for i in range(per):
            res_scr[step * per + i] = out[i * n_tok : (i + 1) * n_tok]
        keep_out(step).start()

    @pl.when(jnp.logical_and(step >= bwd_at, step < att_at))
    def _():
        q = step - bwd_at
        point(0)
        w2 = columns(w2_ref, q)
        d_one = d_two = None
        for b in range(fwd_steps):
            if b == 1:
                point(1)
            up = up_scr[b]
            dh = (dot(up, w2) * slope[b, q].astype(F32)).astype(BF16)
            slope[b, q] = dh
            db1[pl.ds(q, 1)] += jnp.sum(dh.astype(F32), axis=0, keepdims=True)
            one, two = dot(normed_two[b], dh, TN), dot(up, act[b, q], TN)
            d_one, d_two = (one, two) if b == 0 else (d_one + one, d_two + two)
        for t in range(n_grp):
            block = (2,) * n_f + (cut, gw)
            at = (q,) + digits_of(t, n_t) + (slice(None),) * (n_f + 1)
            l = slice(t * gw, (t + 1) * gw)
            acc[at + (slice(0, gw),)] = d_one[:, l].astype(BF16).reshape(block)
            acc[at + (slice(gw, 2 * gw),)] = d_two[:, l].astype(BF16).reshape(block)

    @pl.when(step == att_at - 1)
    def _():
        point(2)

        def back(b, d_proj):
            dn = dot(slope[b, 0], columns(w1_ref, 0), NT)
            for k in range(1, n_q):
                dn = dn + dot(slope[b, k], columns(w1_ref, k), NT)
            mixed, _, xhat, inv = middle(b)
            d = dn * vec_ref[3:4]
            gres = up_scr[b].astype(F32) + inv * (
                d - jnp.mean(d, axis=-1, keepdims=True) - xhat * jnp.mean(d * xhat, axis=-1, keepdims=True)
            )
            gatt = gres.astype(BF16)
            gmix = dot(gatt, wp[...]).astype(BF16)
            for i in range(per):
                r = slice(i * n_tok, (i + 1) * n_tok)
                gres_scr[b * per + i] = gres[r]
                gmix_scr[b * per + i] = gmix[r]
            dvec[2:3] += jnp.sum(gatt.astype(F32), axis=0, keepdims=True)
            dvec[3:4] += jnp.sum(dn * xhat, axis=0, keepdims=True)
            dvec[4:5] += jnp.sum(dn, axis=0, keepdims=True)
            return d_proj + dot(gatt, mixed, TN)

        d_proj = lax.fori_loop(0, fwd_steps, back, jnp.zeros((c, c), F32))
        for t in range(n_grp):
            acc_p[digits_of(t, n_t)] = (
                d_proj[:, t * gw : (t + 1) * gw].astype(BF16).reshape((2,) * n_f + (cut, gw))
            )

    @pl.when(step == att_at)
    def _():
        load_wq.wait()

    @pl.when(step >= att_at)
    def _():
        j = step - att_at
        mb, mf = head_masks(BF16), head_masks(F32)
        point(0)
        x = img_ref[j].astype(F32)
        xhat, inv = standardize(x)
        normed = (xhat * vec_ref[0:1] + vec_ref[1:2]).astype(BF16)
        xp = dot(perm_ref[...], normed).astype(BF16)
        gm = dot(perm_ref[...], gmix_scr[j]).astype(BF16)
        dn = jnp.zeros((n_win * ROWS, c), F32)
        for g in range(n_grp):
            if g > 0:
                point(g)
            c0 = g * 3 * gw
            tab = jnp.zeros((ROWS, GROUP * ROWS), F32)
            cuts = [slice(w * ROWS, (w + 1) * ROWS) for w in range(n_win)]
            dos = [spread(gm[r, g * gw : (g + 1) * gw], mb) for r in cuts]
            dps = [dot(qkv_ref[0, r, c0 + 2 * gw : c0 + 3 * gw], do, NT) for r, do in zip(cuts, dos)]
            ps = [p_ref[0, g, w] for w in range(n_win)]
            dvs = [dot(p, do) for p, do in zip(ps, dos)]
            dss = []
            for p, dp in zip(ps, dps):
                pf = p.astype(F32)
                ds = pf * (dp - jnp.sum(pf * dp, axis=0, keepdims=True))
                tab = tab + ds
                dss.append(ds.astype(BF16))
            dks = [dot(ds, spread(qkv_ref[0, r, c0 : c0 + gw], mb)) for r, ds in zip(cuts, dss)]
            dqs = [dot(ds, qkv_ref[0, r, c0 + gw : c0 + 2 * gw], TN) for r, ds in zip(cuts, dss)]
            for r, dq, dk, dv in zip(cuts, dqs, dks, dvs):
                dqkv_scr[r, :gw] = (gather_heads(dq, mf) * (HD ** -0.5)).astype(BF16)
                dqkv_scr[r, gw : 2 * gw] = dk.astype(BF16)
                dqkv_scr[r, 2 * gw :] = dv.astype(BF16)
            dtab[g] += tab
            dqkv = dqkv_scr[...]
            db[0:1, c0 : c0 + 3 * gw] += jnp.sum(dqkv.astype(F32), axis=0, keepdims=True)
            dw[g] += dot(xp, dqkv, TN)
            dn = dn + dot(dqkv, wq_ref[g], NT)
        hi = dn.astype(BF16)
        lo = (dn - hi.astype(F32)).astype(BF16)
        dn = dot(permt_ref[...], hi) + dot(permt_ref[...], lo)
        d = dn * vec_ref[0:1]
        gin = inv * (
            d - jnp.mean(d, axis=-1, keepdims=True) - xhat * jnp.mean(d * xhat, axis=-1, keepdims=True)
        )
        res_scr[j] = (gres_scr[j] + gin).astype(BF16)
        keep_in(j).start()
        dvec[0:1] += jnp.sum(dn * xhat, axis=0, keepdims=True)
        dvec[1:2] += jnp.sum(dn, axis=0, keepdims=True)

    @pl.when(step == last_step)
    def _():
        for g in range(n_grp):
            value = dw[g].astype(BF16).reshape((2,) * n_f + (cut, 3 * gw))
            late_a[digits_of(g, n_t)] = value[..., : cut // 2, :]
            late_b[digits_of(g, n_t)] = value[..., cut // 2 :, :]
        for red in reduces[n_early : n_early + 2]:
            red.start()
        wide = GROUP * ROWS
        for g in range(n_grp):
            panel = small.at[digits_of(g, n_t)]
            panel[:ROWS] = dtab[g]
            c0 = g * 3 * gw
            panel[ROWS : ROWS + 1] = db[0:1, c0 : c0 + wide]
            panel[ROWS + 1 : ROWS + 2] = jnp.concatenate(
                [db[0:1, c0 + wide : c0 + 3 * gw], jnp.zeros((1, 2 * wide - 3 * gw), F32)], axis=1
            )
            r = ROWS + 2
            for q in range(0, n_q, 2):
                pair = [db1[q + k : q + k + 1, g * gw : (g + 1) * gw] for k in range(2)]
                panel[r : r + 1] = jnp.concatenate(pair, axis=1)
                r = r + 1
            for i in range(6):
                for k in range(c // wide):
                    panel[r : r + 1] = dvec[i : i + 1, k * wide : (k + 1) * wide]
                    r = r + 1
        reduces[n_early + 2].start()
        send_in_(n_img - 1)
        for s in range(n):
            for red in reduces[n_early:][::-1]:
                red.advance(s)
            if s == TAIL_AT:
                for work in tail:
                    work()
        for work in ends:
            work()
        for i in range(fwd_steps):
            spread_out.copy(n_t - 1, i).wait()
        for i in range(n_img):
            spread_in.copy(n_t - 1, i).wait()


SLOTS = (
    ((3, 0), (4, 2), (6, 0), (8, 0), (10, 0)),
    ((4, 0), (6, 0), (8, 0), (10, 0)),
    ((5, 0), (7, 0), (9, 0), (11, 0)),
    ((6, 0), (8, 2), (10, 2), (11, 3)),
    ((6, 0), (8, 2), (10, 2), (11, 3)),
)
TAIL_AT = 2


def layer(live, images, out_grad, mixed, w_all, w_qkv, vecs, b1, qkv, p, perm, permt, fsdp, tp, per=4):
    n_img, t, c = mixed.shape
    rows, cols = qkv.shape[1:]
    n_grp, n_win = p.shape[1:3]
    gw, wide = LANES, GROUP * ROWS
    n_q = b1.shape[0]
    ff_cut = n_q * gw
    cut = c // fsdp
    n_t, n_f = len(bits_of(tp)), len(bits_of(fsdp))
    n = n_t + n_f
    digits = (2,) * n
    n_small = ROWS + 2 + ff_cut // wide + 6 * (c // wide)
    fwd_steps = n_img // per
    att_at = fwd_steps + n_q
    bufs = []
    for lead, block in (
        ((n_q,), (cut, 2 * gw)),
        ((), (cut, gw)),
        ((), (cut // 2, 3 * gw)),
        ((), (cut // 2, 3 * gw)),
    ):
        bufs += [pltpu.VMEM(lead + (2,) * (n - 1 - s) + block, BF16) for s in range(n)]
    both = reduce_orders(n_t, n)[2]
    for s in range(n):
        left = sum(k < n_t for k in both[s + 1 :])
        bufs.append(pltpu.VMEM((2,) * left + (n_small, wide), F32))
    whole = lambda s: pl.BlockSpec(s, lambda i: (0,) * len(s))
    once = lambda s: pl.BlockSpec(s, lambda i: (0,) * len(s), pipeline_mode=pl.Buffered(1))
    image = lambda i: jnp.clip(i - att_at, 0, n_img - 1)
    any_spec = pl.BlockSpec(memory_space=pl.ANY)
    hidden = (fwd_steps, n_q, per * t, n_grp * gw)
    return pl.pallas_call(
        functools.partial(layer_kernel, fsdp=fsdp, tp=tp, per=per, n_q=n_q),
        grid=(att_at + n_img,),
        in_specs=[
            pl.BlockSpec(memory_space=pltpu.SMEM),
            any_spec,
            any_spec,
            once(mixed.shape),
            any_spec,
            any_spec,
            once(vecs.shape),
            once(b1.shape),
            pl.BlockSpec((1, rows, cols), lambda i: (image(i), 0, 0)),
            pl.BlockSpec((1,) + p.shape[1:], lambda i: (image(i), 0, 0, 0, 0)),
            once(perm.shape),
            once(permt.shape),
        ],
        out_specs=[any_spec, any_spec]
        + [whole(s) for s in ((3, cut, gw), (cut, ff_cut), (cut, ff_cut), (cut, gw), (n_small, wide))],
        out_shape=[
            jax.ShapeDtypeStruct((2,) * n_t + (fwd_steps, per, t, c), BF16),
            jax.ShapeDtypeStruct((2,) * n_t + (n_img, t, c), BF16),
            jax.ShapeDtypeStruct((3, cut, gw), F32),
            jax.ShapeDtypeStruct((cut, ff_cut), F32),
            jax.ShapeDtypeStruct((cut, ff_cut), F32),
            jax.ShapeDtypeStruct((cut, gw), F32),
            jax.ShapeDtypeStruct((n_small, wide), F32),
        ],
        scratch_shapes=[
            pltpu.VMEM((n_img, t, c), BF16),
            pltpu.VMEM((n_img, t, c), BF16),
            pltpu.VMEM((n_grp, c, ff_cut), BF16),
            pltpu.VMEM((n_grp, c, ff_cut), BF16),
            pltpu.VMEM((n_grp, c, 3 * gw), BF16),
            pltpu.VMEM((c, c), BF16),
            pltpu.VMEM(hidden, BF16),
            pltpu.VMEM(hidden, BF16),
            pltpu.VMEM((fwd_steps, per * t, c), BF16),
            pltpu.VMEM((fwd_steps, per * t, c), BF16),
            pltpu.VMEM((n_img, t, c), F32),
            pltpu.VMEM((8, n_grp * gw), F32),
            pltpu.VMEM((8, c), F32),
            pltpu.VMEM((rows, 3 * gw), BF16),
            pltpu.VMEM((n_grp, c, 3 * gw), F32),
            pltpu.VMEM((1, cols), F32),
            pltpu.VMEM((n_grp, ROWS, wide), F32),
            pltpu.VMEM((n_img, t, c), BF16),
            pltpu.VMEM((n_q,) + digits + (cut, 2 * gw), BF16),
            pltpu.VMEM(digits + (cut, gw), BF16),
            pltpu.VMEM(digits + (cut // 2, 3 * gw), BF16),
            pltpu.VMEM(digits + (cut // 2, 3 * gw), BF16),
            pltpu.VMEM((2,) * n_t + (n_small, wide), F32),
            *bufs,
            pltpu.SemaphoreType.DMA((5 + n_grp,)),
            pltpu.SemaphoreType.DMA((fwd_steps,)),
            pltpu.SemaphoreType.DMA((n_t, fwd_steps)),
            pltpu.SemaphoreType.DMA((n_t, fwd_steps)),
            pltpu.SemaphoreType.DMA((n_img,)),
            pltpu.SemaphoreType.DMA((n_t, n_img)),
            pltpu.SemaphoreType.DMA((n_t, n_img)),
            pltpu.SemaphoreType.DMA((n_q + 4, n)),
            pltpu.SemaphoreType.DMA((n_q + 4, n)),
        ],
        compiler_params=pltpu.CompilerParams(
            vmem_limit_bytes=60 << 20, collective_id=2, has_side_effects=True
        ),
        name="layer",
    )(live, images, out_grad, mixed, w_all, w_qkv, vecs, b1, qkv, p, perm, permt)


def per_device(
    images,
    attn_norm_gain,
    attn_norm_bias,
    qkv_weight,
    qkv_bias,
    position_table,
    proj_weight,
    proj_bias,
    mlp_norm_gain,
    mlp_norm_bias,
    fc1_weight,
    fc1_bias,
    fc2_weight,
    fc2_bias,
    image_count,
    out_grad,
    *,
    fsdp,
    tp,
):
    index, mask, perm = window_constants()
    span = position_table.shape[0]
    gw = LANES
    cut = qkv_weight.shape[0]
    width = cut * fsdp
    ff_cut = fc1_bias.shape[0]
    n_qkv = qkv_bias.size
    mine = images.shape[0] // tp
    first = lax.axis_index("tp") * mine
    img = lax.dynamic_slice_in_dim(images, first, mine, 0)
    cot = lax.dynamic_slice_in_dim(out_grad, first, mine, 0)
    live = (first + jnp.arange(mine, dtype=jnp.int32) < image_count[0]).astype(F32)
    perm16 = jnp.asarray(perm).astype(BF16)
    consts = (jnp.asarray(index).reshape(1, -1), jnp.asarray(mask), perm16, perm16.T)
    vectors = (attn_norm_gain, attn_norm_bias, proj_bias, mlp_norm_gain, mlp_norm_bias, fc2_bias)
    w_all, w_qkv, qkv, probs, mixed, vecs, b_one = front(
        [v.reshape(1, cut) for v in vectors],
        qkv_bias,
        fc1_bias.reshape(1, ff_cut),
        position_table.T,
        qkv_weight.transpose(1, 0, 2),
        proj_weight.T,
        fc1_weight,
        fc2_weight.T,
        img,
        consts,
        fsdp,
        tp,
    )
    w_all = w_all.reshape(tp, width, w_all.shape[-1])
    w_qkv = w_qkv.reshape(tp, width, 3 * gw)
    output, images_grad, d_qkv, d_one, d_two, d_proj, small = layer(
        live, img, cot, mixed, w_all, w_qkv, vecs, b_one, qkv, probs, consts[2], consts[3], fsdp, tp
    )
    wide = GROUP * ROWS
    hot = (jnp.asarray(index)[None] == jnp.arange(span, dtype=jnp.int32)[:, None, None]).astype(F32)
    d_tab = jnp.einsum(
        "jhi,rji->rh",
        small[:ROWS].reshape(ROWS, GROUP, ROWS),
        hot,
        precision=lax.Precision.HIGHEST,
    )
    at = ROWS + 2
    dqkv_bias = small[ROWS:at].reshape(-1)[:n_qkv].reshape(qkv_bias.shape)
    dfc1_bias = small[at : at + ff_cut // wide].reshape(-1)
    dvec = small[at + ff_cut // wide :].reshape(6, width)
    dvec = lax.dynamic_slice_in_dim(dvec, lax.axis_index("fsdp") * cut, cut, 1)
    return (
        output.reshape(images.shape),
        images_grad.reshape(images.shape),
        dvec[0],
        dvec[1],
        d_qkv.transpose(1, 0, 2),
        dqkv_bias,
        d_tab,
        d_proj.T,
        dvec[2],
        dvec[3],
        dvec[4],
        d_one,
        dfc1_bias,
        d_two.T,
        dvec[5],
    )


def solution(mesh):
    P = jax.sharding.PartitionSpec
    return jax.shard_map(
        functools.partial(per_device, fsdp=mesh.shape["fsdp"], tp=mesh.shape["tp"]),
        mesh=mesh,
        in_specs=(
            P("fsdp", None, None),
            P("fsdp"),
            P("fsdp"),
            P("fsdp", None, "tp"),
            P(None, "tp"),
            P(None, "tp"),
            P("tp", "fsdp"),
            P("fsdp"),
            P("fsdp"),
            P("fsdp"),
            P("fsdp", "tp"),
            P("tp"),
            P("tp", "fsdp"),
            P("fsdp"),
            P("fsdp"),
            P("fsdp", None, None),
        ),
        out_specs=(
            P("fsdp", None, None),
            P("fsdp", None, None),
            P("fsdp"),
            P("fsdp"),
            P("fsdp", None, "tp"),
            P(None, "tp"),
            P(None, "tp"),
            P("tp", "fsdp"),
            P("fsdp"),
            P("fsdp"),
            P("fsdp"),
            P("fsdp", "tp"),
            P("tp"),
            P("tp", "fsdp"),
            P("fsdp"),
        ),
        check_vma=False,
    )
```
